128 devices in a mesh: dp: 16 (over x, z), table: 8 (over y, core).
Axes of the slice: x: 4, y: 4, z: 4, core: 2. Of those that a mesh axis runs over, the one named last changes fastest.
Arguments:
- touched_rows: bfloat16 [32768, 512], P(('dp', 'table')), may hold values from -6 to 6
- row_of_token: int32 [131072], P(('dp', 'table')), may hold values from 0 to 255
- row_owner: int32 [32768, 1], P(('dp', 'table')), may hold values from 0 to 127; in each aligned block of 256 rows (0 to 255, 256 to 511, ...) at most 4 rows name the same one
- owner_row: int32 [32768], P(('dp', 'table')), may hold values from 0 to 1023
- seq_blocks: int32 [2048], P(('dp', 'table')), may hold values from 1 to 4, as said below
- seq_dest: int32 [2048], P(('dp', 'table')), may hold values from 0 to 15, as said below
- grad_out: bfloat16 [65536, 512], P(('dp', 'table')), may hold values from -6 to 6
- w_in: bfloat16 [512, 2048], replicated, may hold values from -0.25 to 0.25
- w_out: bfloat16 [512, 512], replicated, may hold values from -0.25 to 0.25
- gain_in: float32 [512], replicated, may hold values from 0.25 to 1.75
- gain_out: float32 [512], replicated, may hold values from 0.25 to 1.75
Outputs:
- table_grad: float32 [131072, 512], P(('dp', 'table'))
- grad_w_in: float32 [512, 2048], replicated
- grad_w_out: float32 [512, 512], replicated
- grad_gain_in: float32 [512], replicated
- grad_gain_out: float32 [512], replicated
The draws below stay inside these ranges and needn't reach their ends.
Inputs may be any that keep to these rules, and one draw needn't show every extreme that they name: `seq_blocks`: lengths in blocks of 16 tokens. The sequences that one device receives total exactly 32 blocks, and among them one has exactly 4 blocks. `seq_dest`: the 16 slots of a device go to 16 different dp indices, so every device receives exactly one sequence from each device with its table index. `row_owner`: at most 4 of one device's touched rows have the same owner.
All inputs are finite; a program needn't handle non-finite values.
Results may differ from the reference program's by a relative error of at most 0.0091.
Values may be sent and summed in bfloat16 or wider, within the bound.
A program may use at most 128 MiB of HBM per device.

```python
import math
import jax
import jax.numpy as jnp
import numpy as np
from jax import lax

D = 512
HEADS = 4
HDIM = 128
BLK = 16
LMAXB = 4
UNIQ = 256
ROWS_DEV = 1024
SLOT = 64
ARR_TOK = 1024
BAL_TOK = 512
CAP = 4
TOTAL_TOK = 65536
UNIQ_ALL = 32768
ARR_ALL = 131072
N_DP = 16
N_TABLE = 8


def plan_tables(key):
    base_key = jax.random.fold_in(key, 4099)
    quarter = N_DP // 4

    def one_column(column_key):
        key_order, key_shift, key_wobble = jax.random.split(column_key, 3)
        ordering = jax.random.permutation(key_order, N_DP).astype(jnp.int32)
        ranking = jnp.zeros((N_DP,), jnp.int32).at[ordering].set(jnp.arange(N_DP, dtype=jnp.int32))
        slot_ids = jnp.arange(N_DP, dtype=jnp.int32)[None, :]
        source_rank = ranking[:, None]
        target_rank = (source_rank + slot_ids) % N_DP
        target = ordering[target_rank]
        cluster = slot_ids // 4
        shifts = jax.random.randint(key_shift, (N_DP, quarter), 0, LMAXB // 2)
        wobble = jax.random.randint(key_wobble, (N_DP, quarter), 0, 2)
        shift_here = jnp.where(cluster == target_rank % quarter, 0, shifts[target_rank, cluster])
        wobble_here = wobble[target_rank, cluster]
        source_role = source_rank % 4
        blocks = jnp.where(source_role == 0, LMAXB - shift_here, jnp.where(source_role == 3, 1 + shift_here, jnp.where(source_role == 1, 1 + wobble_here, 2 - wobble_here)))
        return (blocks.astype(jnp.int32), target.astype(jnp.int32))
    blocks, target = jax.vmap(one_column)(jax.random.split(base_key, N_TABLE))
    return (jnp.transpose(blocks, (1, 0, 2)).reshape(-1), jnp.transpose(target, (1, 0, 2)).reshape(-1))


def draw_seq_blocks(key, part):
    return plan_tables(key)[0]


def draw_seq_dest(key, part):
    return plan_tables(key)[1]


def set_ends(entries, own_key, least, high):
    shape = entries.shape
    index_at = [jax.random.randint(jax.random.fold_in(own_key, axis), (), 0, shape[axis]) for axis in range(len(shape))]
    entries = entries.at[tuple(index_at)].set(least)
    longest = shape.index(max(shape))
    index_at[longest] = (index_at[longest] + 1) % shape[longest]
    return entries.at[tuple(index_at)].set(high)


def shard_levels(key, extent, cuts, least, high):
    level, own = 1.0, jax.random.fold_in(key, 6)
    for dim, blocks in cuts:
        draws = jnp.exp(jax.random.uniform(jax.random.fold_in(own, dim), (blocks,), jnp.float32, least / len(cuts), high / len(cuts)))
        level = level * jnp.repeat(draws, extent[dim] // blocks).reshape([-1 if axis == dim else 1 for axis in range(len(extent))])
    return level


def rank_bounds(number_of, lean):
    loads = [(1 << 20) // math.isqrt(rank ** lean) + 1 for rank in range(1, number_of + 1)]
    deviation = 1 + sum(loads) // (1 << 30)
    return np.cumsum(np.array([max(1, weight // deviation) for weight in loads]))


def skewed_ids(stream_key, dims, number_of, skew):
    grid = rank_bounds(number_of, skew)
    ticket = jax.random.randint(jax.random.fold_in(stream_key, 1), dims, 0, int(grid[number_of - 1]))
    rank = jnp.searchsorted(jnp.asarray(grid, jnp.int32), ticket, side="right")
    return jax.random.permutation(jax.random.fold_in(stream_key, 2), number_of)[rank].astype(jnp.int32)


def shared_out(own_key, own, number, rows, amount, top, bound, slope):
    order = jax.random.permutation(own_key, amount)
    crowded, ordinary = portions_of(amount, rows * top, bound, slope, True), portions_of(amount, rows * top, bound, slope, False)
    places = jnp.arange(amount)

    def named(lengths, rotation):
        used = int((lengths > 0).sum())
        fixed = max(1, used // 4)
        moved = fixed + (places - fixed + rotation * (used - fixed)) % max(1, amount - fixed)
        return jnp.zeros((amount,), jnp.int32).at[order[jnp.where(places < fixed, places, moved)]].set(jnp.asarray(lengths, jnp.int32))

    lengths = jnp.where(number % 4 == 0, named(crowded, number // 4), named(ordinary, number - number // 4 - 1))
    mixed = jax.random.permutation(jax.random.fold_in(own, 3), amount)
    giver, taker = mixed[0:amount // 2 * 2:2], mixed[1:amount // 2 * 2:2]
    margin = jnp.minimum(lengths[giver] - 1, bound - lengths[taker]) // 2
    margin = jnp.where((giver == order[0]) | (taker == order[0]) | (lengths[taker] == 0), 0, jnp.maximum(margin, 0))
    moved = jax.random.randint(jax.random.fold_in(own, 4), (amount // 2,), 0, 1 << 20) % (margin + 1)
    lengths = lengths.at[giver].add(-moved).at[taker].add(moved)
    labels = jnp.searchsorted(jnp.cumsum(lengths), jnp.arange(rows * top), side="right").astype(jnp.int32)
    grid = labels.reshape(top, rows).T
    grid = grid[jax.random.permutation(jax.random.fold_in(own, 1), rows)]
    rotation = jax.random.randint(jax.random.fold_in(own, 2), (rows, 1), 0, top)
    return jnp.take_along_axis(grid, (jnp.arange(top)[None, :] + rotation) % top, axis=1)


def portions_of(number_of, total, limit, slope, full):
    portions = [(1 << 20) // math.isqrt(standing ** slope) + 1 for standing in range(1, number_of + 1)]
    largest = limit if full else min(limit, max(-(-total // number_of), total * portions[0] // sum(portions)))
    least = 1 if total - largest >= number_of - 1 else 0
    given, spare = [largest] + [least] * (number_of - 1), total - largest - least * (number_of - 1)
    while spare > 0:
        candidates = [i for i in range(1, number_of) if given[i] < largest] or [i for i in range(1, number_of) if given[i] < limit]
        whole, budget = sum([portions[i] for i in candidates]), spare
        for i in candidates:
            addition = min(limit - given[i], max(1, budget * portions[i] // whole), spare)
            given[i] = given[i] + addition
            spare = spare - addition
    return np.array(given)


def noise(stream_key, shape, deviation, bound, cuts=(), held_as=jnp.bfloat16):
    array = deviation * jax.random.normal(stream_key, shape, jnp.float32)
    if cuts:
        array = array * shard_levels(stream_key, shape, cuts, -0.22, 0.18)
    return jnp.clip(array, -bound, bound).astype(held_as)


def setup_inputs(seed: int = 0) -> dict:
    key_list = jax.random.split(jax.random.key(seed), 12)
    touched_rows = noise(key_list[0], (UNIQ_ALL, D), 1.0, 6.0, ((0, 128),))
    row_of_token = set_ends(skewed_ids(key_list[1], (ARR_ALL,), UNIQ, 2), jax.random.fold_in(key_list[1], 3), 0, UNIQ - 1).astype(jnp.int32)
    row_owner_keys = jax.random.split(jax.random.fold_in(key_list[2], 1), UNIQ_ALL // UNIQ)
    row_owner_turns = jax.random.permutation(jax.random.fold_in(key_list[2], 3), UNIQ_ALL // UNIQ)
    row_owner = jax.vmap(lambda own, number: shared_out(jax.random.fold_in(key_list[2], 2), own, number, UNIQ, N_DP * N_TABLE, 1, CAP, 1))(row_owner_keys, row_owner_turns).reshape((UNIQ_ALL, 1))
    owner_row = set_ends(jax.random.randint(key_list[3], (UNIQ_ALL,), 0, ROWS_DEV), jax.random.fold_in(key_list[3], 1), 0, ROWS_DEV - 1).astype(jnp.int32)
    seq_blocks = draw_seq_blocks(jax.random.fold_in(key_list[11], 71), 0)
    seq_dest = draw_seq_dest(jax.random.fold_in(key_list[11], 71), 0)
    grad_out = noise(key_list[6], (TOTAL_TOK, D), 1.0, 6.0, ((0, 128),))
    w_in = noise(key_list[7], (D, 4 * D), D ** -0.5, 0.25)
    w_out = noise(key_list[8], (D, D), D ** -0.5, 0.25)
    gain_in = jnp.clip(1.0 + 0.15 * jax.random.normal(key_list[9], (D,), jnp.float32), 0.25, 1.75)
    gain_out = jnp.clip(1.0 + 0.15 * jax.random.normal(key_list[10], (D,), jnp.float32), 0.25, 1.75)
    return {"touched_rows": touched_rows, "row_of_token": row_of_token, "row_owner": row_owner, "owner_row": owner_row, "seq_blocks": seq_blocks, "seq_dest": seq_dest, "grad_out": grad_out, "w_in": w_in, "w_out": w_out, "gain_in": gain_in, "gain_out": gain_out}


EPSILON = 1e-05

def norm_rows(values, row_gain):
    centre = lax.optimization_barrier(jnp.mean(values, axis=-1, keepdims=True))
    shifted = values - centre
    spread = lax.optimization_barrier(jnp.mean(shifted * shifted, axis=-1, keepdims=True))
    return shifted * lax.rsqrt(spread + EPSILON) * row_gain

def silu_slope(values):
    sigma_v = jax.nn.sigmoid(values)
    return sigma_v * (1.0 + values * (1.0 - sigma_v))

def head_scores(queries, keys_in):
    return jnp.einsum('qhd,khd->hqk', queries.astype(jnp.float32), keys_in.astype(jnp.float32)) * HDIM ** (-0.5)

def device_grads(tokens, grad_y, sequence, w_in, w_out, gain_in, gain_out):
    row_count = tokens.shape[0]
    positions = jnp.arange(row_count)
    allowed = (sequence[:, None] == sequence[None, :]) & (positions[:, None] >= positions[None, :])
    allowed = allowed[None]
    normed, back_in = jax.vjp(norm_rows, tokens.astype(jnp.float32), gain_in)
    normed_half = normed.astype(jnp.bfloat16)
    hidden = jnp.dot(normed_half, w_in, preferred_element_type=jnp.float32)
    active = hidden * jax.nn.sigmoid(hidden)
    gate_part = active[:, :D]
    head_shape = (row_count, HEADS, HDIM)
    values = active[:, D:2 * D].astype(jnp.bfloat16).reshape(head_shape)
    queries = active[:, 2 * D:3 * D].astype(jnp.bfloat16).reshape(head_shape)
    keys_in = active[:, 3 * D:].astype(jnp.bfloat16).reshape(head_shape)
    scores = head_scores(queries, keys_in)
    weights = jnp.where(allowed, scores * jax.nn.sigmoid(scores), 0.0).astype(jnp.bfloat16)
    attended = jnp.einsum('hqk,khd->qhd', weights.astype(jnp.float32), values.astype(jnp.float32)).reshape(row_count, D)
    out_norm, back_out = jax.vjp(norm_rows, attended, gain_out)
    mixed = (out_norm * gate_part).astype(jnp.bfloat16)
    grad_mixed = jnp.dot(grad_y, w_out.T, preferred_element_type=jnp.float32)
    sum_w_out = jnp.dot(mixed.T, grad_y, preferred_element_type=jnp.float32)
    grad_gate = grad_mixed * out_norm
    grad_attended, sum_gain_out = back_out(grad_mixed * gate_part)
    grad_att_half = grad_attended.astype(jnp.bfloat16).reshape(head_shape).astype(jnp.float32)
    grad_weight = jnp.einsum('qhd,khd->hqk', grad_att_half, values.astype(jnp.float32))
    grad_score = jnp.where(allowed, grad_weight * silu_slope(scores) * HDIM ** (-0.5), 0.0).astype(jnp.bfloat16).astype(jnp.float32)
    grad_queries = jnp.einsum('hqk,khd->qhd', grad_score, keys_in.astype(jnp.float32)).reshape(row_count, D)
    grad_keys = jnp.einsum('hqk,qhd->khd', grad_score, queries.astype(jnp.float32)).reshape(row_count, D)
    grad_values = jnp.einsum('hqk,qhd->khd', weights.astype(jnp.float32), grad_att_half).reshape(row_count, D)
    grad_active = jnp.concatenate([grad_gate, grad_values, grad_queries, grad_keys], axis=1)
    grad_hidden = (grad_active * silu_slope(hidden)).astype(jnp.bfloat16)
    sum_w_in = jnp.dot(normed_half.T, grad_hidden, preferred_element_type=jnp.float32)
    grad_normed = jnp.dot(grad_hidden, w_in.T, preferred_element_type=jnp.float32)
    grad_inner, sum_gain_in = back_in(grad_normed)
    grad_tokens = (grad_inner + grad_y.astype(jnp.float32)).astype(jnp.bfloat16)
    return (grad_tokens, (sum_w_in, sum_w_out, sum_gain_in, sum_gain_out))

def reference(touched_rows, row_of_token, row_owner, owner_row, seq_blocks, seq_dest, grad_out, w_in, w_out, gain_in, gain_out):
    groups = N_DP * N_TABLE
    blocks = seq_blocks.reshape(N_DP, N_TABLE, N_DP)
    target = seq_dest.reshape(N_DP, N_TABLE, N_DP)
    peers = jnp.arange(N_DP, dtype=jnp.int32)
    hits = (target[..., None] == peers).astype(jnp.int32)
    sent = lax.optimization_barrier(jnp.sum(blocks[..., None] * hits, axis=2))
    before = jnp.cumsum(sent, axis=0) - sent
    starts = lax.optimization_barrier(jnp.sum(hits * before[:, :, None, :], axis=3))
    table_ids = jnp.arange(N_TABLE, dtype=jnp.int32)[None, :, None]
    inner = jnp.arange(SLOT, dtype=jnp.int32)
    first_row = (target * N_TABLE + table_ids) * BAL_TOK + starts * BLK
    live = inner < (blocks * BLK)[..., None]
    landing_rows = jnp.where(live, first_row[..., None] + inner, TOTAL_TOK).reshape(-1).astype(jnp.int32)
    arrival_ids = jnp.arange(groups * ARR_TOK, dtype=jnp.int32)
    arrival_of = jnp.zeros((TOTAL_TOK,), jnp.int32).at[landing_rows].set(arrival_ids, mode='drop')
    device_of = arrival_of // ARR_TOK
    unique_of = (device_of * UNIQ + jnp.take(row_of_token, arrival_of)).astype(jnp.int32)
    sequence_of = (arrival_of // SLOT).astype(jnp.int32)
    tokens_all = jnp.take(touched_rows, unique_of, axis=0)
    zero_sums = (jnp.zeros((D, 4 * D), jnp.float32), jnp.zeros((D, D), jnp.float32), jnp.zeros((D,), jnp.float32), jnp.zeros((D,), jnp.float32))

    def per_device(running, inputs):
        tokens_here, grad_here, sequence_here = inputs
        grad_tokens, partial_sums = device_grads(tokens_here, grad_here, sequence_here, w_in, w_out, gain_in, gain_out)
        running = jax.tree.map(lambda first_sum, second_sum: first_sum + second_sum, running, partial_sums)
        return (running, grad_tokens)
    totals, grads_all = lax.scan(per_device, zero_sums, (tokens_all.reshape(groups, BAL_TOK, D), grad_out.reshape(groups, BAL_TOK, D), sequence_of.reshape(groups, BAL_TOK)))
    row_grad = jax.ops.segment_sum(grads_all.reshape(-1, D).astype(jnp.float32), unique_of, num_segments=UNIQ * groups)
    landing = (row_owner[:, 0] * ROWS_DEV + owner_row).astype(jnp.int32)
    table_grad = jax.ops.segment_sum(row_grad, landing, num_segments=ROWS_DEV * groups)
    factor = 1.0 / math.sqrt(TOTAL_TOK)
    return (table_grad, totals[0] * factor, totals[1] * factor, totals[2] * factor, totals[3] * factor)
```

```python
import math

import jax
import jax.numpy as jnp
from jax import lax
from jax.experimental import pallas as pl
from jax.experimental.pallas import tpu as pltpu
from jax.sharding import PartitionSpec as P

HEADS = 4
HDIM = 128
BLK = 16
LMAXB = 4
SLOT = 64
ROWS_DEV = 1024
UNIQ = 256
CAP = 4
D = 512
N_DP = 16
N_TABLE = 8
N_DEV = 128
GROUP = 256
N_GROUP = 4
CHUNK = 112
FLAT = 2 * 3 * 16 * CHUNK
EPSILON = 1e-05
MESH = pl.DeviceIdType.MESH
BF = jnp.bfloat16
F32 = jnp.float32


def dot(a, b):
    return jnp.dot(a, b, preferred_element_type=F32)


def dot_t(a, b):
    return lax.dot_general(a, b, (((1,), (1,)), ((), ())), preferred_element_type=F32)


def t_dot(a, b):
    return lax.dot_general(a, b, (((0,), (0,)), ((), ())), preferred_element_type=F32)


def cot_kernel(lens_ref, grad_ref, ret_ref, got, wide, stage, lsend, lrecv, dsend, drecv, own_sem):
    dp = lax.axis_index("dp")
    tb = lax.axis_index("table")

    def peer(i):
        return lax.rem(dp + i, N_DP)

    barrier = pltpu.get_barrier_semaphore()
    for i in range(1, N_DP):
        pl.semaphore_signal(barrier, inc=1, device_id=(peer(i), tb), device_id_type=MESH)
    pl.semaphore_wait(barrier, N_DP - 1)

    def len_copy(i):
        return pltpu.make_async_remote_copy(
            src_ref=lens_ref.at[peer(i)],
            dst_ref=got.at[dp],
            send_sem=lsend.at[i],
            recv_sem=lrecv.at[i],
            device_id=(peer(i), tb),
            device_id_type=MESH,
        )

    for i in range(1, N_DP):
        len_copy(i).start()
    got[dp] = lens_ref[dp]
    for i in range(1, N_DP):
        len_copy(i).wait()

    start = jnp.zeros((1, D), jnp.int32)
    for p in range(N_DP):
        wide[p] = start
        start = start + got[p]

    row = lax.broadcasted_iota(jnp.int32, (SLOT, D), 0)
    col = lax.broadcasted_iota(jnp.int32, (SLOT, D), 1)

    def staged(p):
        hit = (col == wide[p] * BLK + row) & (row < got[p] * BLK)
        return dot(hit.astype(F32).astype(BF), grad_ref[...]).astype(BF)

    def data_copy(i):
        return pltpu.make_async_remote_copy(
            src_ref=stage.at[peer(i)],
            dst_ref=ret_ref.at[dp],
            send_sem=dsend.at[i],
            recv_sem=drecv.at[i],
            device_id=(peer(i), tb),
            device_id_type=MESH,
        )

    for i in range(1, N_DP):
        stage[peer(i)] = staged(peer(i))
        data_copy(i).start()
    stage[dp] = staged(dp)
    own = pltpu.make_async_copy(stage.at[dp], ret_ref.at[dp], own_sem)
    own.start()
    own.wait()
    for i in range(1, N_DP):
        data_copy(i).wait()


def exchange_cotangents(lens, grad_out):
    return pl.pallas_call(
        cot_kernel,
        out_shape=jax.ShapeDtypeStruct((N_DP, SLOT, D), BF),
        in_specs=[pl.BlockSpec(memory_space=pltpu.VMEM)] * 2,
        out_specs=pl.BlockSpec(memory_space=pltpu.VMEM),
        scratch_shapes=[
            pltpu.VMEM((N_DP, 1, D), jnp.int32),
            pltpu.VMEM((N_DP, 1, D), jnp.int32),
            pltpu.VMEM((N_DP, SLOT, D), BF),
            pltpu.SemaphoreType.DMA((N_DP,)),
            pltpu.SemaphoreType.DMA((N_DP,)),
            pltpu.SemaphoreType.DMA((N_DP,)),
            pltpu.SemaphoreType.DMA((N_DP,)),
            pltpu.SemaphoreType.DMA,
        ],
        compiler_params=pltpu.CompilerParams(collective_id=0, has_side_effects=True),
        name="cotangents",
    )(lens, grad_out)


def row_mean(v):
    return jnp.sum(v, axis=-1, keepdims=True) * (1.0 / D)


def layer_kernel(
    dest_ref,
    item_ref,
    touched_ref,
    ret_ref,
    owner_ref,
    orow_ref,
    w_in_ref,
    w_out_ref,
    gin_ref,
    gout_ref,
    flat_ref,
    send_ref,
    meta_ref,
    normed_all,
    mixed_all,
    gy_all,
    gh_all,
    slope,
    gate,
    vqk,
    att,
    gact,
    wts,
    rows_acc,
    gains_acc,
    spread,
):
    g = pl.program_id(0)

    @pl.when(g == 0)
    def _():
        rows_acc[...] = jnp.zeros_like(rows_acc)
        gains_acc[...] = jnp.zeros_like(gains_acc)

    here = pl.ds(pl.multiple_of(g * GROUP, GROUP), GROUP)
    gain_in = gin_ref[...]
    gain_out = gout_ref[...]
    onehot_t = (
        (lax.broadcasted_iota(jnp.int32, (UNIQ, GROUP), 0) == item_ref[...]).astype(F32).astype(BF)
    )
    tok = t_dot(onehot_t, touched_ref[...])
    shifted = tok - row_mean(tok)
    rstd_in = lax.rsqrt(row_mean(shifted * shifted) + EPSILON)
    hat_in = shifted * rstd_in
    normed = (hat_in * gain_in).astype(BF)
    normed_all[here, :] = normed
    for k in range(4):
        cols = slice(k * D, (k + 1) * D)
        hid = dot(normed, w_in_ref[:, cols])
        sig = 0.5 * jnp.tanh(0.5 * hid) + 0.5
        act = hid * sig
        slope[:, cols] = sig + act * (1.0 - sig)
        if k == 0:
            gate[...] = act
        else:
            vqk[k - 1] = act.astype(BF)

    pair = 2 * SLOT
    ri = lax.broadcasted_iota(jnp.int32, (pair, pair), 0)
    ci = lax.broadcasted_iota(jnp.int32, (pair, pair), 1)
    allowed = ((ri < SLOT) == (ci < SLOT)) & (ci <= ri)
    scale = HDIM ** (-0.5)
    for s in range(GROUP // pair):
        rows = slice(s * pair, (s + 1) * pair)
        for h in range(HEADS):
            cols = slice(h * HDIM, (h + 1) * HDIM)
            score = dot_t(vqk[1, rows, cols], vqk[2, rows, cols]) * scale
            sig = 0.5 * jnp.tanh(0.5 * score) + 0.5
            act = score * sig
            weight = jnp.where(allowed, act, 0.0).astype(BF)
            wts[s * HEADS + h, 0] = weight
            wts[s * HEADS + h, 1] = jnp.where(
                allowed, (sig + act * (1.0 - sig)) * scale, 0.0
            ).astype(BF)
            att[rows, cols] = dot(weight, vqk[0, rows, cols])

    attended = att[...]
    shifted_o = attended - row_mean(attended)
    rstd_out = lax.rsqrt(row_mean(shifted_o * shifted_o) + EPSILON)
    hat_out = shifted_o * rstd_out
    out_norm = hat_out * gain_out
    mixed_all[here, :] = (out_norm * gate[...]).astype(BF)

    gy = jnp.concatenate([ret_ref[dest_ref[g * 4 + j]] for j in range(4)], axis=0)
    gy_all[here, :] = gy
    grad_mixed = dot_t(gy, w_out_ref[...])
    gact[:, 0:D] = grad_mixed * out_norm
    cot = grad_mixed * gate[...]
    gains_acc[1:2, :] += jnp.sum(cot * hat_out, axis=0, keepdims=True)
    dhat = cot * gain_out
    grad_att = rstd_out * (dhat - row_mean(dhat) - hat_out * row_mean(dhat * hat_out))
    grad_half = grad_att.astype(BF)
    for s in range(GROUP // pair):
        rows = slice(s * pair, (s + 1) * pair)
        for h in range(HEADS):
            cols = slice(h * HDIM, (h + 1) * HDIM)
            gh_h = grad_half[rows, cols]
            grad_weight = dot_t(gh_h, vqk[0, rows, cols])
            gs = (grad_weight * wts[s * HEADS + h, 1].astype(F32)).astype(BF)
            gact[rows, D + h * HDIM : D + (h + 1) * HDIM] = t_dot(wts[s * HEADS + h, 0], gh_h)
            gact[rows, 2 * D + h * HDIM : 2 * D + (h + 1) * HDIM] = dot(gs, vqk[2, rows, cols])
            gact[rows, 3 * D + h * HDIM : 3 * D + (h + 1) * HDIM] = t_dot(gs, vqk[1, rows, cols])
    gh = (gact[...] * slope[...]).astype(BF)
    gh_all[here, :] = gh
    grad_normed = dot_t(gh, w_in_ref[...])
    gains_acc[0:1, :] += jnp.sum(grad_normed * hat_in, axis=0, keepdims=True)
    dhat_in = grad_normed * gain_in
    grad_inner = rstd_in * (dhat_in - row_mean(dhat_in) - hat_in * row_mean(dhat_in * hat_in))
    grad_tok = (grad_inner + gy.astype(F32)).astype(BF)
    rows_acc[...] += dot(onehot_t, grad_tok)

    @pl.when(g == N_GROUP - 1)
    def _():
        owner = jnp.broadcast_to(owner_ref[...], (UNIQ, UNIQ))
        owner_col = jnp.transpose(owner)
        before = lax.broadcasted_iota(jnp.int32, (UNIQ, UNIQ), 0) < lax.broadcasted_iota(
            jnp.int32, (UNIQ, UNIQ), 1
        )
        rank = jnp.sum(
            jnp.where((owner == owner_col) & before, 1.0, 0.0), axis=0, keepdims=True
        )
        mine = (
            lax.broadcasted_iota(jnp.int32, (N_DEV, UNIQ), 0).astype(F32) == owner_ref[...]
        )
        lane = lax.broadcasted_iota(jnp.int32, (N_DEV, 128), 1)
        row_half = rows_acc[...].astype(BF)
        meta = jnp.zeros((N_DEV, 128), F32)
        for c in range(CAP):
            sel = jnp.where(mine & (rank == float(c)), 1.0, 0.0)
            ids = jnp.sum(sel * orow_ref[...], axis=1, keepdims=True)
            meta = jnp.where(lane == c, ids, meta)
            picked = dot(sel.astype(BF), row_half)
            for k in range(4):
                spread[pl.ds(k * CAP + c, N_DEV, stride=16), :] = picked[
                    :, k * 128 : (k + 1) * 128
                ]
        send_ref[...] = spread[...].astype(BF)
        meta_ref[...] = meta.reshape(N_DEV, 1, 128)
        for k in range(5):
            if k < 4:
                block = t_dot(normed_all[...], gh_all[:, k * D : (k + 1) * D])
            else:
                block = t_dot(mixed_all[...], gy_all[...])
            for j in range(4):
                first = (k * 4 + j) * D
                flat_ref[first : first + D, :] = block[:, j * 128 : (j + 1) * 128].astype(BF)
        flat_ref[20 * D : FLAT, :] = jnp.zeros((FLAT - 20 * D, 128), BF)
        tail = jnp.concatenate(
            [gains_acc[r : r + 1, j * 128 : (j + 1) * 128] for r in range(2) for j in range(4)]
            + [jnp.zeros((8, 128), F32)],
            axis=0,
        )
        flat_ref[20 * D : 20 * D + 16, :] = tail.astype(BF)


def layer(seq_dest, items, touched, returned, owner, orow, w_in, w_out, gain_in, gain_out):
    def whole(*shape):
        return pl.BlockSpec(shape, lambda g, d: (0,) * len(shape))

    return pl.pallas_call(
        layer_kernel,
        out_shape=(
            jax.ShapeDtypeStruct((FLAT, 128), BF),
            jax.ShapeDtypeStruct((N_DEV * 16, 128), BF),
            jax.ShapeDtypeStruct((N_DEV, 1, 128), F32),
        ),
        grid_spec=pltpu.PrefetchScalarGridSpec(
            num_scalar_prefetch=1,
            grid=(N_GROUP,),
            in_specs=[
                pl.BlockSpec((1, GROUP), lambda g, d: (0, g)),
                whole(UNIQ, D),
                whole(N_DP, SLOT, D),
                whole(1, UNIQ),
                whole(1, UNIQ),
                whole(D, 4 * D),
                whole(D, D),
                whole(1, D),
                whole(1, D),
            ],
            out_specs=[whole(FLAT, 128), whole(N_DEV * 16, 128), whole(N_DEV, 1, 128)],
            scratch_shapes=[
                pltpu.VMEM((N_GROUP * GROUP, D), BF),
                pltpu.VMEM((N_GROUP * GROUP, D), BF),
                pltpu.VMEM((N_GROUP * GROUP, D), BF),
                pltpu.VMEM((N_GROUP * GROUP, 4 * D), BF),
                pltpu.VMEM((GROUP, 4 * D), F32),
                pltpu.VMEM((GROUP, D), F32),
                pltpu.VMEM((3, GROUP, D), BF),
                pltpu.VMEM((GROUP, D), F32),
                pltpu.VMEM((GROUP, 4 * D), F32),
                pltpu.VMEM((2 * HEADS, 2, 2 * SLOT, 2 * SLOT), BF),
                pltpu.VMEM((UNIQ, D), F32),
                pltpu.VMEM((8, D), F32),
                pltpu.VMEM((N_DEV * 16, 128), F32),
            ],
        ),
        compiler_params=pltpu.CompilerParams(vmem_limit_bytes=58 << 20),
        name="layer",
    )(seq_dest, items, touched, returned, owner, orow, w_in, w_out, gain_in, gain_out)


def reduce_kernel(
    a_ref,
    send_ref,
    meta_ref,
    g_ref,
    got_ref,
    gotm_ref,
    r0,
    b,
    r1,
    c1,
    r2,
    r3,
    s0,
    s1,
    s2,
    s3,
    t2,
    t1,
    t0,
    asem,
    own_sem,
):
    dp = lax.axis_index("dp")
    tb = lax.axis_index("table")
    x = dp // 4
    z = dp % 4
    y = tb // 2
    core = tb % 2
    me = dp * N_TABLE + tb
    partner = (dp, y * 2 + 1 - core)

    def device(i):
        other = lax.rem(me + i, N_DEV)
        return other, (other // N_TABLE, other % N_TABLE)

    barrier = pltpu.get_barrier_semaphore()

    def greet(i, carry):
        pl.semaphore_signal(barrier, inc=1, device_id=device(i)[1], device_id_type=MESH)
        return carry

    lax.fori_loop(1, N_DEV, greet, 0)
    pl.semaphore_wait(barrier, N_DEV - 1)

    def remote(src, dst, sems, index, to):
        return pltpu.make_async_remote_copy(
            src_ref=src,
            dst_ref=dst,
            send_sem=sems.at[(0,) + index],
            recv_sem=sems.at[(1,) + index],
            device_id=to,
            device_id_type=MESH,
        )

    coords = {"x": x, "y": y, "z": z}

    def along(axis, d):
        v = lax.rem(coords[axis] + d, 4)
        to = {"x": (v * 4 + z, tb), "z": (x * 4 + v, tb), "y": (dp, v * 2 + core)}[axis]
        return v, to

    orders = (("x", "y", "z"), ("y", "z", "x"), ("z", "x", "y"))

    def pair_copy(q):
        return remote(a_ref.at[1 - core, q], r0.at[q], s0, (q,), partner)

    for q in range(3):
        pair_copy(q).start()

    def scatter_out(i, carry):
        other, to = device(i)
        remote(send_ref.at[other], got_ref.at[i], asem, (0,), to).start()
        remote(meta_ref.at[other], gotm_ref.at[i], asem, (1,), to).start()
        return carry

    lax.fori_loop(1, N_DEV, scatter_out, 0)
    own_data = pltpu.make_async_copy(send_ref.at[me], got_ref.at[0], own_sem.at[0])
    own_meta = pltpu.make_async_copy(meta_ref.at[me], gotm_ref.at[0], own_sem.at[1])
    own_data.start()
    own_meta.start()

    def first_copy(q, d):
        v, to = along(orders[q][0], d)
        return remote(b.at[q, v], r1.at[q, d - 1], s1, (q, d - 1), to)

    for q in range(3):
        pair_copy(q).wait()

        def add0(k, carry, q=q):
            b[q, k] = (a_ref[core, q, k].astype(F32) + r0[q, k].astype(F32)).astype(BF)
            return carry

        lax.fori_loop(0, 4, add0, 0)
        for d in range(1, 4):
            first_copy(q, d).start()

    def second_copy(q, d):
        v, to = along(orders[q][1], d)
        return remote(c1.at[q, v], r2.at[q, d - 1], s2, (q, d - 1), to)

    for q in range(3):
        for d in range(1, 4):
            first_copy(q, d).wait()
        mine = coords[orders[q][0]]

        def add1(k, carry, q=q, mine=mine):
            total = b[q, mine, k].astype(F32)
            for d in range(3):
                total = total + r1[q, d, k].astype(F32)
            c1[q, k] = total.astype(BF)
            return carry

        lax.fori_loop(0, 4, add1, 0)
        for d in range(1, 4):
            second_copy(q, d).start()

    def third_copy(q, d):
        mine = coords[orders[q][2]]
        return remote(r3.at[q, mine], r3.at[q, mine], s3, (q, d - 1), along(orders[q][2], d)[1])

    for q in range(3):
        for d in range(1, 4):
            second_copy(q, d).wait()
        total = c1[q, coords[orders[q][1]]].astype(F32)
        for d in range(3):
            total = total + r2[q, d].astype(F32)
        r3[q, coords[orders[q][2]]] = total.astype(BF)
        for d in range(1, 4):
            third_copy(q, d).start()

    def piece(q):
        return g_ref.at[core, q, coords[orders[q][0]], coords[orders[q][1]]]

    def back_two(q, d):
        return remote(piece(q), piece(q), t2, (q, d - 1), along(orders[q][1], d)[1])

    for q in range(3):
        for d in range(1, 4):
            third_copy(q, d).wait()
        total = r3[q, 0].astype(F32)
        for d in range(1, 4):
            total = total + r3[q, d].astype(F32)
        g_ref[core, q, coords[orders[q][0]], coords[orders[q][1]]] = total.astype(BF)
        for d in range(1, 4):
            back_two(q, d).start()

    def back_one(q, d):
        slab = g_ref.at[core, q, coords[orders[q][0]]]
        return remote(slab, slab, t1, (q, d - 1), along(orders[q][0], d)[1])

    for q in range(3):
        for d in range(1, 4):
            back_two(q, d).wait()
        for d in range(1, 4):
            back_one(q, d).start()

    def back_pair(q):
        return remote(g_ref.at[core, q], g_ref.at[core, q], t0, (q,), partner)

    for q in range(3):
        for d in range(1, 4):
            back_one(q, d).wait()
        back_pair(q).start()

    own_data.wait()
    own_meta.wait()
    others = pl.ds(1, N_DEV - 1)
    remote(send_ref.at[others], got_ref.at[others], asem, (0,), partner).wait()
    remote(meta_ref.at[others], gotm_ref.at[others], asem, (1,), partner).wait()
    for q in range(3):
        back_pair(q).wait()


def reduce_all(flat, send, meta):
    vmem = pl.BlockSpec(memory_space=pltpu.VMEM)
    return pl.pallas_call(
        reduce_kernel,
        out_shape=(
            jax.ShapeDtypeStruct((2, 3, 4, 4, CHUNK, 128), BF),
            jax.ShapeDtypeStruct((N_DEV, 16, 128), BF),
            jax.ShapeDtypeStruct((N_DEV, 1, 128), F32),
        ),
        in_specs=[vmem] * 3,
        out_specs=(vmem,) * 3,
        scratch_shapes=[
            pltpu.VMEM((3, 4, 4, CHUNK, 128), BF),
            pltpu.VMEM((3, 4, 4, CHUNK, 128), BF),
            pltpu.VMEM((3, 3, 4, CHUNK, 128), BF),
            pltpu.VMEM((3, 4, CHUNK, 128), BF),
            pltpu.VMEM((3, 3, CHUNK, 128), BF),
            pltpu.VMEM((3, 4, CHUNK, 128), BF),
            pltpu.SemaphoreType.DMA((2, 3)),
            pltpu.SemaphoreType.DMA((2, 3, 3)),
            pltpu.SemaphoreType.DMA((2, 3, 3)),
            pltpu.SemaphoreType.DMA((2, 3, 3)),
            pltpu.SemaphoreType.DMA((2, 3, 3)),
            pltpu.SemaphoreType.DMA((2, 3, 3)),
            pltpu.SemaphoreType.DMA((2, 3)),
            pltpu.SemaphoreType.DMA((2, 2)),
            pltpu.SemaphoreType.DMA((2,)),
        ],
        compiler_params=pltpu.CompilerParams(
            collective_id=1, has_side_effects=True, vmem_limit_bytes=40 << 20
        ),
        name="reduce",
    )(flat.reshape(2, 3, 4, 4, CHUNK, 128), send.reshape(N_DEV, 16, 128), meta)


def finish_kernel(flat_ref, got_ref, meta_ref, table_ref, win_ref, wout_ref, gains_ref, spread, picked, ids, *, factor):
    i = pl.program_id(0)

    @pl.when(i == 0)
    def _():
        spread[...] = got_ref[...].astype(F32)
        for c in range(CAP):
            for k in range(4):
                picked[c * N_DEV : (c + 1) * N_DEV, k * 128 : (k + 1) * 128] = spread[
                    pl.ds(k * CAP + c, N_DEV, stride=16), :
                ].astype(BF)
        ids[...] = jnp.transpose(meta_ref[...].reshape(N_DEV, 128))
        gains_ref[...] = flat_ref[20 * D : 20 * D + 16, :].astype(F32) * factor
        for j in range(4):
            first = (16 + j) * D
            wout_ref[:, j * 128 : (j + 1) * 128] = flat_ref[first : first + D, :].astype(F32) * factor

    rows = (lax.broadcasted_iota(jnp.int32, (256, N_DEV), 0) + i * 256).astype(F32)
    hot = jnp.concatenate(
        [jnp.where(rows == ids[c : c + 1, :], 1.0, 0.0).astype(BF) for c in range(CAP)], axis=1
    )
    table_ref[...] = dot(hot, picked[...])
    for j in range(4):
        first = pl.multiple_of((i * 4 + j) * D, D)
        win_ref[:, j * 128 : (j + 1) * 128] = flat_ref[pl.ds(first, D), :].astype(F32) * factor


def finish(flat, got, meta, factor):
    def whole(*shape):
        return pl.BlockSpec(shape, lambda i: (0,) * len(shape))

    def body(*refs):
        finish_kernel(*refs, factor=factor)

    return pl.pallas_call(
        body,
        out_shape=(
            jax.ShapeDtypeStruct((ROWS_DEV, D), F32),
            jax.ShapeDtypeStruct((D, 4 * D), F32),
            jax.ShapeDtypeStruct((D, D), F32),
            jax.ShapeDtypeStruct((16, 128), F32),
        ),
        grid=(4,),
        in_specs=[whole(FLAT, 128), whole(N_DEV * 16, 128), whole(N_DEV, 1, 128)],
        out_specs=(
            pl.BlockSpec((256, D), lambda i: (i, 0)),
            pl.BlockSpec((D, D), lambda i: (0, i)),
            whole(D, D),
            whole(16, 128),
        ),
        scratch_shapes=[
            pltpu.VMEM((N_DEV * 16, 128), F32),
            pltpu.VMEM((CAP * N_DEV, D), BF),
            pltpu.VMEM((128, N_DEV), F32),
        ],
        compiler_params=pltpu.CompilerParams(vmem_limit_bytes=40 << 20),
        name="finish",
    )(flat.reshape(FLAT, 128), got.reshape(N_DEV * 16, 128), meta)


def on_device(
    touched_rows,
    row_of_token,
    row_owner,
    owner_row,
    seq_blocks,
    seq_dest,
    grad_out,
    w_in,
    w_out,
    gain_in,
    gain_out,
):
    peers = jnp.arange(N_DP, dtype=jnp.int32)
    matches = seq_dest[None, :] == peers[:, None]
    lengths = jnp.sum(jnp.where(matches, seq_blocks[None, :], 0), axis=1)
    lens = jnp.broadcast_to(lengths[:, None, None], (N_DP, 1, D))
    returned = exchange_cotangents(lens, grad_out)
    flat, send, meta = layer(
        seq_dest,
        row_of_token.reshape(1, -1),
        touched_rows,
        returned,
        row_owner.reshape(1, -1).astype(F32),
        owner_row.reshape(1, -1).astype(F32),
        w_in,
        w_out,
        gain_in.reshape(1, -1),
        gain_out.reshape(1, -1),
    )
    flat, got, meta = reduce_all(flat, send, meta)
    factor = 1.0 / math.sqrt(grad_out.shape[0] * N_DEV)
    table, grad_in, grad_w_out, gains = finish(flat, got, meta, factor)
    return (
        table,
        grad_in,
        grad_w_out,
        gains[0:4].reshape(-1),
        gains[4:8].reshape(-1),
    )


def solution(mesh):
    in_specs = (
        P(("dp", "table"), None),
        P(("dp", "table")),
        P(("dp", "table"), None),
        P(("dp", "table")),
        P(("dp", "table")),
        P(("dp", "table")),
        P(("dp", "table"), None),
        P(),
        P(),
        P(),
        P(),
    )
    out_specs = (P(("dp", "table"), None), P(), P(), P(), P())
    return jax.shard_map(
        on_device, mesh=mesh, in_specs=in_specs, out_specs=out_specs, check_vma=False
    )
```

```python
import math

import jax
import jax.numpy as jnp
from jax import lax
from jax.experimental import pallas as pl
from jax.experimental.pallas import tpu as pltpu
from jax.sharding import PartitionSpec as P

HEADS = 4
HDIM = 128
BLK = 16
LMAXB = 4
SLOT = 64
ROWS_DEV = 1024
UNIQ = 256
CAP = 4
D = 512
N_DP = 16
N_TABLE = 8
N_DEV = 128
GROUP = 256
N_GROUP = 4
TOK = 1024
PAIR = 128
CH1 = 48
CH2 = 64
ROWS1 = 96 * CH1
ROWS2 = 96 * CH2
EPSILON = 1e-05
MESH = pl.DeviceIdType.MESH
BF = jnp.bfloat16
F32 = jnp.float32


def dot(a, b):
    return jnp.dot(a, b, preferred_element_type=F32)


def dot_t(a, b):
    return lax.dot_general(a, b, (((1,), (1,)), ((), ())), preferred_element_type=F32)


def t_dot(a, b):
    return lax.dot_general(a, b, (((0,), (0,)), ((), ())), preferred_element_type=F32)


OFFSETS = (
    (0, 1), (1, 0), (3, 0), (0, 3),
    (1, 1), (3, 3), (0, 2), (2, 0),
    (1, 3), (3, 1), (1, 2), (2, 1),
    (3, 2), (2, 3), (2, 2), (0, 0),
)
OWN = 15
ORDERS = (("x", "y", "z"), ("y", "z", "x"), ("z", "x", "y"))


def row_mean(v):
    return jnp.sum(v, axis=-1, keepdims=True) * (1.0 / D)


def sigmoid(v):
    return 0.5 * jnp.tanh(0.5 * v) + 0.5


def iota(shape, dim):
    return lax.broadcasted_iota(jnp.int32, shape, dim)


def step_kernel(
    dest_s,
    dest_l,
    blocks_l,
    items_ref,
    owner_ref,
    orow_ref,
    gin_ref,
    gout_ref,
    touched_hbm,
    grad_hbm,
    w_in_hbm,
    w_out_hbm,
    g1_ref,
    g2_ref,
    got_ref,
    gotm_ref,
    gains_ref,
    touched,
    grad_bal,
    w_in,
    w_out,
    load_sem,
    lens,
    got_len,
    wide,
    stage,
    ret,
    lsem,
    dsem,
    own_sem,
    hot_all,
    norm_t,
    mixed_t,
    hat_in_all,
    rstd_in_all,
    hat_out_all,
    rstd_out_all,
    slope_all,
    gate_all,
    vqk_all,
    att,
    wts,
    half_all,
    gh_all,
    rows_acc,
    gains_acc,
    spread,
    send,
    meta,
    a1,
    a2,
    pr1,
    pr2,
    b1,
    b2,
    fr1,
    fr2,
    c1,
    c2,
    sr1,
    sr2,
    tr1,
    tr2,
    gbuf,
    psem,
    rsem,
    asem,
    gsem,
):
    dp = lax.axis_index("dp")
    tb = lax.axis_index("table")
    x = dp // 4
    z = dp % 4
    y = tb // 2
    core = tb % 2
    me = dp * N_TABLE + tb
    partner = (dp, y * 2 + 1 - core)
    coords = {"x": x, "y": y, "z": z}

    def device(i):
        other = lax.rem(me + i, N_DEV)
        return other, (other // N_TABLE, other % N_TABLE)

    def along(axis, d):
        v = lax.rem(coords[axis] + d, 4)
        to = {"x": (v * 4 + z, tb), "z": (x * 4 + v, tb), "y": (dp, v * 2 + core)}[axis]
        return v, to

    def plus(i):
        dx, dz = OFFSETS[i]
        return lax.rem(x + dx, 4) * 4 + lax.rem(z + dz, 4)

    def minus(i):
        dx, dz = OFFSETS[i]
        return lax.rem(x + 4 - dx, 4) * 4 + lax.rem(z + 4 - dz, 4)

    def remote(src, dst, sems, index, to):
        return pltpu.make_async_remote_copy(
            src_ref=src,
            dst_ref=dst,
            send_sem=sems.at[(0,) + index],
            recv_sem=sems.at[(1,) + index],
            device_id=to,
            device_id_type=MESH,
        )

    loads = [
        pltpu.make_async_copy(touched_hbm, touched, load_sem.at[0]),
        pltpu.make_async_copy(w_in_hbm, w_in, load_sem.at[1]),
        pltpu.make_async_copy(grad_hbm, grad_bal, load_sem.at[2]),
        pltpu.make_async_copy(w_out_hbm, w_out, load_sem.at[3]),
    ]
    for load in loads:
        load.start()

    barrier = pltpu.get_barrier_semaphore()

    def greet(i, carry):
        pl.semaphore_signal(barrier, inc=1, device_id=device(i)[1], device_id_type=MESH)
        return carry

    lax.fori_loop(1, N_DEV, greet, 0)

    hits = dest_l[...] == iota((N_DP, N_DP), 0)
    lengths = jnp.sum(
        jnp.where(hits, blocks_l[...].astype(F32), 0.0), axis=1, keepdims=True
    )
    lengths = jnp.broadcast_to(lengths, (N_DP, D)).astype(jnp.int32)
    for p in range(N_DP):
        lens[p] = lengths[p : p + 1, :]

    gain_in = gin_ref[...]
    gain_out = gout_ref[...]
    gains_acc[...] = jnp.zeros_like(gains_acc)
    lane = iota((1, 128), 1)

    def item_pair(i):
        rows = []
        for k in range(2):
            peer = plus(i + k)
            slot = jnp.int32(0)
            for j in range(N_DP):
                slot = jnp.where(dest_s[j] == peer, j, slot)
            row = items_ref[pl.ds(slot // 2, 1), :]
            turned = pltpu.roll(row, 64, 1)
            rows.append(jnp.where(jnp.broadcast_to(slot % 2, (1, 128)) == k, row, turned))
        return jnp.where(lane < 64, rows[0], rows[1])

    def forward(g):
        here = slice(g * GROUP, (g + 1) * GROUP)
        items = jnp.concatenate([item_pair(4 * g), item_pair(4 * g + 2)], axis=1)
        hot = (iota((UNIQ, GROUP), 0) == items).astype(F32).astype(BF)
        hot_all[:, here] = hot
        tok = t_dot(hot, touched[...])
        shifted = tok - row_mean(tok)
        rstd = lax.rsqrt(row_mean(shifted * shifted) + EPSILON)
        rstd_in_all[here, :] = rstd
        hat = shifted * rstd
        hat_in_all[here, :] = hat
        normed = hat * gain_in
        norm_t[:, here] = jnp.transpose(normed).astype(BF)
        normed = normed.astype(BF)
        for k in range(4):
            cols = slice(k * D, (k + 1) * D)
            hid = dot(normed, w_in[:, cols])
            sig = sigmoid(hid)
            act = hid * sig
            slope_all[here, cols] = sig + act * (1.0 - sig)
            if k == 0:
                gate_all[here, :] = act
            else:
                vqk_all[k - 1, here, :] = act.astype(BF)
        ri = iota((PAIR, PAIR), 0)
        ci = iota((PAIR, PAIR), 1)
        allowed = ((ri < SLOT) == (ci < SLOT)) & (ci <= ri)
        scale = HDIM ** (-0.5)
        for s in range(2):
            rows = slice(g * GROUP + s * PAIR, g * GROUP + (s + 1) * PAIR)
            for h in range(HEADS):
                cols = slice(h * HDIM, (h + 1) * HDIM)
                n = (g * 2 + s) * HEADS + h
                score = dot_t(vqk_all[1, rows, cols], vqk_all[2, rows, cols]) * scale
                sig = sigmoid(score)
                act = score * sig
                weight = jnp.where(allowed, act, 0.0).astype(BF)
                wts[n, 0] = weight
                wts[n, 1] = jnp.where(allowed, (sig + act * (1.0 - sig)) * scale, 0.0).astype(BF)
                att[s * PAIR : (s + 1) * PAIR, cols] = dot(weight, vqk_all[0, rows, cols])
        attended = att[...]
        shifted = attended - row_mean(attended)
        rstd = lax.rsqrt(row_mean(shifted * shifted) + EPSILON)
        rstd_out_all[here, :] = rstd
        hat = shifted * rstd
        hat_out_all[here, :] = hat
        mixed_t[:, here] = jnp.transpose(hat * gain_out * gate_all[here, :]).astype(BF)

    loads[0].wait()
    loads[1].wait()
    forward(0)

    pl.semaphore_wait(barrier, N_DEV - 1)

    def len_copy(i):
        return remote(lens.at[minus(i)], got_len.at[dp], lsem, (i,), (minus(i), tb))

    for i in range(OWN):
        len_copy(i).start()
    got_len[dp] = lens[dp]
    forward(1)
    for i in range(OWN):
        len_copy(i).wait()
    loads[2].wait()
    loads[3].wait()

    start = jnp.zeros((1, D), jnp.int32)
    for p in range(N_DP):
        wide[p] = start
        start = start + got_len[p]
    row_id = iota((SLOT, D), 0)
    col_id = iota((SLOT, D), 1)

    def staged(p):
        hit = (col_id == wide[p] * BLK + row_id) & (row_id < got_len[p] * BLK)
        return dot(hit.astype(F32).astype(BF), grad_bal[...]).astype(BF)

    def data_copy(i):
        return remote(stage.at[i], ret.at[i], dsem, (i,), (minus(i), tb))

    for i in range(OWN):
        stage[i] = staged(minus(i))
        data_copy(i).start()
    ret[OWN] = staged(dp)

    forward(2)
    forward(3)

    def back_a(g):
        here = slice(g * GROUP, (g + 1) * GROUP)
        gy = ret[4 * g : 4 * g + 4].reshape(GROUP, D)
        hat = hat_out_all[here, :]
        grad_mixed = dot_t(gy, w_out[...])
        gh_all[here, 0:D] = (grad_mixed * (hat * gain_out) * slope_all[here, 0:D]).astype(BF)
        cot = grad_mixed * gate_all[here, :]
        gains_acc[1:2, :] += jnp.sum(cot * hat, axis=0, keepdims=True)
        dhat = cot * gain_out
        half_all[here, :] = (
            rstd_out_all[here, :] * (dhat - row_mean(dhat) - hat * row_mean(dhat * hat))
        ).astype(BF)

    def back_b(g):
        for s in range(2):
            rows = slice(g * GROUP + s * PAIR, g * GROUP + (s + 1) * PAIR)
            for h in range(HEADS):
                cols = slice(h * HDIM, (h + 1) * HDIM)
                n = (g * 2 + s) * HEADS + h
                half = half_all[rows, cols]
                grad_weight = dot_t(half, vqk_all[0, rows, cols])
                gs = (grad_weight * wts[n, 1].astype(F32)).astype(BF)
                parts = (
                    t_dot(wts[n, 0], half),
                    dot(gs, vqk_all[2, rows, cols]),
                    t_dot(gs, vqk_all[1, rows, cols]),
                )
                for k in range(3):
                    at = slice((k + 1) * D + h * HDIM, (k + 1) * D + (h + 1) * HDIM)
                    gh_all[rows, at] = (parts[k] * slope_all[rows, at]).astype(BF)

    def back_c(g):
        here = slice(g * GROUP, (g + 1) * GROUP)
        gy = ret[4 * g : 4 * g + 4].reshape(GROUP, D).astype(F32)
        hat = hat_in_all[here, :]
        grad_normed = dot_t(gh_all[here, :], w_in[...])
        gains_acc[0:1, :] += jnp.sum(grad_normed * hat, axis=0, keepdims=True)
        dhat = grad_normed * gain_in
        inner = rstd_in_all[here, :] * (dhat - row_mean(dhat) - hat * row_mean(dhat * hat))
        grad_tok = (inner + gy).astype(BF)
        part = dot(hot_all[:, here], grad_tok)
        if g == 0:
            rows_acc[...] = part
        else:
            rows_acc[...] += part

    def put(dst, first, block):
        for j in range(4):
            dst[first + j * D : first + (j + 1) * D, :] = block[:, j * 128 : (j + 1) * 128].astype(BF)

    def all_reduce(s, ch, a, pr, b, fr, c, sr, tr, out):
        third = 16 * ch
        quarter = 4 * ch

        def at(row, size):
            return pl.ds(pl.multiple_of(row, 16), size)

        def pair(q):
            src = a.at[at(((1 - core) * 3 + q) * third, third)]
            return remote(src, pr.at[q], psem, (s, 0, q), partner)

        def first(q, d):
            v, to = along(ORDERS[q][0], d)
            return remote(b.at[q, at(v * quarter, quarter)], fr.at[q, d - 1], rsem, (s, 0, q, d - 1), to)

        def second(q, d):
            v, to = along(ORDERS[q][1], d)
            return remote(c.at[q, at(v * ch, ch)], sr.at[q, d - 1], rsem, (s, 1, q, d - 1), to)

        def third_copy(q, d):
            mine = coords[ORDERS[q][2]]
            to = along(ORDERS[q][2], d)[1]
            return remote(tr.at[q, mine], tr.at[q, mine], rsem, (s, 2, q, d - 1), to)

        def row_of(q, depth):
            row = (core * 3 + q) * third
            if depth > 0:
                row = row + coords[ORDERS[q][0]] * quarter
            if depth > 1:
                row = row + coords[ORDERS[q][1]] * ch
            return row

        def back_two(q, d):
            ref = out.at[at(row_of(q, 2), ch)]
            return remote(ref, ref, rsem, (s, 3, q, d - 1), along(ORDERS[q][1], d)[1])

        def back_one(q, d):
            ref = out.at[at(row_of(q, 1), quarter)]
            return remote(ref, ref, rsem, (s, 4, q, d - 1), along(ORDERS[q][0], d)[1])

        def back_pair(q):
            ref = out.at[at(row_of(q, 0), third)]
            return remote(ref, ref, psem, (s, 1, q), partner)

        for q in range(3):
            pair(q).start()
        yield
        for q in range(3):
            pair(q).wait()

            def add0(k, carry, q=q):
                rows = at(k * quarter, quarter)
                own = a[at((core * 3 + q) * third + k * quarter, quarter), :].astype(F32)
                b[q, rows, :] = (own + pr[q, rows, :].astype(F32)).astype(BF)
                return carry

            lax.fori_loop(0, 4, add0, 0)
            for d in range(1, 4):
                first(q, d).start()
        yield
        for q in range(3):
            for d in range(1, 4):
                first(q, d).wait()
            total = b[q, at(coords[ORDERS[q][0]] * quarter, quarter), :].astype(F32)
            for d in range(3):
                total = total + fr[q, d].astype(F32)
            c[q] = total.astype(BF)
            for d in range(1, 4):
                second(q, d).start()
        yield
        for q in range(3):
            for d in range(1, 4):
                second(q, d).wait()
            total = c[q, at(coords[ORDERS[q][1]] * ch, ch), :].astype(F32)
            for d in range(3):
                total = total + sr[q, d].astype(F32)
            tr[q, coords[ORDERS[q][2]]] = total.astype(BF)
            for d in range(1, 4):
                third_copy(q, d).start()
        yield
        for q in range(3):
            for d in range(1, 4):
                third_copy(q, d).wait()
            total = tr[q, 0].astype(F32)
            for d in range(1, 4):
                total = total + tr[q, d].astype(F32)
            out[at(row_of(q, 2), ch), :] = total.astype(BF)
            for d in range(1, 4):
                back_two(q, d).start()
        yield
        for q in range(3):
            for d in range(1, 4):
                back_two(q, d).wait()
            for d in range(1, 4):
                back_one(q, d).start()
        yield
        for q in range(3):
            for d in range(1, 4):
                back_one(q, d).wait()
            back_pair(q).start()
        yield
        for q in range(3):
            back_pair(q).wait()
        yield

    def gain_reduce():
        def pair():
            ref = gbuf.at[0, core]
            return remote(ref, ref, gsem, (0, 0), partner)

        def copy(k, d):
            axis = "xyz"[k - 1]
            ref = gbuf.at[k, coords[axis]]
            return remote(ref, ref, gsem, (k, d - 1), along(axis, d)[1])

        gbuf[0, core] = jnp.concatenate(
            [gains_acc[r : r + 1, j * 128 : (j + 1) * 128] for r in range(2) for j in range(4)],
            axis=0,
        )
        pair().start()
        yield
        pair().wait()
        total = gbuf[0, 0] + gbuf[0, 1]
        for k in range(1, 4):
            gbuf[k, coords["xyz"[k - 1]]] = total
            for d in range(1, 4):
                copy(k, d).start()
            yield
            for d in range(1, 4):
                copy(k, d).wait()
            total = (gbuf[k, 0] + gbuf[k, 1]) + (gbuf[k, 2] + gbuf[k, 3])
        gains_ref[...] = total
        yield

    red1 = all_reduce(0, CH1, a1, pr1, b1, fr1, c1, sr1, tr1, g1_ref)
    red2 = all_reduce(1, CH2, a2, pr2, b2, fr2, c2, sr2, tr2, g2_ref)
    red_g = gain_reduce()

    for g in range(N_GROUP):
        for i in range(4 * g, min(4 * g + 4, OWN)):
            data_copy(i).wait_recv()
        back_a(g)
    put(a1, 0, dot(mixed_t[...], ret[...].reshape(TOK, D)))
    put(a1, 4 * D, dot(norm_t[...], gh_all[:, 0:D]))
    a1[8 * D : ROWS1, :] = jnp.zeros((ROWS1 - 8 * D, 128), BF)
    next(red1)
    back_b(0)
    next(red1)
    back_b(1)
    back_b(2)
    next(red1)
    back_b(3)
    for k in range(3):
        put(a2, k * 4 * D, dot(norm_t[...], gh_all[:, (k + 1) * D : (k + 2) * D]))
    next(red2)
    next(red1)
    back_c(0)
    next(red2)
    next(red1)
    back_c(1)
    next(red1)
    back_c(2)
    next(red2)
    back_c(3)

    owner = jnp.broadcast_to(owner_ref[...].astype(F32), (UNIQ, UNIQ))
    owner_col = jnp.transpose(owner)
    before = iota((UNIQ, UNIQ), 0) < iota((UNIQ, UNIQ), 1)
    rank = jnp.sum(jnp.where((owner == owner_col) & before, 1.0, 0.0), axis=0, keepdims=True)
    mine = iota((N_DEV, UNIQ), 0) == owner_ref[...]
    lanes = iota((N_DEV, 128), 1)
    row_half = rows_acc[...].astype(BF)
    ids_all = jnp.zeros((N_DEV, 128), F32)
    order_f = orow_ref[...].astype(F32)
    for c in range(CAP):
        sel = jnp.where(mine & (rank == float(c)), 1.0, 0.0)
        ids = jnp.sum(sel * order_f, axis=1, keepdims=True)
        ids_all = jnp.where(lanes == c, ids, ids_all)
        picked = dot(sel.astype(BF), row_half)
        for k in range(4):
            spread[pl.ds(k * CAP + c, N_DEV, stride=16), :] = picked[:, k * 128 : (k + 1) * 128]
    send[...] = spread[...].astype(BF).reshape(N_DEV, 16, 128)
    meta[...] = ids_all.reshape(N_DEV, 1, 128)

    next(red_g)

    def scatter_out(i, carry):
        other, to = device(i)
        remote(send.at[other], got_ref.at[i], asem, (0,), to).start()
        remote(meta.at[other], gotm_ref.at[i], asem, (1,), to).start()
        return carry

    lax.fori_loop(1, N_DEV, scatter_out, 0)
    got_ref[0] = send[me]
    gotm_ref[0] = meta[me]

    next(red2)
    next(red_g)
    next(red1)
    next(red2)
    next(red_g)
    next(red2)
    next(red_g)
    next(red2)
    next(red_g)
    next(red1)
    others = pl.ds(1, N_DEV - 1)
    remote(send.at[others], got_ref.at[others], asem, (0,), partner).wait()
    remote(meta.at[others], gotm_ref.at[others], asem, (1,), partner).wait()
    for i in range(OWN):
        data_copy(i).wait_send()
    next(red2)


def run_step(seq_dest, seq_blocks, items, owner, orow, gain_in, gain_out, touched, grad_out, w_in, w_out):
    smem = pl.BlockSpec(memory_space=pltpu.SMEM)
    vmem = pl.BlockSpec(memory_space=pltpu.VMEM)
    far = pl.BlockSpec(memory_space=pl.ANY)
    v = pltpu.VMEM
    dma = pltpu.SemaphoreType.DMA
    scratch = [
        v((UNIQ, D), BF),
        v((D, D), BF),
        v((D, 4 * D), BF),
        v((D, D), BF),
        dma((4,)),
        v((N_DP, 1, D), jnp.int32),
        v((N_DP, 1, D), jnp.int32),
        v((N_DP, 1, D), jnp.int32),
        v((N_DP, SLOT, D), BF),
        v((N_DP, SLOT, D), BF),
        dma((2, N_DP)),
        dma((2, N_DP)),
        dma((1,)),
        v((UNIQ, TOK), BF),
        v((D, TOK), BF),
        v((D, TOK), BF),
        v((TOK, D), F32),
        v((TOK, 1), F32),
        v((TOK, D), F32),
        v((TOK, 1), F32),
        v((TOK, 4 * D), F32),
        v((TOK, D), F32),
        v((3, TOK, D), BF),
        v((GROUP, D), F32),
        v((N_GROUP * 2 * HEADS, 2, PAIR, PAIR), BF),
        v((TOK, D), BF),
        v((TOK, 4 * D), BF),
        v((UNIQ, D), F32),
        v((8, D), F32),
        v((N_DEV * 16, 128), F32),
        v((N_DEV, 16, 128), BF),
        v((N_DEV, 1, 128), F32),
        v((ROWS1, 128), BF),
        v((ROWS2, 128), BF),
    ]
    for shape in ((3, 16), (3, 16), (3, 3, 4), (3, 4), (3, 3, 1), (3, 4, 1)):
        for ch in (CH1, CH2):
            scratch.append(v(shape[:-1] + (shape[-1] * ch, 128), BF))
    scratch += [
        v((4, 4, 8, 128), F32),
        dma((2, 2, 2, 3)),
        dma((2, 2, 5, 3, 3)),
        dma((2, 2)),
        dma((2, 4, 3)),
    ]
    return pl.pallas_call(
        step_kernel,
        out_shape=(
            jax.ShapeDtypeStruct((ROWS1, 128), BF),
            jax.ShapeDtypeStruct((ROWS2, 128), BF),
            jax.ShapeDtypeStruct((N_DEV, 16, 128), BF),
            jax.ShapeDtypeStruct((N_DEV, 1, 128), F32),
            jax.ShapeDtypeStruct((8, 128), F32),
        ),
        in_specs=[smem] + [vmem] * 7 + [far] * 4,
        out_specs=(vmem,) * 5,
        scratch_shapes=scratch,
        compiler_params=pltpu.CompilerParams(
            collective_id=0, has_side_effects=True, vmem_limit_bytes=67_000_000
        ),
        name="step",
    )(
        seq_dest,
        seq_dest.reshape(1, -1),
        seq_blocks.reshape(1, -1),
        items.reshape(8, 128),
        owner.reshape(1, -1),
        orow.reshape(1, -1),
        gain_in.reshape(1, -1),
        gain_out.reshape(1, -1),
        touched,
        grad_out,
        w_in,
        w_out,
    )


def finish_kernel(
    out_ref, gate_ref, rest_ref, got_ref, meta_ref, gains_in, table_ref, win_ref, wout_ref, gin_ref, gout_ref, spread, picked, ids, *, factor
):
    i = pl.program_id(0)

    def unpack(src, dst):
        for j in range(4):
            dst[:, j * 128 : (j + 1) * 128] = src[j * D : (j + 1) * D, :].astype(F32) * factor

    @pl.when(i == 0)
    def _():
        spread[...] = got_ref[...].astype(F32)
        for c in range(CAP):
            for k in range(4):
                picked[c * N_DEV : (c + 1) * N_DEV, k * 128 : (k + 1) * 128] = spread[
                    pl.ds(k * CAP + c, N_DEV, stride=16), :
                ].astype(BF)
        ids[...] = jnp.transpose(meta_ref[...].reshape(N_DEV, 128))
        for j in range(4):
            gin_ref[:, j * 128 : (j + 1) * 128] = gains_in[j : j + 1, :] * factor
            gout_ref[:, j * 128 : (j + 1) * 128] = gains_in[4 + j : 5 + j, :] * factor
        unpack(out_ref, wout_ref)
        unpack(gate_ref, win_ref)

    @pl.when(i > 0)
    def _():
        unpack(rest_ref, win_ref)

    rows = (iota((256, N_DEV), 0) + i * 256).astype(F32)
    hot = jnp.concatenate(
        [jnp.where(rows == ids[c : c + 1, :], 1.0, 0.0).astype(BF) for c in range(CAP)], axis=1
    )
    table_ref[...] = dot(hot, picked[...])


def finish(g1, g2, got, meta, gains, factor):
    def fixed(*shape):
        return pl.BlockSpec(shape, lambda i: (0,) * len(shape))

    def body(*refs):
        finish_kernel(*refs, factor=factor)

    return pl.pallas_call(
        body,
        out_shape=(
            jax.ShapeDtypeStruct((ROWS_DEV, D), F32),
            jax.ShapeDtypeStruct((D, 4 * D), F32),
            jax.ShapeDtypeStruct((D, D), F32),
            jax.ShapeDtypeStruct((1, D), F32),
            jax.ShapeDtypeStruct((1, D), F32),
        ),
        grid=(4,),
        in_specs=[
            pl.BlockSpec((4 * D, 128), lambda i: (0, 0)),
            pl.BlockSpec((4 * D, 128), lambda i: (1, 0)),
            pl.BlockSpec((4 * D, 128), lambda i: (jnp.maximum(i - 1, 0), 0)),
            fixed(N_DEV * 16, 128),
            fixed(N_DEV, 1, 128),
            fixed(8, 128),
        ],
        out_specs=(
            pl.BlockSpec((256, D), lambda i: (i, 0)),
            pl.BlockSpec((D, D), lambda i: (0, i)),
            fixed(D, D),
            fixed(1, D),
            fixed(1, D),
        ),
        scratch_shapes=[
            pltpu.VMEM((N_DEV * 16, 128), F32),
            pltpu.VMEM((CAP * N_DEV, D), BF),
            pltpu.VMEM((128, N_DEV), F32),
        ],
        compiler_params=pltpu.CompilerParams(vmem_limit_bytes=40 << 20),
        name="finish",
    )(g1, g1, g2, got.reshape(N_DEV * 16, 128), meta, gains)


def on_device(
    touched_rows,
    row_of_token,
    row_owner,
    owner_row,
    seq_blocks,
    seq_dest,
    grad_out,
    w_in,
    w_out,
    gain_in,
    gain_out,
):
    g1, g2, got, meta, gains = run_step(
        seq_dest,
        seq_blocks,
        row_of_token,
        row_owner,
        owner_row,
        gain_in,
        gain_out,
        touched_rows,
        grad_out,
        w_in,
        w_out,
    )
    factor = 1.0 / math.sqrt(grad_out.shape[0] * N_DEV)
    table, grad_in, grad_w_out, gin, gout = finish(g1, g2, got, meta, gains, factor)
    return (table, grad_in, grad_w_out, gin.reshape(-1), gout.reshape(-1))


def solution(mesh):
    in_specs = (
        P(("dp", "table"), None),
        P(("dp", "table")),
        P(("dp", "table"), None),
        P(("dp", "table")),
        P(("dp", "table")),
        P(("dp", "table")),
        P(("dp", "table"), None),
        P(),
        P(),
        P(),
        P(),
    )
    out_specs = (P(("dp", "table"), None), P(), P(), P(), P())
    return jax.shard_map(
        on_device, mesh=mesh, in_specs=in_specs, out_specs=out_specs, check_vma=False
    )
```

```python
import math

import jax
import jax.numpy as jnp
from jax import lax
from jax.experimental import pallas as pl
from jax.experimental.pallas import tpu as pltpu
from jax.sharding import PartitionSpec as P

HEADS = 4
HDIM = 128
BLK = 16
LMAXB = 4
SLOT = 64
ROWS_DEV = 1024
UNIQ = 256
CAP = 4
D = 512
N_DP = 16
N_TABLE = 8
N_DEV = 128
GROUP = 256
N_GROUP = 4
TOK = 1024
PAIR = 128
CH1 = 48
CH2 = 64
ROWS1 = 96 * CH1
ROWS2 = 96 * CH2
EPSILON = 1e-05
MESH = pl.DeviceIdType.MESH
BF = jnp.bfloat16
F32 = jnp.float32


def dot(a, b):
    return jnp.dot(a, b, preferred_element_type=F32)


def dot_t(a, b):
    return lax.dot_general(a, b, (((1,), (1,)), ((), ())), preferred_element_type=F32)


def t_dot(a, b):
    return lax.dot_general(a, b, (((0,), (0,)), ((), ())), preferred_element_type=F32)


OFFSETS = (
    (0, 1), (1, 0), (3, 0), (0, 3),
    (1, 1), (3, 3), (0, 2), (2, 0),
    (1, 3), (3, 1), (1, 2), (2, 1),
    (3, 2), (2, 3), (2, 2), (0, 0),
)
OWN = 15
ORDERS = (("x", "y", "z"), ("y", "z", "x"), ("z", "x", "y"))


def row_mean(v):
    return jnp.sum(v, axis=-1, keepdims=True) * (1.0 / D)


def sigmoid(v):
    return 0.5 * jnp.tanh(0.5 * v) + 0.5


def iota(shape, dim):
    return lax.broadcasted_iota(jnp.int32, shape, dim)


def step_kernel(
    dest_s,
    dest_l,
    blocks_l,
    items_ref,
    owner_ref,
    orow_ref,
    gin_ref,
    gout_ref,
    touched_hbm,
    grad_hbm,
    w_in_hbm,
    w_out_hbm,
    g1_ref,
    g2_ref,
    got_ref,
    gotm_ref,
    gains_ref,
    touched,
    grad_bal,
    w_in,
    w_out,
    load_sem,
    lens,
    got_len,
    wide,
    stage,
    ret,
    lsem,
    dsem,
    own_sem,
    hot_all,
    norm_t,
    mixed_t,
    hat_in_all,
    rstd_in_all,
    hat_out_all,
    rstd_out_all,
    slope_all,
    gate_all,
    vqk_all,
    att,
    wts,
    half_all,
    gh_all,
    rows_acc,
    gains_acc,
    spread,
    send,
    meta,
    sel_all,
    a1,
    a2,
    pr1,
    pr2,
    b1,
    b2,
    fr1,
    fr2,
    c1,
    c2,
    sr1,
    sr2,
    tr1,
    tr2,
    gbuf,
    psem,
    rsem,
    bsem,
    asem,
    gsem,
):
    dp = lax.axis_index("dp")
    tb = lax.axis_index("table")
    x = dp // 4
    z = dp % 4
    y = tb // 2
    core = tb % 2
    me = dp * N_TABLE + tb
    partner = (dp, y * 2 + 1 - core)
    coords = {"x": x, "y": y, "z": z}

    def device(i):
        other = lax.rem(me + i, N_DEV)
        return other, (other // N_TABLE, other % N_TABLE)

    def along(axis, d):
        v = lax.rem(coords[axis] + d, 4)
        to = {"x": (v * 4 + z, tb), "z": (x * 4 + v, tb), "y": (dp, v * 2 + core)}[axis]
        return v, to

    def plus(i):
        dx, dz = OFFSETS[i]
        return lax.rem(x + dx, 4) * 4 + lax.rem(z + dz, 4)

    def minus(i):
        dx, dz = OFFSETS[i]
        return lax.rem(x + 4 - dx, 4) * 4 + lax.rem(z + 4 - dz, 4)

    def remote(src, dst, sems, index, to):
        return pltpu.make_async_remote_copy(
            src_ref=src,
            dst_ref=dst,
            send_sem=sems.at[(0,) + index],
            recv_sem=sems.at[(1,) + index],
            device_id=to,
            device_id_type=MESH,
        )

    loads = [
        pltpu.make_async_copy(touched_hbm, touched, load_sem.at[0]),
        pltpu.make_async_copy(w_in_hbm, w_in, load_sem.at[1]),
        pltpu.make_async_copy(grad_hbm, grad_bal, load_sem.at[2]),
        pltpu.make_async_copy(w_out_hbm, w_out, load_sem.at[3]),
    ]
    for load in loads:
        load.start()

    barrier = pltpu.get_barrier_semaphore()

    def greet(i, carry):
        pl.semaphore_signal(barrier, inc=1, device_id=device(i)[1], device_id_type=MESH)
        return carry

    lax.fori_loop(1, N_DEV, greet, 0)

    hits = dest_l[...] == iota((N_DP, N_DP), 0)
    lengths = jnp.sum(
        jnp.where(hits, blocks_l[...].astype(F32), 0.0), axis=1, keepdims=True
    )
    lengths = jnp.broadcast_to(lengths, (N_DP, D)).astype(jnp.int32)
    for p in range(N_DP):
        lens[p] = lengths[p : p + 1, :]

    gain_in = gin_ref[...]
    gain_out = gout_ref[...]
    gains_acc[...] = jnp.zeros_like(gains_acc)
    lane = iota((1, 128), 1)

    def item_pair(i):
        rows = []
        for k in range(2):
            peer = plus(i + k)
            slot = jnp.int32(0)
            for j in range(N_DP):
                slot = jnp.where(dest_s[j] == peer, j, slot)
            row = items_ref[pl.ds(slot // 2, 1), :]
            turned = pltpu.roll(row, 64, 1)
            rows.append(jnp.where(jnp.broadcast_to(slot % 2, (1, 128)) == k, row, turned))
        return jnp.where(lane < 64, rows[0], rows[1])

    def forward(g):
        here = slice(g * GROUP, (g + 1) * GROUP)
        items = jnp.concatenate([item_pair(4 * g), item_pair(4 * g + 2)], axis=1)
        hot = (iota((UNIQ, GROUP), 0) == items).astype(F32).astype(BF)
        hot_all[:, here] = hot
        tok = t_dot(hot, touched[...])
        shifted = tok - row_mean(tok)
        rstd = lax.rsqrt(row_mean(shifted * shifted) + EPSILON)
        rstd_in_all[here, :] = rstd
        hat = shifted * rstd
        hat_in_all[here, :] = hat
        normed = hat * gain_in
        norm_t[:, here] = jnp.transpose(normed).astype(BF)
        normed = normed.astype(BF)
        for k in range(4):
            cols = slice(k * D, (k + 1) * D)
            hid = dot(normed, w_in[:, cols])
            sig = sigmoid(hid)
            act = hid * sig
            slope_all[here, cols] = sig + act * (1.0 - sig)
            if k == 0:
                gate_all[here, :] = act
            else:
                vqk_all[k - 1, here, :] = act.astype(BF)
        ri = iota((PAIR, PAIR), 0)
        ci = iota((PAIR, PAIR), 1)
        allowed = ((ri < SLOT) == (ci < SLOT)) & (ci <= ri)
        scale = HDIM ** (-0.5)
        for s in range(2):
            rows = slice(g * GROUP + s * PAIR, g * GROUP + (s + 1) * PAIR)
            for h in range(HEADS):
                cols = slice(h * HDIM, (h + 1) * HDIM)
                n = (g * 2 + s) * HEADS + h
                score = dot_t(vqk_all[1, rows, cols], vqk_all[2, rows, cols]) * scale
                sig = sigmoid(score)
                act = score * sig
                weight = jnp.where(allowed, act, 0.0).astype(BF)
                wts[n, 0] = weight
                wts[n, 1] = jnp.where(allowed, (sig + act * (1.0 - sig)) * scale, 0.0).astype(BF)
                att[s * PAIR : (s + 1) * PAIR, cols] = dot(weight, vqk_all[0, rows, cols])
        attended = att[...]
        shifted = attended - row_mean(attended)
        rstd = lax.rsqrt(row_mean(shifted * shifted) + EPSILON)
        rstd_out_all[here, :] = rstd
        hat = shifted * rstd
        hat_out_all[here, :] = hat
        mixed_t[:, here] = jnp.transpose(hat * gain_out * gate_all[here, :]).astype(BF)

    loads[0].wait()
    loads[1].wait()
    forward(0)

    pl.semaphore_wait(barrier, N_DEV - 1)

    def len_copy(i):
        return remote(lens.at[minus(i)], got_len.at[dp], lsem, (i,), (minus(i), tb))

    for i in range(OWN):
        len_copy(i).start()
    got_len[dp] = lens[dp]
    owner = jnp.broadcast_to(owner_ref[...].astype(F32), (UNIQ, UNIQ))
    owner_col = jnp.transpose(owner)
    before = iota((UNIQ, UNIQ), 0) < iota((UNIQ, UNIQ), 1)
    rank = jnp.sum(jnp.where((owner == owner_col) & before, 1.0, 0.0), axis=0, keepdims=True)
    mine = iota((N_DEV, UNIQ), 0) == owner_ref[...]
    lanes = iota((N_DEV, 128), 1)
    ids_all = jnp.zeros((N_DEV, 128), F32)
    order_f = orow_ref[...].astype(F32)
    for c in range(CAP):
        sel = jnp.where(mine & (rank == float(c)), 1.0, 0.0)
        sel_all[c] = sel.astype(BF)
        ids_all = jnp.where(lanes == c, jnp.sum(sel * order_f, axis=1, keepdims=True), ids_all)
    meta[...] = ids_all.reshape(N_DEV, 1, 128)
    forward(1)
    for i in range(OWN):
        len_copy(i).wait()
    loads[2].wait()
    loads[3].wait()

    start = jnp.zeros((1, D), jnp.int32)
    for p in range(N_DP):
        wide[p] = start
        start = start + got_len[p]
    row_id = iota((SLOT, D), 0)
    col_id = iota((SLOT, D), 1)

    def pick(p):
        hit = (col_id == wide[p] * BLK + row_id) & (row_id < got_len[p] * BLK)
        return hit.astype(F32).astype(BF)

    def data_copy(i):
        return remote(stage.at[i], ret.at[i], dsem, (i,), (minus(i), tb))

    for g in range(N_GROUP):
        hot = jnp.concatenate([pick(minus(4 * g + k)) for k in range(4)], axis=0)
        slabs = dot(hot, grad_bal[...]).astype(BF)
        for k in range(4):
            i = 4 * g + k
            slab = slabs[k * SLOT : (k + 1) * SLOT, :]
            if i == OWN:
                ret[OWN] = slab
            else:
                stage[i] = slab
                data_copy(i).start()

    def meta_out(i, carry):
        other, to = device(i)
        remote(meta.at[other], gotm_ref.at[i], asem, (1,), to).start()
        return carry

    lax.fori_loop(1, N_DEV, meta_out, 0)
    gotm_ref[0] = meta[me]

    forward(2)
    forward(3)

    def back_a(g):
        here = slice(g * GROUP, (g + 1) * GROUP)
        gy = ret[4 * g : 4 * g + 4].reshape(GROUP, D)
        hat = hat_out_all[here, :]
        grad_mixed = dot_t(gy, w_out[...])
        gh_all[here, 0:D] = (grad_mixed * (hat * gain_out) * slope_all[here, 0:D]).astype(BF)
        cot = grad_mixed * gate_all[here, :]
        gains_acc[1:2, :] += jnp.sum(cot * hat, axis=0, keepdims=True)
        dhat = cot * gain_out
        half_all[here, :] = (
            rstd_out_all[here, :] * (dhat - row_mean(dhat) - hat * row_mean(dhat * hat))
        ).astype(BF)

    def back_b(g):
        for s in range(2):
            rows = slice(g * GROUP + s * PAIR, g * GROUP + (s + 1) * PAIR)
            for h in range(HEADS):
                cols = slice(h * HDIM, (h + 1) * HDIM)
                n = (g * 2 + s) * HEADS + h
                half = half_all[rows, cols]
                grad_weight = dot_t(half, vqk_all[0, rows, cols])
                gs = (grad_weight * wts[n, 1].astype(F32)).astype(BF)
                parts = (
                    t_dot(wts[n, 0], half),
                    dot(gs, vqk_all[2, rows, cols]),
                    t_dot(gs, vqk_all[1, rows, cols]),
                )
                for k in range(3):
                    at = slice((k + 1) * D + h * HDIM, (k + 1) * D + (h + 1) * HDIM)
                    gh_all[rows, at] = (parts[k] * slope_all[rows, at]).astype(BF)

    def back_c(g):
        here = slice(g * GROUP, (g + 1) * GROUP)
        gy = ret[4 * g : 4 * g + 4].reshape(GROUP, D).astype(F32)
        hat = hat_in_all[here, :]
        grad_normed = dot_t(gh_all[here, :], w_in[...])
        gains_acc[0:1, :] += jnp.sum(grad_normed * hat, axis=0, keepdims=True)
        dhat = grad_normed * gain_in
        inner = rstd_in_all[here, :] * (dhat - row_mean(dhat) - hat * row_mean(dhat * hat))
        grad_tok = (inner + gy).astype(BF)
        part = dot(hot_all[:, here], grad_tok)
        if g == 0:
            rows_acc[...] = part
        else:
            rows_acc[...] += part

    def put(dst, first, block):
        for j in range(4):
            dst[first + j * D : first + (j + 1) * D, :] = block[:, j * 128 : (j + 1) * 128].astype(BF)

    def all_reduce(s, ch, a, pr, b, fr, c, sr, tr, out):
        third = 16 * ch
        quarter = 4 * ch

        def at(row, size):
            return pl.ds(pl.multiple_of(row, 16), size)

        def pair(q, d):
            v = along(ORDERS[q][0], d)[0]
            src = a.at[at(((1 - core) * 3 + q) * third + v * quarter, quarter)]
            return remote(src, pr.at[q, at(v * quarter, quarter)], psem, (s, 0, q, d), partner)

        def add_pair(q, d):
            v = along(ORDERS[q][0], d)[0]
            own = a[at((core * 3 + q) * third + v * quarter, quarter), :].astype(F32)
            rows = at(v * quarter, quarter)
            b[q, rows, :] = (own + pr[q, rows, :].astype(F32)).astype(BF)

        def first(q, d):
            v, to = along(ORDERS[q][0], d)
            return remote(b.at[q, at(v * quarter, quarter)], fr.at[q, d - 1], rsem, (s, 0, q, d - 1), to)

        def second(q, d):
            v, to = along(ORDERS[q][1], d)
            return remote(c.at[q, at(v * ch, ch)], sr.at[q, d - 1], rsem, (s, 1, q, d - 1), to)

        def third_copy(q, d):
            mine = coords[ORDERS[q][2]]
            to = along(ORDERS[q][2], d)[1]
            return remote(tr.at[q, mine], tr.at[q, mine], rsem, (s, 2, q, d - 1), to)

        def piece(q, da, db):
            va = along(ORDERS[q][0], 4 - da)[0]
            vb = along(ORDERS[q][1], 4 - db)[0]
            return at((core * 3 + q) * third + va * quarter + vb * ch, ch)

        def back_two(q, d):
            ref = out.at[piece(q, 0, 0)]
            return remote(ref, ref, rsem, (s, 3, q, d - 1), along(ORDERS[q][1], d)[1])

        def back_one(q, d, k):
            ref = out.at[piece(q, 0, k)]
            return remote(ref, ref, bsem, (s, q, d - 1, k), along(ORDERS[q][0], d)[1])

        def back_pair(q, d):
            va = along(ORDERS[q][0], 4 - d)[0]
            ref = out.at[at((core * 3 + q) * third + va * quarter, quarter)]
            return remote(ref, ref, psem, (s, 1, q, d), partner)

        for d in (2, 1, 3, 0):
            for q in range(3):
                pair(q, d).start()
        yield
        for d in (2, 1, 3, 0):
            for q in range(3):
                pair(q, d).wait()
                add_pair(q, d)
                if d:
                    first(q, d).start()
        yield
        for q in range(3):
            for d in range(1, 4):
                first(q, d).wait()
            total = b[q, at(coords[ORDERS[q][0]] * quarter, quarter), :].astype(F32)
            for d in range(3):
                total = total + fr[q, d].astype(F32)
            c[q] = total.astype(BF)
            for d in range(1, 4):
                second(q, d).start()
        yield
        for q in range(3):
            for d in range(1, 4):
                second(q, d).wait()
            total = c[q, at(coords[ORDERS[q][1]] * ch, ch), :].astype(F32)
            for d in range(3):
                total = total + sr[q, d].astype(F32)
            tr[q, coords[ORDERS[q][2]]] = total.astype(BF)
            for d in range(1, 4):
                third_copy(q, d).start()
        yield
        for q in range(3):
            for d in range(1, 4):
                third_copy(q, d).wait()
            total = tr[q, 0].astype(F32)
            for d in range(1, 4):
                total = total + tr[q, d].astype(F32)
            out[piece(q, 0, 0), :] = total.astype(BF)
            for d in (2, 1, 3):
                back_two(q, d).start()
            for d in (2, 1, 3):
                back_one(q, d, 0).start()
        yield
        for k in (1, 3, 2):
            for q in range(3):
                back_two(q, k).wait()
                for d in (2, 1, 3):
                    back_one(q, d, k).start()
        for q in range(3):
            back_pair(q, 0).start()
        yield
        for d in (1, 3, 2):
            for q in range(3):
                for k in range(4):
                    back_one(q, d, k).wait()
                back_pair(q, d).start()
        yield
        for d in (0, 1, 3, 2):
            for q in range(3):
                back_pair(q, d).wait()
        yield

    def gain_reduce():
        def pair():
            ref = gbuf.at[0, core]
            return remote(ref, ref, gsem, (0, 0), partner)

        def copy(k, d):
            axis = "xyz"[k - 1]
            ref = gbuf.at[k, coords[axis]]
            return remote(ref, ref, gsem, (k, d - 1), along(axis, d)[1])

        gbuf[0, core] = jnp.concatenate(
            [gains_acc[r : r + 1, j * 128 : (j + 1) * 128] for r in range(2) for j in range(4)],
            axis=0,
        )
        pair().start()
        yield
        pair().wait()
        total = gbuf[0, 0] + gbuf[0, 1]
        for k in range(1, 4):
            gbuf[k, coords["xyz"[k - 1]]] = total
            for d in range(1, 4):
                copy(k, d).start()
            yield
            for d in range(1, 4):
                copy(k, d).wait()
            total = (gbuf[k, 0] + gbuf[k, 1]) + (gbuf[k, 2] + gbuf[k, 3])
        gains_ref[...] = total
        yield

    red1 = all_reduce(0, CH1, a1, pr1, b1, fr1, c1, sr1, tr1, g1_ref)
    red2 = all_reduce(1, CH2, a2, pr2, b2, fr2, c2, sr2, tr2, g2_ref)
    red_g = gain_reduce()

    for g in range(N_GROUP):
        for i in range(4 * g, min(4 * g + 4, OWN)):
            data_copy(i).wait_recv()
        back_a(g)
        if g < N_GROUP - 1:
            back_b(g)
            back_c(g)
    put(a1, 0, dot(mixed_t[...], ret[...].reshape(TOK, D)))
    put(a1, 4 * D, dot(norm_t[...], gh_all[:, 0:D]))
    a1[8 * D : ROWS1, :] = jnp.zeros((ROWS1 - 8 * D, 128), BF)
    next(red1)
    back_b(3)
    next(red1)
    for k in range(3):
        put(a2, k * 4 * D, dot(norm_t[...], gh_all[:, (k + 1) * D : (k + 2) * D]))
    next(red2)
    next(red1)
    back_c(3)
    next(red2)

    row_half = rows_acc[...].astype(BF)
    for c in range(CAP):
        picked = dot(sel_all[c], row_half)
        for k in range(4):
            spread[pl.ds(k * CAP + c, N_DEV, stride=16), :] = picked[:, k * 128 : (k + 1) * 128]
    send[...] = spread[...].astype(BF).reshape(N_DEV, 16, 128)

    next(red_g)

    def scatter_out(i, carry):
        other, to = device(i)
        remote(send.at[other], got_ref.at[i], asem, (0,), to).start()
        return carry

    lax.fori_loop(1, N_DEV, scatter_out, 0)
    got_ref[0] = send[me]

    next(red1)
    next(red_g)
    next(red2)
    next(red1)
    next(red_g)
    next(red2)
    next(red1)
    next(red_g)
    next(red2)
    next(red1)
    next(red_g)
    next(red2)
    next(red2)
    next(red1)
    others = pl.ds(1, N_DEV - 1)
    remote(send.at[others], got_ref.at[others], asem, (0,), partner).wait()
    remote(meta.at[others], gotm_ref.at[others], asem, (1,), partner).wait()
    for i in range(OWN):
        data_copy(i).wait_send()
    next(red2)


def run_step(seq_dest, seq_blocks, items, owner, orow, gain_in, gain_out, touched, grad_out, w_in, w_out):
    smem = pl.BlockSpec(memory_space=pltpu.SMEM)
    vmem = pl.BlockSpec(memory_space=pltpu.VMEM)
    far = pl.BlockSpec(memory_space=pl.ANY)
    v = pltpu.VMEM
    dma = pltpu.SemaphoreType.DMA
    scratch = [
        v((UNIQ, D), BF),
        v((D, D), BF),
        v((D, 4 * D), BF),
        v((D, D), BF),
        dma((4,)),
        v((N_DP, 1, D), jnp.int32),
        v((N_DP, 1, D), jnp.int32),
        v((N_DP, 1, D), jnp.int32),
        v((N_DP, SLOT, D), BF),
        v((N_DP, SLOT, D), BF),
        dma((2, N_DP)),
        dma((2, N_DP)),
        dma((1,)),
        v((UNIQ, TOK), BF),
        v((D, TOK), BF),
        v((D, TOK), BF),
        v((TOK, D), F32),
        v((TOK, 1), F32),
        v((TOK, D), F32),
        v((TOK, 1), F32),
        v((TOK, 4 * D), F32),
        v((TOK, D), F32),
        v((3, TOK, D), BF),
        v((GROUP, D), F32),
        v((N_GROUP * 2 * HEADS, 2, PAIR, PAIR), BF),
        v((TOK, D), BF),
        v((TOK, 4 * D), BF),
        v((UNIQ, D), F32),
        v((8, D), F32),
        v((N_DEV * 16, 128), F32),
        v((N_DEV, 16, 128), BF),
        v((N_DEV, 1, 128), F32),
        v((CAP, N_DEV, UNIQ), BF),
        v((ROWS1, 128), BF),
        v((ROWS2, 128), BF),
    ]
    for shape in ((3, 16), (3, 16), (3, 3, 4), (3, 4), (3, 3, 1), (3, 4, 1)):
        for ch in (CH1, CH2):
            scratch.append(v(shape[:-1] + (shape[-1] * ch, 128), BF))
    scratch += [
        v((4, 4, 8, 128), F32),
        dma((2, 2, 2, 3, 4)),
        dma((2, 2, 4, 3, 3)),
        dma((2, 2, 3, 3, 4)),
        dma((2, 2)),
        dma((2, 4, 3)),
    ]
    return pl.pallas_call(
        step_kernel,
        out_shape=(
            jax.ShapeDtypeStruct((ROWS1, 128), BF),
            jax.ShapeDtypeStruct((ROWS2, 128), BF),
            jax.ShapeDtypeStruct((N_DEV, 16, 128), BF),
            jax.ShapeDtypeStruct((N_DEV, 1, 128), F32),
            jax.ShapeDtypeStruct((8, 128), F32),
        ),
        in_specs=[smem] + [vmem] * 7 + [far] * 4,
        out_specs=(vmem,) * 5,
        scratch_shapes=scratch,
        compiler_params=pltpu.CompilerParams(
            collective_id=0, has_side_effects=True, vmem_limit_bytes=67_000_000
        ),
        name="step",
    )(
        seq_dest,
        seq_dest.reshape(1, -1),
        seq_blocks.reshape(1, -1),
        items.reshape(8, 128),
        owner.reshape(1, -1),
        orow.reshape(1, -1),
        gain_in.reshape(1, -1),
        gain_out.reshape(1, -1),
        touched,
        grad_out,
        w_in,
        w_out,
    )


def finish_kernel(
    out_ref, gate_ref, rest_ref, got_ref, meta_ref, gains_in, table_ref, win_ref, wout_ref, gin_ref, gout_ref, spread, picked, ids, *, factor
):
    i = pl.program_id(0)

    def unpack(src, dst):
        for j in range(4):
            dst[:, j * 128 : (j + 1) * 128] = src[j * D : (j + 1) * D, :].astype(F32) * factor

    @pl.when(i == 0)
    def _():
        spread[...] = got_ref[...].astype(F32)
        for c in range(CAP):
            for k in range(4):
                picked[c * N_DEV : (c + 1) * N_DEV, k * 128 : (k + 1) * 128] = spread[
                    pl.ds(k * CAP + c, N_DEV, stride=16), :
                ].astype(BF)
        ids[...] = jnp.transpose(meta_ref[...].reshape(N_DEV, 128))
        for j in range(4):
            gin_ref[:, j * 128 : (j + 1) * 128] = gains_in[j : j + 1, :] * factor
            gout_ref[:, j * 128 : (j + 1) * 128] = gains_in[4 + j : 5 + j, :] * factor
        unpack(out_ref, wout_ref)
        unpack(gate_ref, win_ref)

    @pl.when(i > 0)
    def _():
        unpack(rest_ref, win_ref)

    rows = (iota((256, N_DEV), 0) + i * 256).astype(F32)
    hot = jnp.concatenate(
        [jnp.where(rows == ids[c : c + 1, :], 1.0, 0.0).astype(BF) for c in range(CAP)], axis=1
    )
    table_ref[...] = dot(hot, picked[...])


def finish(g1, g2, got, meta, gains, factor):
    def fixed(*shape):
        return pl.BlockSpec(shape, lambda i: (0,) * len(shape))

    def body(*refs):
        finish_kernel(*refs, factor=factor)

    return pl.pallas_call(
        body,
        out_shape=(
            jax.ShapeDtypeStruct((ROWS_DEV, D), F32),
            jax.ShapeDtypeStruct((D, 4 * D), F32),
            jax.ShapeDtypeStruct((D, D), F32),
            jax.ShapeDtypeStruct((1, D), F32),
            jax.ShapeDtypeStruct((1, D), F32),
        ),
        grid=(4,),
        in_specs=[
            pl.BlockSpec((4 * D, 128), lambda i: (0, 0)),
            pl.BlockSpec((4 * D, 128), lambda i: (1, 0)),
            pl.BlockSpec((4 * D, 128), lambda i: (jnp.maximum(i - 1, 0), 0)),
            fixed(N_DEV * 16, 128),
            fixed(N_DEV, 1, 128),
            fixed(8, 128),
        ],
        out_specs=(
            pl.BlockSpec((256, D), lambda i: (i, 0)),
            pl.BlockSpec((D, D), lambda i: (0, i)),
            fixed(D, D),
            fixed(1, D),
            fixed(1, D),
        ),
        scratch_shapes=[
            pltpu.VMEM((N_DEV * 16, 128), F32),
            pltpu.VMEM((CAP * N_DEV, D), BF),
            pltpu.VMEM((128, N_DEV), F32),
        ],
        compiler_params=pltpu.CompilerParams(vmem_limit_bytes=67_000_000),
        name="finish",
    )(g1, g1, g2, got.reshape(N_DEV * 16, 128), meta, gains)


def on_device(
    touched_rows,
    row_of_token,
    row_owner,
    owner_row,
    seq_blocks,
    seq_dest,
    grad_out,
    w_in,
    w_out,
    gain_in,
    gain_out,
):
    g1, g2, got, meta, gains = run_step(
        seq_dest,
        seq_blocks,
        row_of_token,
        row_owner,
        owner_row,
        gain_in,
        gain_out,
        touched_rows,
        grad_out,
        w_in,
        w_out,
    )
    factor = 1.0 / math.sqrt(grad_out.shape[0] * N_DEV)
    table, grad_in, grad_w_out, gin, gout = finish(g1, g2, got, meta, gains, factor)
    return (table, grad_in, grad_w_out, gin.reshape(-1), gout.reshape(-1))


def solution(mesh):
    in_specs = (
        P(("dp", "table"), None),
        P(("dp", "table")),
        P(("dp", "table"), None),
        P(("dp", "table")),
        P(("dp", "table")),
        P(("dp", "table")),
        P(("dp", "table"), None),
        P(),
        P(),
        P(),
        P(),
    )
    out_specs = (P(("dp", "table"), None), P(), P(), P(), P())
    return jax.shard_map(
        on_device, mesh=mesh, in_specs=in_specs, out_specs=out_specs, check_vma=False
    )
```

```python
import math

import jax
import jax.numpy as jnp
from jax import lax
from jax.experimental import pallas as pl
from jax.experimental.pallas import tpu as pltpu
from jax.sharding import PartitionSpec as P

HEADS = 4
HDIM = 128
BLK = 16
LMAXB = 4
SLOT = 64
ROWS_DEV = 1024
UNIQ = 256
CAP = 4
D = 512
N_DP = 16
N_TABLE = 8
N_DEV = 128
GROUP = 256
N_GROUP = 4
TOK = 1024
PAIR = 128
CH1 = 48
CH2 = 64
ROWS1 = 96 * CH1
ROWS2 = 96 * CH2
EPSILON = 1e-05
MESH = pl.DeviceIdType.MESH
BF = jnp.bfloat16
F32 = jnp.float32


def dot(a, b):
    return jnp.dot(a, b, preferred_element_type=F32)


def dot_t(a, b):
    return lax.dot_general(a, b, (((1,), (1,)), ((), ())), preferred_element_type=F32)


def t_dot(a, b):
    return lax.dot_general(a, b, (((0,), (0,)), ((), ())), preferred_element_type=F32)


OFFSETS = (
    (0, 1), (1, 0), (3, 0), (0, 3),
    (1, 1), (3, 3), (0, 2), (2, 0),
    (1, 3), (3, 1), (1, 2), (2, 1),
    (3, 2), (2, 3), (2, 2), (0, 0),
)
OWN = 15
ORDERS = (("x", "y", "z"), ("y", "z", "x"), ("z", "x", "y"))


def row_mean(v):
    return jnp.sum(v, axis=-1, keepdims=True) * (1.0 / D)


def sigmoid(v):
    return 0.5 * jnp.tanh(0.5 * v) + 0.5


def iota(shape, dim):
    return lax.broadcasted_iota(jnp.int32, shape, dim)


def step_kernel(
    dest_s,
    dest_l,
    blocks_l,
    items_ref,
    owner_ref,
    orow_ref,
    gin_ref,
    gout_ref,
    touched_hbm,
    grad_hbm,
    w_in_hbm,
    w_out_hbm,
    g1_out,
    g2_out,
    picked_out,
    ids_out,
    gains_out,
    touched,
    grad_bal,
    w_in,
    w_out,
    load_sem,
    lens,
    got_len,
    wide,
    stage,
    ret,
    lsem,
    dsem,
    ready,
    out_sem,
    hot_all,
    norm_t,
    mixed_t,
    hat_in_all,
    rstd_in_all,
    hat_out_all,
    rstd_out_all,
    slope_all,
    gate_all,
    vqk_all,
    att,
    wts,
    half_all,
    gh_all,
    rows_acc,
    gains_acc,
    spread,
    send,
    meta,
    sel_all,
    a1,
    a2,
    pr1,
    pr2,
    b1,
    b2,
    fr1,
    fr2,
    c1,
    c2,
    sr1,
    sr2,
    tr1,
    tr2,
    gbuf,
    psem,
    rsem,
    bsem,
    asem,
    gsem,
    g1_ref,
    g2_ref,
    got_ref,
    gotm_ref,
    picked_ref,
    ids_ref,
    gains_ref,
):
    dp = lax.axis_index("dp")
    tb = lax.axis_index("table")
    x = dp // 4
    z = dp % 4
    y = tb // 2
    core = tb % 2
    me = dp * N_TABLE + tb
    partner = (dp, y * 2 + 1 - core)
    coords = {"x": x, "y": y, "z": z}

    def device(i):
        other = lax.rem(me + i, N_DEV)
        return other, (other // N_TABLE, other % N_TABLE)

    def along(axis, d):
        v = lax.rem(coords[axis] + d, 4)
        to = {"x": (v * 4 + z, tb), "z": (x * 4 + v, tb), "y": (dp, v * 2 + core)}[axis]
        return v, to

    def plus(i):
        dx, dz = OFFSETS[i]
        return lax.rem(x + dx, 4) * 4 + lax.rem(z + dz, 4)

    def minus(i):
        dx, dz = OFFSETS[i]
        return lax.rem(x + 4 - dx, 4) * 4 + lax.rem(z + 4 - dz, 4)

    def remote(src, dst, sems, index, to):
        return pltpu.make_async_remote_copy(
            src_ref=src,
            dst_ref=dst,
            send_sem=sems.at[(0,) + index],
            recv_sem=sems.at[(1,) + index],
            device_id=to,
            device_id_type=MESH,
        )

    loads = [
        pltpu.make_async_copy(touched_hbm, touched, load_sem.at[0]),
        pltpu.make_async_copy(w_in_hbm, w_in, load_sem.at[1]),
        pltpu.make_async_copy(grad_hbm, grad_bal, load_sem.at[2]),
        pltpu.make_async_copy(w_out_hbm, w_out, load_sem.at[3]),
    ]
    for load in loads:
        load.start()

    barrier = pltpu.get_barrier_semaphore()

    def column(i):
        return (dp, lax.rem(tb + i, N_TABLE))

    for i in range(OWN):
        pl.semaphore_signal(barrier, inc=1, device_id=(plus(i), tb), device_id_type=MESH)
    for i in range(1, N_TABLE):
        pl.semaphore_signal(barrier, inc=1, device_id=column(i), device_id_type=MESH)

    hits = dest_l[...] == iota((N_DP, N_DP), 0)
    lengths = jnp.sum(
        jnp.where(hits, blocks_l[...].astype(F32), 0.0), axis=1, keepdims=True
    )
    lengths = jnp.broadcast_to(lengths, (N_DP, D)).astype(jnp.int32)
    for p in range(N_DP):
        lens[p] = lengths[p : p + 1, :]

    gain_in = gin_ref[...]
    gain_out = gout_ref[...]
    gains_acc[...] = jnp.zeros_like(gains_acc)
    lane = iota((1, 128), 1)

    def item_pair(i):
        rows = []
        for k in range(2):
            peer = plus(i + k)
            slot = jnp.int32(0)
            for j in range(N_DP):
                slot = jnp.where(dest_s[j] == peer, j, slot)
            row = items_ref[pl.ds(slot // 2, 1), :]
            turned = pltpu.roll(row, 64, 1)
            rows.append(jnp.where(jnp.broadcast_to(slot % 2, (1, 128)) == k, row, turned))
        return jnp.where(lane < 64, rows[0], rows[1])

    def forward(g):
        here = slice(g * GROUP, (g + 1) * GROUP)
        items = jnp.concatenate([item_pair(4 * g), item_pair(4 * g + 2)], axis=1)
        hot = (iota((UNIQ, GROUP), 0) == items).astype(F32).astype(BF)
        hot_all[:, here] = hot
        tok = t_dot(hot, touched[...])
        shifted = tok - row_mean(tok)
        rstd = lax.rsqrt(row_mean(shifted * shifted) + EPSILON)
        rstd_in_all[here, :] = rstd
        hat = shifted * rstd
        hat_in_all[here, :] = hat
        normed = hat * gain_in
        norm_t[:, here] = jnp.transpose(normed).astype(BF)
        normed = normed.astype(BF)
        for k in range(4):
            cols = slice(k * D, (k + 1) * D)
            hid = dot(normed, w_in[:, cols])
            sig = sigmoid(hid)
            act = hid * sig
            slope_all[here, cols] = sig + act * (1.0 - sig)
            if k == 0:
                gate_all[here, :] = act
            else:
                vqk_all[k - 1, here, :] = act.astype(BF)
        ri = iota((PAIR, PAIR), 0)
        ci = iota((PAIR, PAIR), 1)
        allowed = ((ri < SLOT) == (ci < SLOT)) & (ci <= ri)
        scale = HDIM ** (-0.5)
        for s in range(2):
            rows = slice(g * GROUP + s * PAIR, g * GROUP + (s + 1) * PAIR)
            for h in range(HEADS):
                cols = slice(h * HDIM, (h + 1) * HDIM)
                n = (g * 2 + s) * HEADS + h
                score = dot_t(vqk_all[1, rows, cols], vqk_all[2, rows, cols]) * scale
                sig = sigmoid(score)
                act = score * sig
                weight = jnp.where(allowed, act, 0.0).astype(BF)
                wts[n, 0] = weight
                wts[n, 1] = jnp.where(allowed, (sig + act * (1.0 - sig)) * scale, 0.0).astype(BF)
                att[s * PAIR : (s + 1) * PAIR, cols] = dot(weight, vqk_all[0, rows, cols])
        attended = att[...]
        shifted = attended - row_mean(attended)
        rstd = lax.rsqrt(row_mean(shifted * shifted) + EPSILON)
        rstd_out_all[here, :] = rstd
        hat = shifted * rstd
        hat_out_all[here, :] = hat
        mixed_t[:, here] = jnp.transpose(hat * gain_out * gate_all[here, :]).astype(BF)

    loads[0].wait()
    loads[1].wait()
    forward(0)

    pl.semaphore_wait(barrier, OWN + N_TABLE - 1)

    def len_copy(i):
        return remote(lens.at[minus(i)], got_len.at[dp], lsem, (i,), (minus(i), tb))

    for i in range(OWN):
        len_copy(i).start()
    got_len[dp] = lens[dp]
    for i in range(1, N_TABLE):
        pl.semaphore_signal(ready, inc=1, device_id=column(i), device_id_type=MESH)
    owner = jnp.broadcast_to(owner_ref[...].astype(F32), (UNIQ, UNIQ))
    owner_col = jnp.transpose(owner)
    before = iota((UNIQ, UNIQ), 0) < iota((UNIQ, UNIQ), 1)
    rank = jnp.sum(jnp.where((owner == owner_col) & before, 1.0, 0.0), axis=0, keepdims=True)
    mine = iota((N_DEV, UNIQ), 0) == owner_ref[...]
    lanes = iota((N_DEV, 128), 1)
    ids_all = jnp.zeros((N_DEV, 128), F32)
    order_f = orow_ref[...].astype(F32)
    for c in range(CAP):
        sel = jnp.where(mine & (rank == float(c)), 1.0, 0.0)
        sel_all[c] = sel.astype(BF)
        ids_all = jnp.where(lanes == c, jnp.sum(sel * order_f, axis=1, keepdims=True), ids_all)
    meta[...] = ids_all.reshape(N_DEV, 1, 128)
    forward(1)
    for i in range(OWN):
        len_copy(i).wait()
    loads[2].wait()
    loads[3].wait()

    start = jnp.zeros((1, D), jnp.int32)
    for p in range(N_DP):
        wide[p] = start
        start = start + got_len[p]
    row_id = iota((SLOT, D), 0)
    col_id = iota((SLOT, D), 1)

    def pick(p):
        hit = (col_id == wide[p] * BLK + row_id) & (row_id < got_len[p] * BLK)
        return hit.astype(F32).astype(BF)

    def data_copy(i):
        return remote(stage.at[i], ret.at[i], dsem, (i,), (minus(i), tb))

    for g in range(N_GROUP):
        hot = jnp.concatenate([pick(minus(4 * g + k)) for k in range(4)], axis=0)
        slabs = dot(hot, grad_bal[...]).astype(BF)
        for k in range(4):
            i = 4 * g + k
            slab = slabs[k * SLOT : (k + 1) * SLOT, :]
            if i == OWN:
                ret[OWN] = slab
            else:
                stage[i] = slab
                data_copy(i).start()

    def meta_out(i, carry):
        other, to = device(i)
        remote(meta.at[other], gotm_ref.at[i], asem, (1,), to).start()
        return carry

    pl.semaphore_wait(ready, N_TABLE - 1)
    lax.fori_loop(1, N_DEV, meta_out, 0)
    gotm_ref[0] = meta[me]

    forward(2)
    forward(3)

    def back_a(g):
        here = slice(g * GROUP, (g + 1) * GROUP)
        gy = ret[4 * g : 4 * g + 4].reshape(GROUP, D)
        hat = hat_out_all[here, :]
        grad_mixed = dot_t(gy, w_out[...])
        gh_all[here, 0:D] = (grad_mixed * (hat * gain_out) * slope_all[here, 0:D]).astype(BF)
        cot = grad_mixed * gate_all[here, :]
        gains_acc[1:2, :] += jnp.sum(cot * hat, axis=0, keepdims=True)
        dhat = cot * gain_out
        half_all[here, :] = (
            rstd_out_all[here, :] * (dhat - row_mean(dhat) - hat * row_mean(dhat * hat))
        ).astype(BF)

    def back_b(g):
        for s in range(2):
            rows = slice(g * GROUP + s * PAIR, g * GROUP + (s + 1) * PAIR)
            for h in range(HEADS):
                cols = slice(h * HDIM, (h + 1) * HDIM)
                n = (g * 2 + s) * HEADS + h
                half = half_all[rows, cols]
                grad_weight = dot_t(half, vqk_all[0, rows, cols])
                gs = (grad_weight * wts[n, 1].astype(F32)).astype(BF)
                parts = (
                    t_dot(wts[n, 0], half),
                    dot(gs, vqk_all[2, rows, cols]),
                    t_dot(gs, vqk_all[1, rows, cols]),
                )
                for k in range(3):
                    at = slice((k + 1) * D + h * HDIM, (k + 1) * D + (h + 1) * HDIM)
                    gh_all[rows, at] = (parts[k] * slope_all[rows, at]).astype(BF)

    def back_c(g):
        here = slice(g * GROUP, (g + 1) * GROUP)
        gy = ret[4 * g : 4 * g + 4].reshape(GROUP, D).astype(F32)
        hat = hat_in_all[here, :]
        grad_normed = dot_t(gh_all[here, :], w_in[...])
        gains_acc[0:1, :] += jnp.sum(grad_normed * hat, axis=0, keepdims=True)
        dhat = grad_normed * gain_in
        inner = rstd_in_all[here, :] * (dhat - row_mean(dhat) - hat * row_mean(dhat * hat))
        grad_tok = (inner + gy).astype(BF)
        part = dot(hot_all[:, here], grad_tok)
        if g == 0:
            rows_acc[...] = part
        else:
            rows_acc[...] += part

    def put(dst, first, block):
        for j in range(4):
            dst[first + j * D : first + (j + 1) * D, :] = block[:, j * 128 : (j + 1) * 128].astype(BF)

    def all_reduce(s, ch, a, pr, b, fr, c, sr, tr, out):
        third = 16 * ch
        quarter = 4 * ch

        def at(row, size):
            return pl.ds(pl.multiple_of(row, 16), size)

        def pair(q, d):
            v = along(ORDERS[q][0], d)[0]
            src = a.at[at(((1 - core) * 3 + q) * third + v * quarter, quarter)]
            return remote(src, pr.at[q, at(v * quarter, quarter)], psem, (s, 0, q, d), partner)

        def add_pair(q, d):
            v = along(ORDERS[q][0], d)[0]
            own = a[at((core * 3 + q) * third + v * quarter, quarter), :].astype(F32)
            rows = at(v * quarter, quarter)
            b[q, rows, :] = (own + pr[q, rows, :].astype(F32)).astype(BF)

        def first(q, d):
            v, to = along(ORDERS[q][0], d)
            return remote(b.at[q, at(v * quarter, quarter)], fr.at[q, d - 1], rsem, (s, 0, q, d - 1), to)

        def second(q, d):
            v, to = along(ORDERS[q][1], d)
            return remote(c.at[q, at(v * ch, ch)], sr.at[q, d - 1], rsem, (s, 1, q, d - 1), to)

        def third_copy(q, d):
            mine = coords[ORDERS[q][2]]
            to = along(ORDERS[q][2], d)[1]
            return remote(tr.at[q, mine], tr.at[q, mine], rsem, (s, 2, q, d - 1), to)

        def piece(q, da, db):
            va = along(ORDERS[q][0], 4 - da)[0]
            vb = along(ORDERS[q][1], 4 - db)[0]
            return at((core * 3 + q) * third + va * quarter + vb * ch, ch)

        def back_two(q, d):
            ref = out.at[piece(q, 0, 0)]
            return remote(ref, ref, rsem, (s, 3, q, d - 1), along(ORDERS[q][1], d)[1])

        def back_one(q, d, k):
            ref = out.at[piece(q, 0, k)]
            return remote(ref, ref, bsem, (s, q, d - 1, k), along(ORDERS[q][0], d)[1])

        def back_pair(q, d):
            va = along(ORDERS[q][0], 4 - d)[0]
            ref = out.at[at((core * 3 + q) * third + va * quarter, quarter)]
            return remote(ref, ref, psem, (s, 1, q, d), partner)

        for d in (2, 1, 3, 0):
            for q in range(3):
                pair(q, d).start()
        yield
        for d in (2, 1, 3, 0):
            for q in range(3):
                pair(q, d).wait()
                add_pair(q, d)
                if d:
                    first(q, d).start()
        yield
        for q in range(3):
            for d in range(1, 4):
                first(q, d).wait()
            total = b[q, at(coords[ORDERS[q][0]] * quarter, quarter), :].astype(F32)
            for d in range(3):
                total = total + fr[q, d].astype(F32)
            c[q] = total.astype(BF)
            for d in range(1, 4):
                second(q, d).start()
        yield
        for q in range(3):
            for d in range(1, 4):
                second(q, d).wait()
            total = c[q, at(coords[ORDERS[q][1]] * ch, ch), :].astype(F32)
            for d in range(3):
                total = total + sr[q, d].astype(F32)
            tr[q, coords[ORDERS[q][2]]] = total.astype(BF)
            for d in range(1, 4):
                third_copy(q, d).start()
        yield
        for q in range(3):
            for d in range(1, 4):
                third_copy(q, d).wait()
            total = tr[q, 0].astype(F32)
            for d in range(1, 4):
                total = total + tr[q, d].astype(F32)
            out[piece(q, 0, 0), :] = total.astype(BF)
            for d in (2, 1, 3):
                back_two(q, d).start()
            for d in (2, 1, 3):
                back_one(q, d, 0).start()
        yield
        for k in (1, 3, 2):
            for q in range(3):
                back_two(q, k).wait()
                for d in (2, 1, 3):
                    back_one(q, d, k).start()
        for q in range(3):
            back_pair(q, 0).start()
        yield
        for d in (1, 3, 2):
            for q in range(3):
                for k in range(4):
                    back_one(q, d, k).wait()
                back_pair(q, d).start()
        yield
        for d in (0, 1, 3, 2):
            for q in range(3):
                back_pair(q, d).wait()
        yield

    def gain_reduce():
        def pair():
            ref = gbuf.at[0, core]
            return remote(ref, ref, gsem, (0, 0), partner)

        def copy(k, d):
            axis = "xyz"[k - 1]
            ref = gbuf.at[k, coords[axis]]
            return remote(ref, ref, gsem, (k, d - 1), along(axis, d)[1])

        gbuf[0, core] = jnp.concatenate(
            [gains_acc[r : r + 1, j * 128 : (j + 1) * 128] for r in range(2) for j in range(4)],
            axis=0,
        )
        pair().start()
        yield
        pair().wait()
        total = gbuf[0, 0] + gbuf[0, 1]
        for k in range(1, 4):
            gbuf[k, coords["xyz"[k - 1]]] = total
            for d in range(1, 4):
                copy(k, d).start()
            yield
            for d in range(1, 4):
                copy(k, d).wait()
            total = (gbuf[k, 0] + gbuf[k, 1]) + (gbuf[k, 2] + gbuf[k, 3])
        gains_ref[...] = total
        yield

    red1 = all_reduce(0, CH1, a1, pr1, b1, fr1, c1, sr1, tr1, g1_ref)
    red2 = all_reduce(1, CH2, a2, pr2, b2, fr2, c2, sr2, tr2, g2_ref)
    red_g = gain_reduce()

    for g in range(N_GROUP):
        for i in range(4 * g, min(4 * g + 4, OWN)):
            data_copy(i).wait_recv()
        back_a(g)
        if g < N_GROUP - 1:
            back_b(g)
    put(a1, 0, dot(mixed_t[...], ret[...].reshape(TOK, D)))
    put(a1, 4 * D, dot(norm_t[...], gh_all[:, 0:D]))
    a1[8 * D : ROWS1, :] = jnp.zeros((ROWS1 - 8 * D, 128), BF)
    next(red1)
    back_b(3)
    next(red1)
    for k in range(3):
        put(a2, k * 4 * D, dot(norm_t[...], gh_all[:, (k + 1) * D : (k + 2) * D]))
    next(red2)
    next(red1)
    back_c(0)
    next(red2)
    back_c(1)
    next(red1)
    back_c(2)
    back_c(3)
    next(red_g)

    row_half = rows_acc[...].astype(BF)
    for c in range(CAP):
        picked = dot(sel_all[c], row_half)
        for k in range(4):
            spread[pl.ds(k * CAP + c, N_DEV, stride=16), :] = picked[:, k * 128 : (k + 1) * 128]
    send[...] = spread[...].astype(BF).reshape(N_DEV, 16, 128)
    got_ref[0] = send[me]

    def scatter_out(i, carry):
        other, to = device(i)
        remote(send.at[other], got_ref.at[i], asem, (0,), to).start()
        return carry

    next(red2)
    lax.fori_loop(1, 49, scatter_out, 0)
    next(red1)
    next(red_g)
    lax.fori_loop(49, 81, scatter_out, 0)
    next(red2)
    next(red1)
    next(red_g)
    lax.fori_loop(81, N_DEV, scatter_out, 0)
    next(red2)
    next(red1)
    next(red_g)
    next(red2)
    next(red_g)
    next(red1)

    def out_copy(src, dst, n):
        return pltpu.make_async_copy(src, dst, out_sem.at[n])

    outs = [out_copy(g1_ref, g1_out, 0), out_copy(gains_ref, gains_out, 1)]
    for o in outs:
        o.start()
    others = pl.ds(1, N_DEV - 1)
    remote(send.at[others], got_ref.at[others], asem, (0,), partner).wait()
    remote(meta.at[others], gotm_ref.at[others], asem, (1,), partner).wait()
    next(red2)
    half = pl.ds(pl.multiple_of(core * (ROWS2 // 2), 16), ROWS2 // 2)
    rest = pl.ds(pl.multiple_of((1 - core) * (ROWS2 // 2), 16), ROWS2 // 2)
    outs.append(out_copy(g2_ref.at[half], g2_out.at[half], 2))
    outs[-1].start()
    spread[...] = got_ref[...].reshape(N_DEV * 16, 128).astype(F32)
    for c in range(CAP):
        for k in range(4):
            picked_ref[c * N_DEV : (c + 1) * N_DEV, k * 128 : (k + 1) * 128] = spread[
                pl.ds(k * CAP + c, N_DEV, stride=16), :
            ].astype(BF)
    ids_ref[...] = jnp.transpose(gotm_ref[...].reshape(N_DEV, 128))
    outs.append(out_copy(picked_ref, picked_out, 3))
    outs[-1].start()
    outs.append(out_copy(ids_ref, ids_out, 4))
    outs[-1].start()
    for i in range(OWN):
        data_copy(i).wait_send()
    next(red2)
    outs.append(out_copy(g2_ref.at[rest], g2_out.at[rest], 5))
    outs[-1].start()
    for o in outs:
        o.wait()


def run_step(seq_dest, seq_blocks, items, owner, orow, gain_in, gain_out, touched, grad_out, w_in, w_out):
    smem = pl.BlockSpec(memory_space=pltpu.SMEM)
    vmem = pl.BlockSpec(memory_space=pltpu.VMEM)
    far = pl.BlockSpec(memory_space=pl.ANY)
    v = pltpu.VMEM
    dma = pltpu.SemaphoreType.DMA
    scratch = [
        v((UNIQ, D), BF),
        v((D, D), BF),
        v((D, 4 * D), BF),
        v((D, D), BF),
        dma((4,)),
        v((N_DP, 1, D), jnp.int32),
        v((N_DP, 1, D), jnp.int32),
        v((N_DP, 1, D), jnp.int32),
        v((N_DP, SLOT, D), BF),
        v((N_DP, SLOT, D), BF),
        dma((2, N_DP)),
        dma((2, N_DP)),
        pltpu.SemaphoreType.REGULAR,
        dma((6,)),
        v((UNIQ, TOK), BF),
        v((D, TOK), BF),
        v((D, TOK), BF),
        v((TOK, D), F32),
        v((TOK, 1), F32),
        v((TOK, D), F32),
        v((TOK, 1), F32),
        v((TOK, 4 * D), F32),
        v((TOK, D), F32),
        v((3, TOK, D), BF),
        v((GROUP, D), F32),
        v((N_GROUP * 2 * HEADS, 2, PAIR, PAIR), BF),
        v((TOK, D), BF),
        v((TOK, 4 * D), BF),
        v((UNIQ, D), F32),
        v((8, D), F32),
        v((N_DEV * 16, 128), F32),
        v((N_DEV, 16, 128), BF),
        v((N_DEV, 1, 128), F32),
        v((CAP, N_DEV, UNIQ), BF),
        v((ROWS1, 128), BF),
        v((ROWS2, 128), BF),
    ]
    for shape in ((3, 16), (3, 16), (3, 3, 4), (3, 4), (3, 3, 1), (3, 4, 1)):
        for ch in (CH1, CH2):
            scratch.append(v(shape[:-1] + (shape[-1] * ch, 128), BF))
    scratch += [
        v((4, 4, 8, 128), F32),
        dma((2, 2, 2, 3, 4)),
        dma((2, 2, 4, 3, 3)),
        dma((2, 2, 3, 3, 4)),
        dma((2, 2)),
        dma((2, 4, 3)),
        v((ROWS1, 128), BF),
        v((ROWS2, 128), BF),
        v((N_DEV, 16, 128), BF),
        v((N_DEV, 1, 128), F32),
        v((CAP * N_DEV, D), BF),
        v((128, N_DEV), F32),
        v((8, 128), F32),
    ]
    return pl.pallas_call(
        step_kernel,
        out_shape=(
            jax.ShapeDtypeStruct((ROWS1, 128), BF),
            jax.ShapeDtypeStruct((ROWS2, 128), BF),
            jax.ShapeDtypeStruct((CAP * N_DEV, D), BF),
            jax.ShapeDtypeStruct((128, N_DEV), F32),
            jax.ShapeDtypeStruct((8, 128), F32),
        ),
        in_specs=[smem] + [vmem] * 7 + [far] * 4,
        out_specs=(far,) * 5,
        scratch_shapes=scratch,
        compiler_params=pltpu.CompilerParams(
            collective_id=0, has_side_effects=True, vmem_limit_bytes=67_000_000
        ),
        name="step",
    )(
        seq_dest,
        seq_dest.reshape(1, -1),
        seq_blocks.reshape(1, -1),
        items.reshape(8, 128),
        owner.reshape(1, -1),
        orow.reshape(1, -1),
        gain_in.reshape(1, -1),
        gain_out.reshape(1, -1),
        touched,
        grad_out,
        w_in,
        w_out,
    )


def finish_kernel(
    out_ref, gate_ref, rest_ref, picked_ref, ids_ref, gains_in, table_ref, win_ref, wout_ref, gin_ref, gout_ref, *, factor
):
    i = pl.program_id(0)

    def unpack(src, dst):
        for j in range(4):
            dst[:, j * 128 : (j + 1) * 128] = src[j * D : (j + 1) * D, :].astype(F32) * factor

    @pl.when(i == 0)
    def _():
        for j in range(4):
            gin_ref[:, j * 128 : (j + 1) * 128] = gains_in[j : j + 1, :] * factor
            gout_ref[:, j * 128 : (j + 1) * 128] = gains_in[4 + j : 5 + j, :] * factor
        unpack(out_ref, wout_ref)

    @pl.when(i == 1)
    def _():
        unpack(gate_ref, win_ref)

    @pl.when(i > 1)
    def _():
        unpack(rest_ref, win_ref)

    @pl.when(i > 0)
    def _():
        rows = (iota((256, N_DEV), 0) + (i - 1) * 256).astype(F32)
        hot = jnp.concatenate(
            [jnp.where(rows == ids_ref[c : c + 1, :], 1.0, 0.0).astype(BF) for c in range(CAP)],
            axis=1,
        )
        table_ref[...] = dot(hot, picked_ref[...])


def finish(g1, g2, picked, ids, gains, factor):
    def fixed(*shape):
        return pl.BlockSpec(shape, lambda i: (0,) * len(shape))

    def body(*refs):
        finish_kernel(*refs, factor=factor)

    return pl.pallas_call(
        body,
        out_shape=(
            jax.ShapeDtypeStruct((ROWS_DEV, D), F32),
            jax.ShapeDtypeStruct((D, 4 * D), F32),
            jax.ShapeDtypeStruct((D, D), F32),
            jax.ShapeDtypeStruct((1, D), F32),
            jax.ShapeDtypeStruct((1, D), F32),
        ),
        grid=(5,),
        in_specs=[
            pl.BlockSpec((4 * D, 128), lambda i: (0, 0)),
            pl.BlockSpec((4 * D, 128), lambda i: (1, 0)),
            pl.BlockSpec((4 * D, 128), lambda i: (jnp.maximum(i - 2, 0), 0)),
            fixed(CAP * N_DEV, D),
            pl.BlockSpec((8, N_DEV), lambda i: (0, 0)),
            fixed(8, 128),
        ],
        out_specs=(
            pl.BlockSpec((256, D), lambda i: (jnp.maximum(i - 1, 0), 0)),
            pl.BlockSpec((D, D), lambda i: (0, jnp.maximum(i - 1, 0))),
            fixed(D, D),
            fixed(1, D),
            fixed(1, D),
        ),
        compiler_params=pltpu.CompilerParams(vmem_limit_bytes=67_000_000),
        name="finish",
    )(g1, g1, g2, picked, ids, gains)


def on_device(
    touched_rows,
    row_of_token,
    row_owner,
    owner_row,
    seq_blocks,
    seq_dest,
    grad_out,
    w_in,
    w_out,
    gain_in,
    gain_out,
):
    g1, g2, picked, ids, gains = run_step(
        seq_dest,
        seq_blocks,
        row_of_token,
        row_owner,
        owner_row,
        gain_in,
        gain_out,
        touched_rows,
        grad_out,
        w_in,
        w_out,
    )
    factor = 1.0 / math.sqrt(grad_out.shape[0] * N_DEV)
    table, grad_in, grad_w_out, gin, gout = finish(g1, g2, picked, ids, gains, factor)
    return (table, grad_in, grad_w_out, gin.reshape(-1), gout.reshape(-1))


def solution(mesh):
    in_specs = (
        P(("dp", "table"), None),
        P(("dp", "table")),
        P(("dp", "table"), None),
        P(("dp", "table")),
        P(("dp", "table")),
        P(("dp", "table")),
        P(("dp", "table"), None),
        P(),
        P(),
        P(),
        P(),
    )
    out_specs = (P(("dp", "table"), None), P(), P(), P(), P())
    return jax.shard_map(
        on_device, mesh=mesh, in_specs=in_specs, out_specs=out_specs, check_vma=False
    )
```

```python
import math

import jax
import jax.numpy as jnp
from jax import lax
from jax.experimental import pallas as pl
from jax.experimental.pallas import tpu as pltpu
from jax.sharding import PartitionSpec as P

HEADS = 4
HDIM = 128
BLK = 16
LMAXB = 4
SLOT = 64
ROWS_DEV = 1024
UNIQ = 256
CAP = 4
D = 512
N_DP = 16
N_TABLE = 8
N_DEV = 128
GROUP = 256
N_GROUP = 4
TOK = 1024
PAIR = 128
CH1 = 48
CH2 = 64
ROWS1 = 96 * CH1
ROWS2 = 96 * CH2
EPSILON = 1e-05
MESH = pl.DeviceIdType.MESH
BF = jnp.bfloat16
F32 = jnp.float32


def dot(a, b):
    return jnp.dot(a, b, preferred_element_type=F32)


def dot_t(a, b):
    return lax.dot_general(a, b, (((1,), (1,)), ((), ())), preferred_element_type=F32)


def t_dot(a, b):
    return lax.dot_general(a, b, (((0,), (0,)), ((), ())), preferred_element_type=F32)


OFFSETS = (
    (0, 1), (1, 0), (3, 0), (0, 3),
    (1, 1), (3, 3), (0, 2), (2, 0),
    (1, 3), (3, 1), (1, 2), (2, 1),
    (3, 2), (2, 3), (2, 2), (0, 0),
)
OWN = 15
ORDERS = (("x", "y", "z"), ("y", "z", "x"), ("z", "x", "y"))


def row_mean(v):
    return jnp.sum(v, axis=-1, keepdims=True) * (1.0 / D)


def sigmoid(v):
    return 0.5 * jnp.tanh(0.5 * v) + 0.5


def iota(shape, dim):
    return lax.broadcasted_iota(jnp.int32, shape, dim)


def step_kernel(
    dest_s,
    dest_l,
    blocks_l,
    items_ref,
    owner_ref,
    orow_ref,
    gin_ref,
    gout_ref,
    touched_hbm,
    grad_hbm,
    w_in_hbm,
    w_out_hbm,
    g1_out,
    g2_out,
    picked_out,
    ids_out,
    gains_out,
    touched,
    grad_bal,
    w_in,
    w_out,
    load_sem,
    lens,
    got_len,
    wide,
    stage,
    ret,
    lsem,
    dsem,
    ready,
    out_sem,
    hot_all,
    norm_t,
    mixed_t,
    hat_in_all,
    rstd_in_all,
    hat_out_all,
    rstd_out_all,
    slope_all,
    gate_all,
    vqk_all,
    att,
    wts,
    half_all,
    gh_all,
    rows_acc,
    gains_acc,
    spread,
    send,
    meta,
    sel_all,
    a1,
    a2,
    pr1,
    pr2,
    b1,
    b2,
    fr1,
    fr2,
    c1,
    c2,
    sr1,
    sr2,
    tr1,
    tr2,
    gbuf,
    psem,
    rsem,
    bsem,
    asem,
    gsem,
    g1_ref,
    g2_ref,
    got_ref,
    gotm_ref,
    picked_ref,
    ids_ref,
    gains_ref,
):
    dp = lax.axis_index("dp")
    tb = lax.axis_index("table")
    x = dp // 4
    z = dp % 4
    y = tb // 2
    core = tb % 2
    me = dp * N_TABLE + tb
    partner = (dp, y * 2 + 1 - core)
    coords = {"x": x, "y": y, "z": z}

    def device(i):
        other = lax.rem(me + i, N_DEV)
        return other, (other // N_TABLE, other % N_TABLE)

    def along(axis, d):
        v = lax.rem(coords[axis] + d, 4)
        to = {"x": (v * 4 + z, tb), "z": (x * 4 + v, tb), "y": (dp, v * 2 + core)}[axis]
        return v, to

    def plus(i):
        dx, dz = OFFSETS[i]
        return lax.rem(x + dx, 4) * 4 + lax.rem(z + dz, 4)

    def minus(i):
        dx, dz = OFFSETS[i]
        return lax.rem(x + 4 - dx, 4) * 4 + lax.rem(z + 4 - dz, 4)

    def remote(src, dst, sems, index, to):
        return pltpu.make_async_remote_copy(
            src_ref=src,
            dst_ref=dst,
            send_sem=sems.at[(0,) + index],
            recv_sem=sems.at[(1,) + index],
            device_id=to,
            device_id_type=MESH,
        )

    loads = [
        pltpu.make_async_copy(touched_hbm, touched, load_sem.at[0]),
        pltpu.make_async_copy(w_in_hbm, w_in, load_sem.at[1]),
        pltpu.make_async_copy(grad_hbm, grad_bal, load_sem.at[2]),
        pltpu.make_async_copy(w_out_hbm, w_out, load_sem.at[3]),
    ]
    for load in loads:
        load.start()

    barrier = pltpu.get_barrier_semaphore()

    def column(i):
        return (dp, lax.rem(tb + i, N_TABLE))

    for i in range(OWN):
        pl.semaphore_signal(barrier, inc=1, device_id=(plus(i), tb), device_id_type=MESH)
    for i in range(1, N_TABLE):
        pl.semaphore_signal(barrier, inc=1, device_id=column(i), device_id_type=MESH)

    hits = dest_l[...] == iota((N_DP, N_DP), 0)
    lengths = jnp.sum(
        jnp.where(hits, blocks_l[...].astype(F32), 0.0), axis=1, keepdims=True
    )
    lengths = jnp.broadcast_to(lengths, (N_DP, D)).astype(jnp.int32)
    for p in range(N_DP):
        lens[p] = lengths[p : p + 1, :]

    gain_in = gin_ref[...]
    gain_out = gout_ref[...]
    gains_acc[...] = jnp.zeros_like(gains_acc)
    lane = iota((1, 128), 1)

    def item_pair(i):
        rows = []
        for k in range(2):
            peer = plus(i + k)
            slot = jnp.int32(0)
            for j in range(N_DP):
                slot = jnp.where(dest_s[j] == peer, j, slot)
            row = items_ref[pl.ds(slot // 2, 1), :]
            turned = pltpu.roll(row, 64, 1)
            rows.append(jnp.where(jnp.broadcast_to(slot % 2, (1, 128)) == k, row, turned))
        return jnp.where(lane < 64, rows[0], rows[1])

    def forward(g):
        here = slice(g * GROUP, (g + 1) * GROUP)
        items = jnp.concatenate([item_pair(4 * g), item_pair(4 * g + 2)], axis=1)
        hot = (iota((UNIQ, GROUP), 0) == items).astype(F32).astype(BF)
        hot_all[:, here] = hot
        tok = t_dot(hot, touched[...])
        shifted = tok - row_mean(tok)
        rstd = lax.rsqrt(row_mean(shifted * shifted) + EPSILON)
        rstd_in_all[here, :] = rstd
        hat = shifted * rstd
        hat_in_all[here, :] = hat
        normed = hat * gain_in
        norm_t[:, here] = jnp.transpose(normed).astype(BF)
        normed = normed.astype(BF)
        for k in range(4):
            cols = slice(k * D, (k + 1) * D)
            hid = dot(normed, w_in[:, cols])
            sig = sigmoid(hid)
            act = hid * sig
            slope_all[here, cols] = sig + act * (1.0 - sig)
            if k == 0:
                gate_all[here, :] = act
            else:
                vqk_all[k - 1, here, :] = act.astype(BF)
        ri = iota((PAIR, PAIR), 0)
        ci = iota((PAIR, PAIR), 1)
        allowed = ((ri < SLOT) == (ci < SLOT)) & (ci <= ri)
        scale = HDIM ** (-0.5)
        for s in range(2):
            rows = slice(g * GROUP + s * PAIR, g * GROUP + (s + 1) * PAIR)
            for h in range(HEADS):
                cols = slice(h * HDIM, (h + 1) * HDIM)
                n = (g * 2 + s) * HEADS + h
                score = dot_t(vqk_all[1, rows, cols], vqk_all[2, rows, cols]) * scale
                sig = sigmoid(score)
                act = score * sig
                weight = jnp.where(allowed, act, 0.0).astype(BF)
                wts[n, 0] = weight
                wts[n, 1] = jnp.where(allowed, (sig + act * (1.0 - sig)) * scale, 0.0).astype(BF)
                att[s * PAIR : (s + 1) * PAIR, cols] = dot(weight, vqk_all[0, rows, cols])
        attended = att[...]
        shifted = attended - row_mean(attended)
        rstd = lax.rsqrt(row_mean(shifted * shifted) + EPSILON)
        rstd_out_all[here, :] = rstd
        hat = shifted * rstd
        hat_out_all[here, :] = hat
        mixed_t[:, here] = jnp.transpose(hat * gain_out * gate_all[here, :]).astype(BF)

    pl.semaphore_wait(barrier, OWN + N_TABLE - 1)

    def len_copy(i):
        return remote(lens.at[minus(i)], got_len.at[dp], lsem, (i,), (minus(i), tb))

    for i in range(OWN):
        len_copy(i).start()
    got_len[dp] = lens[dp]
    for i in range(1, N_TABLE):
        pl.semaphore_signal(ready, inc=1, device_id=column(i), device_id_type=MESH)
    loads[0].wait()
    loads[1].wait()
    forward(0)
    for i in range(OWN):
        len_copy(i).wait()
    loads[2].wait()
    loads[3].wait()

    start = jnp.zeros((1, D), jnp.int32)
    for p in range(N_DP):
        wide[p] = start
        start = start + got_len[p]
    row_id = iota((SLOT, D), 0)
    col_id = iota((SLOT, D), 1)

    def pick(p):
        hit = (col_id == wide[p] * BLK + row_id) & (row_id < got_len[p] * BLK)
        return hit.astype(F32).astype(BF)

    def data_copy(i):
        return remote(stage.at[i], ret.at[i], dsem, (i,), (minus(i), tb))

    for g in range(N_GROUP):
        hot = jnp.concatenate([pick(minus(4 * g + k)) for k in range(4)], axis=0)
        slabs = dot(hot, grad_bal[...]).astype(BF)
        for k in range(4):
            i = 4 * g + k
            slab = slabs[k * SLOT : (k + 1) * SLOT, :]
            if i == OWN:
                ret[OWN] = slab
            else:
                stage[i] = slab
                data_copy(i).start()

    forward(1)

    owner = jnp.broadcast_to(owner_ref[...].astype(F32), (UNIQ, UNIQ))
    owner_col = jnp.transpose(owner)
    before = iota((UNIQ, UNIQ), 0) < iota((UNIQ, UNIQ), 1)
    rank = jnp.sum(jnp.where((owner == owner_col) & before, 1.0, 0.0), axis=0, keepdims=True)
    mine = iota((N_DEV, UNIQ), 0) == owner_ref[...]
    lanes = iota((N_DEV, 128), 1)
    ids_all = jnp.zeros((N_DEV, 128), F32)
    order_f = orow_ref[...].astype(F32)
    for c in range(CAP):
        sel = jnp.where(mine & (rank == float(c)), 1.0, 0.0)
        sel_all[c] = sel.astype(BF)
        ids_all = jnp.where(lanes == c, jnp.sum(sel * order_f, axis=1, keepdims=True), ids_all)
    meta[...] = ids_all.reshape(N_DEV, 1, 128)

    def meta_out(i, carry):
        other, to = device(i)
        remote(meta.at[other], gotm_ref.at[i], asem, (1,), to).start()
        return carry

    pl.semaphore_wait(ready, N_TABLE - 1)
    lax.fori_loop(1, N_DEV, meta_out, 0)
    gotm_ref[0] = meta[me]

    forward(2)
    forward(3)

    def back_a(g):
        here = slice(g * GROUP, (g + 1) * GROUP)
        gy = ret[4 * g : 4 * g + 4].reshape(GROUP, D)
        hat = hat_out_all[here, :]
        grad_mixed = dot_t(gy, w_out[...])
        gh_all[here, 0:D] = (grad_mixed * (hat * gain_out) * slope_all[here, 0:D]).astype(BF)
        cot = grad_mixed * gate_all[here, :]
        gains_acc[1:2, :] += jnp.sum(cot * hat, axis=0, keepdims=True)
        dhat = cot * gain_out
        half_all[here, :] = (
            rstd_out_all[here, :] * (dhat - row_mean(dhat) - hat * row_mean(dhat * hat))
        ).astype(BF)

    def back_b(g):
        for s in range(2):
            rows = slice(g * GROUP + s * PAIR, g * GROUP + (s + 1) * PAIR)
            for h in range(HEADS):
                cols = slice(h * HDIM, (h + 1) * HDIM)
                n = (g * 2 + s) * HEADS + h
                half = half_all[rows, cols]
                grad_weight = dot_t(half, vqk_all[0, rows, cols])
                gs = (grad_weight * wts[n, 1].astype(F32)).astype(BF)
                parts = (
                    t_dot(wts[n, 0], half),
                    dot(gs, vqk_all[2, rows, cols]),
                    t_dot(gs, vqk_all[1, rows, cols]),
                )
                for k in range(3):
                    at = slice((k + 1) * D + h * HDIM, (k + 1) * D + (h + 1) * HDIM)
                    gh_all[rows, at] = (parts[k] * slope_all[rows, at]).astype(BF)

    def back_c(g):
        here = slice(g * GROUP, (g + 1) * GROUP)
        gy = ret[4 * g : 4 * g + 4].reshape(GROUP, D).astype(F32)
        hat = hat_in_all[here, :]
        grad_normed = dot_t(gh_all[here, :], w_in[...])
        gains_acc[0:1, :] += jnp.sum(grad_normed * hat, axis=0, keepdims=True)
        dhat = grad_normed * gain_in
        inner = rstd_in_all[here, :] * (dhat - row_mean(dhat) - hat * row_mean(dhat * hat))
        grad_tok = (inner + gy).astype(BF)
        part = dot(hot_all[:, here], grad_tok)
        if g == 0:
            rows_acc[...] = part
        else:
            rows_acc[...] += part

    def put(dst, first, block):
        for j in range(4):
            dst[first + j * D : first + (j + 1) * D, :] = block[:, j * 128 : (j + 1) * 128].astype(BF)

    def all_reduce(s, ch, a, pr, b, fr, c, sr, tr, out):
        third = 16 * ch
        quarter = 4 * ch

        def at(row, size):
            return pl.ds(pl.multiple_of(row, 16), size)

        def pair(q, d):
            v = along(ORDERS[q][0], d)[0]
            src = a.at[at(((1 - core) * 3 + q) * third + v * quarter, quarter)]
            return remote(src, pr.at[q, at(v * quarter, quarter)], psem, (s, 0, q, d), partner)

        def add_pair(q, d):
            v = along(ORDERS[q][0], d)[0]
            own = a[at((core * 3 + q) * third + v * quarter, quarter), :].astype(F32)
            rows = at(v * quarter, quarter)
            b[q, rows, :] = (own + pr[q, rows, :].astype(F32)).astype(BF)

        def first(q, d):
            v, to = along(ORDERS[q][0], d)
            return remote(b.at[q, at(v * quarter, quarter)], fr.at[q, d - 1], rsem, (s, 0, q, d - 1), to)

        def second(q, d):
            v, to = along(ORDERS[q][1], d)
            return remote(c.at[q, at(v * ch, ch)], sr.at[q, d - 1], rsem, (s, 1, q, d - 1), to)

        def third_copy(q, d):
            mine = coords[ORDERS[q][2]]
            to = along(ORDERS[q][2], d)[1]
            return remote(tr.at[q, mine], tr.at[q, mine], rsem, (s, 2, q, d - 1), to)

        def piece(q, da, db):
            va = along(ORDERS[q][0], 4 - da)[0]
            vb = along(ORDERS[q][1], 4 - db)[0]
            return at((core * 3 + q) * third + va * quarter + vb * ch, ch)

        def back_two(q, d):
            ref = out.at[piece(q, 0, 0)]
            return remote(ref, ref, rsem, (s, 3, q, d - 1), along(ORDERS[q][1], d)[1])

        def back_one(q, d, k):
            ref = out.at[piece(q, 0, k)]
            return remote(ref, ref, bsem, (s, q, d - 1, k), along(ORDERS[q][0], d)[1])

        def back_pair(q, d):
            va = along(ORDERS[q][0], 4 - d)[0]
            ref = out.at[at((core * 3 + q) * third + va * quarter, quarter)]
            return remote(ref, ref, psem, (s, 1, q, d), partner)

        for d in (2, 1, 3, 0):
            for q in range(3):
                pair(q, d).start()
        yield
        for d in (2, 1, 3, 0):
            for q in range(3):
                pair(q, d).wait()
                add_pair(q, d)
                if d:
                    first(q, d).start()
        yield
        for q in range(3):
            for d in range(1, 4):
                first(q, d).wait()
            total = b[q, at(coords[ORDERS[q][0]] * quarter, quarter), :].astype(F32)
            for d in range(3):
                total = total + fr[q, d].astype(F32)
            c[q] = total.astype(BF)
            for d in range(1, 4):
                second(q, d).start()
        yield
        for q in range(3):
            for d in range(1, 4):
                second(q, d).wait()
            total = c[q, at(coords[ORDERS[q][1]] * ch, ch), :].astype(F32)
            for d in range(3):
                total = total + sr[q, d].astype(F32)
            tr[q, coords[ORDERS[q][2]]] = total.astype(BF)
            for d in range(1, 4):
                third_copy(q, d).start()
        yield
        for q in range(3):
            for d in range(1, 4):
                third_copy(q, d).wait()
            total = tr[q, 0].astype(F32)
            for d in range(1, 4):
                total = total + tr[q, d].astype(F32)
            out[piece(q, 0, 0), :] = total.astype(BF)
            for d in (2, 1, 3):
                back_two(q, d).start()
            for d in (2, 1, 3):
                back_one(q, d, 0).start()
        yield
        for k in (1, 3, 2):
            for q in range(3):
                back_two(q, k).wait()
                for d in (2, 1, 3):
                    back_one(q, d, k).start()
        for q in range(3):
            back_pair(q, 0).start()
        yield
        for d in (1, 3, 2):
            for q in range(3):
                for k in range(4):
                    back_one(q, d, k).wait()
                back_pair(q, d).start()
        yield
        for d in (0, 1, 3, 2):
            for q in range(3):
                back_pair(q, d).wait()
        yield

    def gain_reduce():
        def pair():
            ref = gbuf.at[0, core]
            return remote(ref, ref, gsem, (0, 0), partner)

        def copy(k, d):
            axis = "xyz"[k - 1]
            ref = gbuf.at[k, coords[axis]]
            return remote(ref, ref, gsem, (k, d - 1), along(axis, d)[1])

        gbuf[0, core] = jnp.concatenate(
            [gains_acc[r : r + 1, j * 128 : (j + 1) * 128] for r in range(2) for j in range(4)],
            axis=0,
        )
        pair().start()
        yield
        pair().wait()
        total = gbuf[0, 0] + gbuf[0, 1]
        for k in range(1, 4):
            gbuf[k, coords["xyz"[k - 1]]] = total
            for d in range(1, 4):
                copy(k, d).start()
            yield
            for d in range(1, 4):
                copy(k, d).wait()
            total = (gbuf[k, 0] + gbuf[k, 1]) + (gbuf[k, 2] + gbuf[k, 3])
        gains_ref[...] = total
        yield

    red1 = all_reduce(0, CH1, a1, pr1, b1, fr1, c1, sr1, tr1, g1_ref)
    red2 = all_reduce(1, CH2, a2, pr2, b2, fr2, c2, sr2, tr2, g2_ref)
    red_g = gain_reduce()

    for g in range(N_GROUP):
        for i in range(4 * g, min(4 * g + 4, OWN)):
            data_copy(i).wait_recv()
        back_a(g)
        if g < N_GROUP - 1:
            back_b(g)
    put(a1, 0, dot(mixed_t[...], ret[...].reshape(TOK, D)))
    put(a1, 4 * D, dot(norm_t[...], gh_all[:, 0:D]))
    a1[8 * D : ROWS1, :] = jnp.zeros((ROWS1 - 8 * D, 128), BF)
    next(red1)
    back_b(3)
    next(red1)
    for k in range(3):
        put(a2, k * 4 * D, dot(norm_t[...], gh_all[:, (k + 1) * D : (k + 2) * D]))
    next(red2)
    next(red1)
    back_c(0)
    next(red2)
    back_c(1)
    next(red1)
    back_c(2)
    back_c(3)
    next(red_g)

    row_half = rows_acc[...].astype(BF)
    for c in range(CAP):
        picked = dot(sel_all[c], row_half)
        for k in range(4):
            spread[pl.ds(k * CAP + c, N_DEV, stride=16), :] = picked[:, k * 128 : (k + 1) * 128]
    send[...] = spread[...].astype(BF).reshape(N_DEV, 16, 128)
    got_ref[0] = send[me]

    def scatter_out(i, carry):
        other, to = device(i)
        remote(send.at[other], got_ref.at[i], asem, (0,), to).start()
        return carry

    next(red2)
    lax.fori_loop(1, 49, scatter_out, 0)
    next(red1)
    next(red_g)
    lax.fori_loop(49, 81, scatter_out, 0)
    next(red2)
    next(red1)
    next(red_g)
    lax.fori_loop(81, N_DEV, scatter_out, 0)
    next(red2)
    next(red1)
    next(red_g)
    next(red2)
    next(red_g)
    next(red1)

    def out_copy(src, dst, n):
        return pltpu.make_async_copy(src, dst, out_sem.at[n])

    outs = [out_copy(g1_ref, g1_out, 0), out_copy(gains_ref, gains_out, 1)]
    for o in outs:
        o.start()
    others = pl.ds(1, N_DEV - 1)
    remote(send.at[others], got_ref.at[others], asem, (0,), partner).wait()
    remote(meta.at[others], gotm_ref.at[others], asem, (1,), partner).wait()
    next(red2)
    half = pl.ds(pl.multiple_of(core * (ROWS2 // 2), 16), ROWS2 // 2)
    rest = pl.ds(pl.multiple_of((1 - core) * (ROWS2 // 2), 16), ROWS2 // 2)
    outs.append(out_copy(g2_ref.at[half], g2_out.at[half], 2))
    outs[-1].start()
    spread[...] = got_ref[...].reshape(N_DEV * 16, 128).astype(F32)
    for c in range(CAP):
        for k in range(4):
            picked_ref[c * N_DEV : (c + 1) * N_DEV, k * 128 : (k + 1) * 128] = spread[
                pl.ds(k * CAP + c, N_DEV, stride=16), :
            ].astype(BF)
    ids_ref[...] = jnp.transpose(gotm_ref[...].reshape(N_DEV, 128))
    outs.append(out_copy(picked_ref, picked_out, 3))
    outs[-1].start()
    outs.append(out_copy(ids_ref, ids_out, 4))
    outs[-1].start()
    for i in range(OWN):
        data_copy(i).wait_send()
    next(red2)
    outs.append(out_copy(g2_ref.at[rest], g2_out.at[rest], 5))
    outs[-1].start()
    for o in outs:
        o.wait()


def run_step(seq_dest, seq_blocks, items, owner, orow, gain_in, gain_out, touched, grad_out, w_in, w_out):
    smem = pl.BlockSpec(memory_space=pltpu.SMEM)
    vmem = pl.BlockSpec(memory_space=pltpu.VMEM)
    far = pl.BlockSpec(memory_space=pl.ANY)
    v = pltpu.VMEM
    dma = pltpu.SemaphoreType.DMA
    scratch = [
        v((UNIQ, D), BF),
        v((D, D), BF),
        v((D, 4 * D), BF),
        v((D, D), BF),
        dma((4,)),
        v((N_DP, 1, D), jnp.int32),
        v((N_DP, 1, D), jnp.int32),
        v((N_DP, 1, D), jnp.int32),
        v((N_DP, SLOT, D), BF),
        v((N_DP, SLOT, D), BF),
        dma((2, N_DP)),
        dma((2, N_DP)),
        pltpu.SemaphoreType.REGULAR,
        dma((6,)),
        v((UNIQ, TOK), BF),
        v((D, TOK), BF),
        v((D, TOK), BF),
        v((TOK, D), F32),
        v((TOK, 1), F32),
        v((TOK, D), F32),
        v((TOK, 1), F32),
        v((TOK, 4 * D), F32),
        v((TOK, D), F32),
        v((3, TOK, D), BF),
        v((GROUP, D), F32),
        v((N_GROUP * 2 * HEADS, 2, PAIR, PAIR), BF),
        v((TOK, D), BF),
        v((TOK, 4 * D), BF),
        v((UNIQ, D), F32),
        v((8, D), F32),
        v((N_DEV * 16, 128), F32),
        v((N_DEV, 16, 128), BF),
        v((N_DEV, 1, 128), F32),
        v((CAP, N_DEV, UNIQ), BF),
        v((ROWS1, 128), BF),
        v((ROWS2, 128), BF),
    ]
    for shape in ((3, 16), (3, 16), (3, 3, 4), (3, 4), (3, 3, 1), (3, 4, 1)):
        for ch in (CH1, CH2):
            scratch.append(v(shape[:-1] + (shape[-1] * ch, 128), BF))
    scratch += [
        v((4, 4, 8, 128), F32),
        dma((2, 2, 2, 3, 4)),
        dma((2, 2, 4, 3, 3)),
        dma((2, 2, 3, 3, 4)),
        dma((2, 2)),
        dma((2, 4, 3)),
        v((ROWS1, 128), BF),
        v((ROWS2, 128), BF),
        v((N_DEV, 16, 128), BF),
        v((N_DEV, 1, 128), F32),
        v((CAP * N_DEV, D), BF),
        v((128, N_DEV), F32),
        v((8, 128), F32),
    ]
    return pl.pallas_call(
        step_kernel,
        out_shape=(
            jax.ShapeDtypeStruct((ROWS1, 128), BF),
            jax.ShapeDtypeStruct((ROWS2, 128), BF),
            jax.ShapeDtypeStruct((CAP * N_DEV, D), BF),
            jax.ShapeDtypeStruct((128, N_DEV), F32),
            jax.ShapeDtypeStruct((8, 128), F32),
        ),
        in_specs=[smem] + [vmem] * 7 + [far] * 4,
        out_specs=(far,) * 5,
        scratch_shapes=scratch,
        compiler_params=pltpu.CompilerParams(
            collective_id=0, has_side_effects=True, vmem_limit_bytes=67_000_000
        ),
        name="step",
    )(
        seq_dest,
        seq_dest.reshape(1, -1),
        seq_blocks.reshape(1, -1),
        items.reshape(8, 128),
        owner.reshape(1, -1),
        orow.reshape(1, -1),
        gain_in.reshape(1, -1),
        gain_out.reshape(1, -1),
        touched,
        grad_out,
        w_in,
        w_out,
    )


def finish_kernel(
    g1_hbm,
    g2_hbm,
    picked_hbm,
    ids_ref,
    gains_in,
    table_out,
    win_out,
    wout_out,
    gin_ref,
    gout_ref,
    g1,
    g2,
    picked,
    table,
    win,
    wout,
    in_sem,
    out_sem,
    *,
    factor
):
    part = 4 * D

    def take(n):
        if n == 0:
            return pltpu.make_async_copy(picked_hbm, picked, in_sem.at[0])
        far, near = (g1_hbm, g1) if n < 3 else (g2_hbm, g2)
        rows = pl.ds(((n - 1) if n < 3 else (n - 3)) * part, part)
        return pltpu.make_async_copy(far.at[rows], near.at[rows], in_sem.at[n])

    def give(n):
        if n < 4:
            rows = pl.ds(n * 256, 256)
            return pltpu.make_async_copy(table.at[rows], table_out.at[rows], out_sem.at[n])
        if n == 4:
            return pltpu.make_async_copy(wout, wout_out, out_sem.at[n])
        cols = pl.ds((n - 5) * D, D)
        return pltpu.make_async_copy(win.at[n - 5], win_out.at[:, cols], out_sem.at[n])

    for n in range(6):
        take(n).start()
    for j in range(4):
        gin_ref[:, j * 128 : (j + 1) * 128] = gains_in[j : j + 1, :] * factor
        gout_ref[:, j * 128 : (j + 1) * 128] = gains_in[4 + j : 5 + j, :] * factor
    take(0).wait()
    for n in range(4):
        rows = (iota((256, N_DEV), 0) + n * 256).astype(F32)
        hot = jnp.concatenate(
            [jnp.where(rows == ids_ref[c : c + 1, :], 1.0, 0.0).astype(BF) for c in range(CAP)],
            axis=1,
        )
        table[n * 256 : (n + 1) * 256, :] = dot(hot, picked[...])
        give(n).start()
    for n in range(5):
        take(n + 1).wait()
        src, first = (g1, n * part) if n < 2 else (g2, (n - 2) * part)
        for j in range(4):
            block = src[first + j * D : first + (j + 1) * D, :].astype(F32) * factor
            cols = slice(j * 128, (j + 1) * 128)
            if n == 0:
                wout[:, cols] = block
            else:
                win[n - 1, :, cols] = block
        give(4 + n).start()
    for n in range(9):
        give(n).wait()


def finish(g1, g2, picked, ids, gains, factor):
    far = pl.BlockSpec(memory_space=pl.ANY)
    vmem = pl.BlockSpec(memory_space=pltpu.VMEM)

    def body(*refs):
        finish_kernel(*refs, factor=factor)

    return pl.pallas_call(
        body,
        out_shape=(
            jax.ShapeDtypeStruct((ROWS_DEV, D), F32),
            jax.ShapeDtypeStruct((D, 4 * D), F32),
            jax.ShapeDtypeStruct((D, D), F32),
            jax.ShapeDtypeStruct((1, D), F32),
            jax.ShapeDtypeStruct((1, D), F32),
        ),
        in_specs=[far] * 3 + [vmem] * 2,
        out_specs=(far, far, far, vmem, vmem),
        scratch_shapes=[
            pltpu.VMEM((ROWS1, 128), BF),
            pltpu.VMEM((ROWS2, 128), BF),
            pltpu.VMEM((CAP * N_DEV, D), BF),
            pltpu.VMEM((ROWS_DEV, D), F32),
            pltpu.VMEM((4, D, D), F32),
            pltpu.VMEM((D, D), F32),
            pltpu.SemaphoreType.DMA((6,)),
            pltpu.SemaphoreType.DMA((9,)),
        ],
        compiler_params=pltpu.CompilerParams(vmem_limit_bytes=67_000_000),
        name="finish",
    )(g1, g2, picked, ids, gains)


def on_device(
    touched_rows,
    row_of_token,
    row_owner,
    owner_row,
    seq_blocks,
    seq_dest,
    grad_out,
    w_in,
    w_out,
    gain_in,
    gain_out,
):
    g1, g2, picked, ids, gains = run_step(
        seq_dest,
        seq_blocks,
        row_of_token,
        row_owner,
        owner_row,
        gain_in,
        gain_out,
        touched_rows,
        grad_out,
        w_in,
        w_out,
    )
    factor = 1.0 / math.sqrt(grad_out.shape[0] * N_DEV)
    table, grad_in, grad_w_out, gin, gout = finish(g1, g2, picked, ids, gains, factor)
    return (table, grad_in, grad_w_out, gin.reshape(-1), gout.reshape(-1))


def solution(mesh):
    in_specs = (
        P(("dp", "table"), None),
        P(("dp", "table")),
        P(("dp", "table"), None),
        P(("dp", "table")),
        P(("dp", "table")),
        P(("dp", "table")),
        P(("dp", "table"), None),
        P(),
        P(),
        P(),
        P(),
    )
    out_specs = (P(("dp", "table"), None), P(), P(), P(), P())
    return jax.shard_map(
        on_device, mesh=mesh, in_specs=in_specs, out_specs=out_specs, check_vma=False
    )
```

```python
import math

import jax
import jax.numpy as jnp
from jax import lax
from jax.experimental import pallas as pl
from jax.experimental.pallas import tpu as pltpu
from jax.sharding import PartitionSpec as P

HEADS = 4
HDIM = 128
BLK = 16
LMAXB = 4
SLOT = 64
ROWS_DEV = 1024
UNIQ = 256
CAP = 4
D = 512
N_DP = 16
N_TABLE = 8
N_DEV = 128
GROUP = 256
N_GROUP = 4
TOK = 1024
PAIR = 128
CH1 = 48
CH2 = 64
ROWS1 = 96 * CH1
ROWS2 = 96 * CH2
EPSILON = 1e-05
MESH = pl.DeviceIdType.MESH
BF = jnp.bfloat16
F32 = jnp.float32


def dot(a, b):
    return jnp.dot(a, b, preferred_element_type=F32)


def dot_t(a, b):
    return lax.dot_general(a, b, (((1,), (1,)), ((), ())), preferred_element_type=F32)


def t_dot(a, b):
    return lax.dot_general(a, b, (((0,), (0,)), ((), ())), preferred_element_type=F32)


OFFSETS = tuple((i // 4, i % 4) for i in range(1, 16)) + ((0, 0),)
OWN = 15
ORDERS = (("x", "y", "z"), ("y", "z", "x"), ("z", "x", "y"))


def row_mean(v):
    return jnp.sum(v, axis=-1, keepdims=True) * (1.0 / D)


def sigmoid(v):
    return 0.5 * jnp.tanh(0.5 * v) + 0.5


def iota(shape, dim):
    return lax.broadcasted_iota(jnp.int32, shape, dim)


def step_kernel(
    dest_s,
    dest_l,
    blocks_l,
    items_ref,
    owner_ref,
    orow_ref,
    gin_ref,
    gout_ref,
    touched_hbm,
    grad_hbm,
    w_in_hbm,
    w_out_hbm,
    g1_ref,
    g2_ref,
    picked_ref,
    ids_ref,
    gains_ref,
    touched,
    grad_bal,
    w_in,
    w_out,
    load_sem,
    lens,
    got_len,
    wide,
    stage,
    ret,
    lsem,
    dsem,
    ready,
    hot_all,
    norm_t,
    mixed_t,
    hat_in_all,
    rstd_in_all,
    hat_out_all,
    rstd_out_all,
    slope_all,
    gate_all,
    vqk_all,
    att,
    wts,
    half_all,
    gh_all,
    rows_acc,
    gains_acc,
    spread,
    send,
    meta,
    sel_all,
    a1,
    a2,
    pr1,
    pr2,
    b1,
    b2,
    fr1,
    fr2,
    c1,
    c2,
    sr1,
    sr2,
    tr1,
    tr2,
    gbuf,
    psem,
    rsem,
    bsem,
    asem,
    gsem,
    got_ref,
    gotm_ref,
):
    dp = lax.axis_index("dp")
    tb = lax.axis_index("table")
    x = dp // 4
    z = dp % 4
    y = tb // 2
    core = tb % 2
    me = dp * N_TABLE + tb
    partner = (dp, y * 2 + 1 - core)
    coords = {"x": x, "y": y, "z": z}

    def device(i):
        other = lax.rem(me + i, N_DEV)
        return other, (other // N_TABLE, other % N_TABLE)

    def along(axis, d):
        v = lax.rem(coords[axis] + d, 4)
        to = {"x": (v * 4 + z, tb), "z": (x * 4 + v, tb), "y": (dp, v * 2 + core)}[axis]
        return v, to

    def plus(i):
        dx, dz = OFFSETS[i]
        return lax.rem(x + dx, 4) * 4 + lax.rem(z + dz, 4)

    def minus(i):
        dx, dz = OFFSETS[i]
        return lax.rem(x + 4 - dx, 4) * 4 + lax.rem(z + 4 - dz, 4)

    def remote(src, dst, sems, index, to):
        return pltpu.make_async_remote_copy(
            src_ref=src,
            dst_ref=dst,
            send_sem=sems.at[(0,) + index],
            recv_sem=sems.at[(1,) + index],
            device_id=to,
            device_id_type=MESH,
        )

    loads = [
        pltpu.make_async_copy(touched_hbm, touched, load_sem.at[0]),
        pltpu.make_async_copy(w_in_hbm, w_in, load_sem.at[1]),
        pltpu.make_async_copy(grad_hbm, grad_bal, load_sem.at[2]),
        pltpu.make_async_copy(w_out_hbm, w_out, load_sem.at[3]),
    ]
    for load in loads:
        load.start()

    barrier = pltpu.get_barrier_semaphore()

    def column(i):
        return (dp, lax.rem(tb + i, N_TABLE))

    for i in range(OWN):
        pl.semaphore_signal(barrier, inc=1, device_id=(plus(i), tb), device_id_type=MESH)
    for i in range(1, N_TABLE):
        pl.semaphore_signal(barrier, inc=1, device_id=column(i), device_id_type=MESH)

    hits = dest_l[...] == iota((N_DP, N_DP), 0)
    lengths = jnp.sum(
        jnp.where(hits, blocks_l[...].astype(F32), 0.0), axis=1, keepdims=True
    )
    lengths = jnp.broadcast_to(lengths, (N_DP, D)).astype(jnp.int32)
    for p in range(N_DP):
        lens[p] = lengths[p : p + 1, :]

    gain_in = gin_ref[...]
    gain_out = gout_ref[...]
    gains_acc[...] = jnp.zeros_like(gains_acc)
    lane = iota((1, 128), 1)

    def item_pair(i):
        rows = []
        for k in range(2):
            peer = plus(i + k)
            slot = jnp.int32(0)
            for j in range(N_DP):
                slot = jnp.where(dest_s[j] == peer, j, slot)
            row = items_ref[pl.ds(slot // 2, 1), :]
            turned = pltpu.roll(row, 64, 1)
            rows.append(jnp.where(jnp.broadcast_to(slot % 2, (1, 128)) == k, row, turned))
        return jnp.where(lane < 64, rows[0], rows[1])

    def forward(g):
        here = slice(g * GROUP, (g + 1) * GROUP)
        items = jnp.concatenate([item_pair(4 * g), item_pair(4 * g + 2)], axis=1)
        hot = (iota((UNIQ, GROUP), 0) == items).astype(F32).astype(BF)
        hot_all[:, here] = hot
        tok = t_dot(hot, touched[...])
        shifted = tok - row_mean(tok)
        rstd = lax.rsqrt(row_mean(shifted * shifted) + EPSILON)
        rstd_in_all[here, :] = rstd
        hat = shifted * rstd
        hat_in_all[here, :] = hat
        normed = hat * gain_in
        norm_t[:, here] = jnp.transpose(normed).astype(BF)
        normed = normed.astype(BF)
        for k in range(4):
            cols = slice(k * D, (k + 1) * D)
            hid = dot(normed, w_in[:, cols])
            sig = sigmoid(hid)
            act = hid * sig
            slope_all[here, cols] = sig + act * (1.0 - sig)
            if k == 0:
                gate_all[here, :] = act
            else:
                vqk_all[k - 1, here, :] = act.astype(BF)
        ri = iota((PAIR, PAIR), 0)
        ci = iota((PAIR, PAIR), 1)
        allowed = ((ri < SLOT) == (ci < SLOT)) & (ci <= ri)
        scale = HDIM ** (-0.5)
        for s in range(2):
            rows = slice(g * GROUP + s * PAIR, g * GROUP + (s + 1) * PAIR)
            for h in range(HEADS):
                cols = slice(h * HDIM, (h + 1) * HDIM)
                n = (g * 2 + s) * HEADS + h
                score = dot_t(vqk_all[1, rows, cols], vqk_all[2, rows, cols]) * scale
                sig = sigmoid(score)
                act = score * sig
                weight = jnp.where(allowed, act, 0.0).astype(BF)
                wts[n, 0] = weight
                wts[n, 1] = jnp.where(allowed, (sig + act * (1.0 - sig)) * scale, 0.0).astype(BF)
                att[s * PAIR : (s + 1) * PAIR, cols] = dot(weight, vqk_all[0, rows, cols])
        attended = att[...]
        shifted = attended - row_mean(attended)
        rstd = lax.rsqrt(row_mean(shifted * shifted) + EPSILON)
        rstd_out_all[here, :] = rstd
        hat = shifted * rstd
        hat_out_all[here, :] = hat
        mixed_t[:, here] = jnp.transpose(hat * gain_out * gate_all[here, :]).astype(BF)

    pl.semaphore_wait(barrier, OWN + N_TABLE - 1)

    def len_copy(i):
        return remote(lens.at[minus(i)], got_len.at[dp], lsem, (i,), (minus(i), tb))

    for i in range(OWN):
        len_copy(i).start()
    got_len[dp] = lens[dp]
    for i in range(1, N_TABLE):
        pl.semaphore_signal(ready, inc=1, device_id=column(i), device_id_type=MESH)
    loads[0].wait()
    loads[1].wait()
    forward(0)
    for i in range(OWN):
        len_copy(i).wait()
    loads[2].wait()
    loads[3].wait()

    start = jnp.zeros((1, D), jnp.int32)
    for p in range(N_DP):
        wide[p] = start
        start = start + got_len[p]
    row_id = iota((SLOT, D), 0)
    col_id = iota((SLOT, D), 1)

    def pick(p):
        hit = (col_id == wide[p] * BLK + row_id) & (row_id < got_len[p] * BLK)
        return hit.astype(F32).astype(BF)

    def data_copy(i):
        return remote(stage.at[i], ret.at[i], dsem, (i,), (minus(i), tb))

    for g in range(N_GROUP):
        hot = jnp.concatenate([pick(minus(4 * g + k)) for k in range(4)], axis=0)
        slabs = dot(hot, grad_bal[...]).astype(BF)
        for k in range(4):
            i = 4 * g + k
            slab = slabs[k * SLOT : (k + 1) * SLOT, :]
            if i == OWN:
                ret[OWN] = slab
            else:
                stage[i] = slab
                data_copy(i).start()

    forward(1)

    owner = jnp.broadcast_to(owner_ref[...].astype(F32), (UNIQ, UNIQ))
    owner_col = jnp.transpose(owner)
    before = iota((UNIQ, UNIQ), 0) < iota((UNIQ, UNIQ), 1)
    rank = jnp.sum(jnp.where((owner == owner_col) & before, 1.0, 0.0), axis=0, keepdims=True)
    mine = iota((N_DEV, UNIQ), 0) == owner_ref[...]
    lanes = iota((N_DEV, 128), 1)
    ids_all = jnp.zeros((N_DEV, 128), F32)
    order_f = orow_ref[...].astype(F32)
    for c in range(CAP):
        sel = jnp.where(mine & (rank == float(c)), 1.0, 0.0)
        sel_all[c] = sel.astype(BF)
        ids_all = jnp.where(lanes == c, jnp.sum(sel * order_f, axis=1, keepdims=True), ids_all)
    meta[...] = ids_all.reshape(N_DEV, 1, 128)

    def meta_out(i, carry):
        other, to = device(i)
        remote(meta.at[other], gotm_ref.at[i], asem, (1,), to).start()
        return carry

    pl.semaphore_wait(ready, N_TABLE - 1)
    lax.fori_loop(1, N_DEV, meta_out, 0)
    gotm_ref[0] = meta[me]

    forward(2)
    forward(3)

    def back_a(g):
        here = slice(g * GROUP, (g + 1) * GROUP)
        gy = ret[4 * g : 4 * g + 4].reshape(GROUP, D)
        hat = hat_out_all[here, :]
        grad_mixed = dot_t(gy, w_out[...])
        gh_all[here, 0:D] = (grad_mixed * (hat * gain_out) * slope_all[here, 0:D]).astype(BF)
        cot = grad_mixed * gate_all[here, :]
        gains_acc[1:2, :] += jnp.sum(cot * hat, axis=0, keepdims=True)
        dhat = cot * gain_out
        half_all[here, :] = (
            rstd_out_all[here, :] * (dhat - row_mean(dhat) - hat * row_mean(dhat * hat))
        ).astype(BF)

    def back_b(g):
        for s in range(2):
            rows = slice(g * GROUP + s * PAIR, g * GROUP + (s + 1) * PAIR)
            for h in range(HEADS):
                cols = slice(h * HDIM, (h + 1) * HDIM)
                n = (g * 2 + s) * HEADS + h
                half = half_all[rows, cols]
                grad_weight = dot_t(half, vqk_all[0, rows, cols])
                gs = (grad_weight * wts[n, 1].astype(F32)).astype(BF)
                parts = (
                    t_dot(wts[n, 0], half),
                    dot(gs, vqk_all[2, rows, cols]),
                    t_dot(gs, vqk_all[1, rows, cols]),
                )
                for k in range(3):
                    at = slice((k + 1) * D + h * HDIM, (k + 1) * D + (h + 1) * HDIM)
                    gh_all[rows, at] = (parts[k] * slope_all[rows, at]).astype(BF)

    def back_c(g):
        here = slice(g * GROUP, (g + 1) * GROUP)
        gy = ret[4 * g : 4 * g + 4].reshape(GROUP, D).astype(F32)
        hat = hat_in_all[here, :]
        grad_normed = dot_t(gh_all[here, :], w_in[...])
        gains_acc[0:1, :] += jnp.sum(grad_normed * hat, axis=0, keepdims=True)
        dhat = grad_normed * gain_in
        inner = rstd_in_all[here, :] * (dhat - row_mean(dhat) - hat * row_mean(dhat * hat))
        grad_tok = (inner + gy).astype(BF)
        part = dot(hot_all[:, here], grad_tok)
        if g == 0:
            rows_acc[...] = part
        else:
            rows_acc[...] += part

    def put(dst, first, block):
        for j in range(4):
            dst[first + j * D : first + (j + 1) * D, :] = block[:, j * 128 : (j + 1) * 128].astype(BF)

    def all_reduce(s, ch, a, pr, b, fr, c, sr, tr, out):
        third = 16 * ch
        quarter = 4 * ch

        def at(row, size):
            return pl.ds(pl.multiple_of(row, 16), size)

        def pair(q, d):
            v = along(ORDERS[q][0], d)[0]
            src = a.at[at(((1 - core) * 3 + q) * third + v * quarter, quarter)]
            return remote(src, pr.at[q, at(v * quarter, quarter)], psem, (s, 0, q, d), partner)

        def add_pair(q, d):
            v = along(ORDERS[q][0], d)[0]
            own = a[at((core * 3 + q) * third + v * quarter, quarter), :].astype(F32)
            rows = at(v * quarter, quarter)
            b[q, rows, :] = (own + pr[q, rows, :].astype(F32)).astype(BF)

        def first(q, d):
            v, to = along(ORDERS[q][0], d)
            return remote(b.at[q, at(v * quarter, quarter)], fr.at[q, d - 1], rsem, (s, 0, q, d - 1), to)

        def second(q, d):
            v, to = along(ORDERS[q][1], d)
            return remote(c.at[q, at(v * ch, ch)], sr.at[q, d - 1], rsem, (s, 1, q, d - 1), to)

        def third_copy(q, d):
            mine = coords[ORDERS[q][2]]
            to = along(ORDERS[q][2], d)[1]
            return remote(tr.at[q, mine], tr.at[q, mine], rsem, (s, 2, q, d - 1), to)

        def piece(q, da, db):
            va = along(ORDERS[q][0], 4 - da)[0]
            vb = along(ORDERS[q][1], 4 - db)[0]
            return at((core * 3 + q) * third + va * quarter + vb * ch, ch)

        def back_two(q, d):
            ref = out.at[piece(q, 0, 0)]
            return remote(ref, ref, rsem, (s, 3, q, d - 1), along(ORDERS[q][1], d)[1])

        def back_one(q, d, k):
            ref = out.at[piece(q, 0, k)]
            return remote(ref, ref, bsem, (s, q, d - 1, k), along(ORDERS[q][0], d)[1])

        def back_pair(q, d):
            va = along(ORDERS[q][0], 4 - d)[0]
            ref = out.at[at((core * 3 + q) * third + va * quarter, quarter)]
            return remote(ref, ref, psem, (s, 1, q, d), partner)

        for d in (2, 1, 3, 0):
            for q in range(3):
                pair(q, d).start()
        yield
        for d in (2, 1, 3, 0):
            for q in range(3):
                pair(q, d).wait()
                add_pair(q, d)
                if d:
                    first(q, d).start()
        yield
        for q in range(3):
            for d in range(1, 4):
                first(q, d).wait()
            total = b[q, at(coords[ORDERS[q][0]] * quarter, quarter), :].astype(F32)
            for d in range(3):
                total = total + fr[q, d].astype(F32)
            c[q] = total.astype(BF)
            for d in range(1, 4):
                second(q, d).start()
        yield
        for q in range(3):
            for d in range(1, 4):
                second(q, d).wait()
            total = c[q, at(coords[ORDERS[q][1]] * ch, ch), :].astype(F32)
            for d in range(3):
                total = total + sr[q, d].astype(F32)
            tr[q, coords[ORDERS[q][2]]] = total.astype(BF)
            for d in range(1, 4):
                third_copy(q, d).start()
        yield
        for q in range(3):
            for d in range(1, 4):
                third_copy(q, d).wait()
            total = tr[q, 0].astype(F32)
            for d in range(1, 4):
                total = total + tr[q, d].astype(F32)
            out[piece(q, 0, 0), :] = total.astype(BF)
            for d in (2, 1, 3):
                back_two(q, d).start()
            for d in (2, 1, 3):
                back_one(q, d, 0).start()
        yield
        for k in (1, 3, 2):
            for q in range(3):
                back_two(q, k).wait()
                for d in (2, 1, 3):
                    back_one(q, d, k).start()
        for q in range(3):
            back_pair(q, 0).start()
        yield
        for d in (1, 3, 2):
            for q in range(3):
                for k in range(4):
                    back_one(q, d, k).wait()
                back_pair(q, d).start()
        yield
        for d in (0, 1, 3, 2):
            for q in range(3):
                back_pair(q, d).wait()
        yield

    def gain_reduce():
        def pair():
            ref = gbuf.at[0, core]
            return remote(ref, ref, gsem, (0, 0), partner)

        def copy(k, d):
            axis = "xyz"[k - 1]
            ref = gbuf.at[k, coords[axis]]
            return remote(ref, ref, gsem, (k, d - 1), along(axis, d)[1])

        gbuf[0, core] = jnp.concatenate(
            [gains_acc[r : r + 1, j * 128 : (j + 1) * 128] for r in range(2) for j in range(4)],
            axis=0,
        )
        pair().start()
        yield
        pair().wait()
        total = gbuf[0, 0] + gbuf[0, 1]
        for k in range(1, 4):
            gbuf[k, coords["xyz"[k - 1]]] = total
            for d in range(1, 4):
                copy(k, d).start()
            yield
            for d in range(1, 4):
                copy(k, d).wait()
            total = (gbuf[k, 0] + gbuf[k, 1]) + (gbuf[k, 2] + gbuf[k, 3])
        gains_ref[...] = total
        yield

    red1 = all_reduce(0, CH1, a1, pr1, b1, fr1, c1, sr1, tr1, g1_ref)
    red2 = all_reduce(1, CH2, a2, pr2, b2, fr2, c2, sr2, tr2, g2_ref)
    red_g = gain_reduce()

    for g in range(N_GROUP):
        for i in range(4 * g, min(4 * g + 4, OWN)):
            data_copy(i).wait_recv()
        back_a(g)
        if g < N_GROUP - 1:
            back_b(g)
    put(a1, 0, dot(mixed_t[...], ret[...].reshape(TOK, D)))
    put(a1, 4 * D, dot(norm_t[...], gh_all[:, 0:D]))
    a1[8 * D : ROWS1, :] = jnp.zeros((ROWS1 - 8 * D, 128), BF)
    next(red1)
    back_b(3)
    next(red1)
    for k in range(3):
        put(a2, k * 4 * D, dot(norm_t[...], gh_all[:, (k + 1) * D : (k + 2) * D]))
    next(red2)
    next(red1)
    back_c(0)
    next(red2)
    back_c(1)
    next(red1)
    back_c(2)
    back_c(3)
    next(red_g)

    row_half = rows_acc[...].astype(BF)
    for c in range(CAP):
        picked = dot(sel_all[c], row_half)
        for k in range(4):
            spread[pl.ds(k * CAP + c, N_DEV, stride=16), :] = picked[:, k * 128 : (k + 1) * 128]
    send[...] = spread[...].astype(BF).reshape(N_DEV, 16, 128)
    got_ref[0] = send[me]

    def scatter_out(i, carry):
        other, to = device(i)
        remote(send.at[other], got_ref.at[i], asem, (0,), to).start()
        return carry

    next(red2)
    lax.fori_loop(1, 49, scatter_out, 0)
    next(red1)
    next(red_g)
    lax.fori_loop(49, 81, scatter_out, 0)
    next(red2)
    next(red1)
    next(red_g)
    lax.fori_loop(81, N_DEV, scatter_out, 0)
    next(red2)
    next(red1)
    next(red_g)
    next(red2)
    next(red_g)
    next(red1)

    others = pl.ds(1, N_DEV - 1)
    remote(send.at[others], got_ref.at[others], asem, (0,), partner).wait()
    remote(meta.at[others], gotm_ref.at[others], asem, (1,), partner).wait()
    next(red2)
    spread[...] = got_ref[...].reshape(N_DEV * 16, 128).astype(F32)
    for c in range(CAP):
        for k in range(4):
            picked_ref[c * N_DEV : (c + 1) * N_DEV, k * 128 : (k + 1) * 128] = spread[
                pl.ds(k * CAP + c, N_DEV, stride=16), :
            ].astype(BF)
    ids_ref[...] = jnp.transpose(gotm_ref[...].reshape(N_DEV, 128))
    for i in range(OWN):
        data_copy(i).wait_send()
    next(red2)


def run_step(seq_dest, seq_blocks, items, owner, orow, gain_in, gain_out, touched, grad_out, w_in, w_out):
    smem = pl.BlockSpec(memory_space=pltpu.SMEM)
    vmem = pl.BlockSpec(memory_space=pltpu.VMEM)
    far = pl.BlockSpec(memory_space=pl.ANY)
    v = pltpu.VMEM
    dma = pltpu.SemaphoreType.DMA
    scratch = [
        v((UNIQ, D), BF),
        v((D, D), BF),
        v((D, 4 * D), BF),
        v((D, D), BF),
        dma((4,)),
        v((N_DP, 1, D), jnp.int32),
        v((N_DP, 1, D), jnp.int32),
        v((N_DP, 1, D), jnp.int32),
        v((N_DP, SLOT, D), BF),
        v((N_DP, SLOT, D), BF),
        dma((2, N_DP)),
        dma((2, N_DP)),
        pltpu.SemaphoreType.REGULAR,
        v((UNIQ, TOK), BF),
        v((D, TOK), BF),
        v((D, TOK), BF),
        v((TOK, D), F32),
        v((TOK, 1), F32),
        v((TOK, D), F32),
        v((TOK, 1), F32),
        v((TOK, 4 * D), F32),
        v((TOK, D), F32),
        v((3, TOK, D), BF),
        v((GROUP, D), F32),
        v((N_GROUP * 2 * HEADS, 2, PAIR, PAIR), BF),
        v((TOK, D), BF),
        v((TOK, 4 * D), BF),
        v((UNIQ, D), F32),
        v((8, D), F32),
        v((N_DEV * 16, 128), F32),
        v((N_DEV, 16, 128), BF),
        v((N_DEV, 1, 128), F32),
        v((CAP, N_DEV, UNIQ), BF),
        v((ROWS1, 128), BF),
        v((ROWS2, 128), BF),
    ]
    for shape in ((3, 16), (3, 16), (3, 3, 4), (3, 4), (3, 3, 1), (3, 4, 1)):
        for ch in (CH1, CH2):
            scratch.append(v(shape[:-1] + (shape[-1] * ch, 128), BF))
    scratch += [
        v((4, 4, 8, 128), F32),
        dma((2, 2, 2, 3, 4)),
        dma((2, 2, 4, 3, 3)),
        dma((2, 2, 3, 3, 4)),
        dma((2, 2)),
        dma((2, 4, 3)),
        v((N_DEV, 16, 128), BF),
        v((N_DEV, 1, 128), F32),
    ]
    return pl.pallas_call(
        step_kernel,
        out_shape=(
            pltpu.VMEM((ROWS1, 128), BF),
            pltpu.VMEM((ROWS2, 128), BF),
            pltpu.VMEM((CAP * N_DEV, D), BF),
            pltpu.VMEM((128, N_DEV), F32),
            pltpu.VMEM((8, 128), F32),
        ),
        in_specs=[smem] + [vmem] * 7 + [far] * 4,
        out_specs=(vmem,) * 5,
        scratch_shapes=scratch,
        compiler_params=pltpu.CompilerParams(
            collective_id=0, has_side_effects=True, vmem_limit_bytes=60_000_000
        ),
        name="step",
    )(
        seq_dest,
        seq_dest.reshape(1, -1),
        seq_blocks.reshape(1, -1),
        items.reshape(8, 128),
        owner.reshape(1, -1),
        orow.reshape(1, -1),
        gain_in.reshape(1, -1),
        gain_out.reshape(1, -1),
        touched,
        grad_out,
        w_in,
        w_out,
    )


def finish_kernel(
    g1,
    g2,
    picked,
    ids_ref,
    gains_in,
    table_out,
    win_out,
    wout_out,
    gin_ref,
    gout_ref,
    table,
    win,
    wout,
    out_sem,
    *,
    factor
):
    part = 4 * D

    def give(n):
        if n < 4:
            rows = pl.ds(n * 256, 256)
            return pltpu.make_async_copy(table.at[rows], table_out.at[rows], out_sem.at[n])
        if n == 4:
            return pltpu.make_async_copy(wout, wout_out, out_sem.at[n])
        cols = pl.ds((n - 5) * D, D)
        return pltpu.make_async_copy(win.at[n - 5], win_out.at[:, cols], out_sem.at[n])

    for j in range(4):
        gin_ref[:, j * 128 : (j + 1) * 128] = gains_in[j : j + 1, :] * factor
        gout_ref[:, j * 128 : (j + 1) * 128] = gains_in[4 + j : 5 + j, :] * factor
    for n in range(4):
        rows = (iota((256, N_DEV), 0) + n * 256).astype(F32)
        hot = jnp.concatenate(
            [jnp.where(rows == ids_ref[c : c + 1, :], 1.0, 0.0).astype(BF) for c in range(CAP)],
            axis=1,
        )
        table[n * 256 : (n + 1) * 256, :] = dot(hot, picked[...])
        give(n).start()
    for n in range(5):
        src, first = (g1, n * part) if n < 2 else (g2, (n - 2) * part)
        for j in range(4):
            block = src[first + j * D : first + (j + 1) * D, :].astype(F32) * factor
            cols = slice(j * 128, (j + 1) * 128)
            if n == 0:
                wout[:, cols] = block
            else:
                win[n - 1, :, cols] = block
        give(4 + n).start()
    for n in range(9):
        give(n).wait()


def finish(g1, g2, picked, ids, gains, factor):
    far = pl.BlockSpec(memory_space=pl.ANY)
    vmem = pl.BlockSpec(memory_space=pltpu.VMEM)

    def body(*refs):
        finish_kernel(*refs, factor=factor)

    return pl.pallas_call(
        body,
        out_shape=(
            jax.ShapeDtypeStruct((ROWS_DEV, D), F32),
            jax.ShapeDtypeStruct((D, 4 * D), F32),
            jax.ShapeDtypeStruct((D, D), F32),
            jax.ShapeDtypeStruct((1, D), F32),
            jax.ShapeDtypeStruct((1, D), F32),
        ),
        in_specs=[vmem] * 5,
        out_specs=(far, far, far, vmem, vmem),
        scratch_shapes=[
            pltpu.VMEM((ROWS_DEV, D), F32),
            pltpu.VMEM((4, D, D), F32),
            pltpu.VMEM((D, D), F32),
            pltpu.SemaphoreType.DMA((9,)),
        ],
        compiler_params=pltpu.CompilerParams(vmem_limit_bytes=24_000_000),
        name="finish",
    )(g1, g2, picked, ids, gains)


def on_device(
    touched_rows,
    row_of_token,
    row_owner,
    owner_row,
    seq_blocks,
    seq_dest,
    grad_out,
    w_in,
    w_out,
    gain_in,
    gain_out,
):
    g1, g2, picked, ids, gains = run_step(
        seq_dest,
        seq_blocks,
        row_of_token,
        row_owner,
        owner_row,
        gain_in,
        gain_out,
        touched_rows,
        grad_out,
        w_in,
        w_out,
    )
    factor = 1.0 / math.sqrt(grad_out.shape[0] * N_DEV)
    table, grad_in, grad_w_out, gin, gout = finish(g1, g2, picked, ids, gains, factor)
    return (table, grad_in, grad_w_out, gin.reshape(-1), gout.reshape(-1))


def solution(mesh):
    in_specs = (
        P(("dp", "table"), None),
        P(("dp", "table")),
        P(("dp", "table"), None),
        P(("dp", "table")),
        P(("dp", "table")),
        P(("dp", "table")),
        P(("dp", "table"), None),
        P(),
        P(),
        P(),
        P(),
    )
    out_specs = (P(("dp", "table"), None), P(), P(), P(), P())
    return jax.shard_map(
        on_device, mesh=mesh, in_specs=in_specs, out_specs=out_specs, check_vma=False
    )
```

```python
import math

import jax
import jax.numpy as jnp
from jax import lax
from jax.experimental import pallas as pl
from jax.experimental.pallas import tpu as pltpu
from jax.sharding import PartitionSpec as P

HEADS = 4
HDIM = 128
BLK = 16
LMAXB = 4
SLOT = 64
ROWS_DEV = 1024
UNIQ = 256
CAP = 4
D = 512
N_DP = 16
N_TABLE = 8
N_DEV = 128
GROUP = 256
N_GROUP = 4
TOK = 1024
PAIR = 128
CH1 = 48
CH2 = 64
ROWS1 = 96 * CH1
ROWS2 = 96 * CH2
EPSILON = 1e-05
MESH = pl.DeviceIdType.MESH
BF = jnp.bfloat16
F32 = jnp.float32


def dot(a, b):
    return jnp.dot(a, b, preferred_element_type=F32)


def dot_t(a, b):
    return lax.dot_general(a, b, (((1,), (1,)), ((), ())), preferred_element_type=F32)


def t_dot(a, b):
    return lax.dot_general(a, b, (((0,), (0,)), ((), ())), preferred_element_type=F32)


OFFSETS = tuple((i // 4, i % 4) for i in range(1, 16)) + ((0, 0),)
OWN = 15
ORDERS = (("x", "y", "z"), ("y", "z", "x"), ("z", "x", "y"))


def row_mean(v):
    return jnp.sum(v, axis=-1, keepdims=True) * (1.0 / D)


def sigmoid(v):
    return 0.5 * jnp.tanh(0.5 * v) + 0.5


def iota(shape, dim):
    return lax.broadcasted_iota(jnp.int32, shape, dim)


def step_kernel(
    dest_s,
    dest_l,
    blocks_l,
    items_ref,
    owner_ref,
    orow_ref,
    gin_ref,
    gout_ref,
    touched_hbm,
    grad_hbm,
    w_in_hbm,
    w_out_hbm,
    g1_ref,
    g2_ref,
    picked_ref,
    ids_ref,
    gains_ref,
    touched,
    grad_bal,
    w_in,
    w_out,
    load_sem,
    lens,
    got_len,
    wide,
    stage,
    ret,
    lsem,
    dsem,
    ready,
    hot_all,
    norm_t,
    mixed_t,
    hat_in_all,
    rstd_in_all,
    hat_out_all,
    rstd_out_all,
    slope_all,
    gate_all,
    vqk_all,
    att,
    wts,
    half_all,
    gh_all,
    rows_acc,
    gains_acc,
    spread,
    send,
    meta,
    sel_all,
    a1,
    a2,
    pr1,
    pr2,
    b1,
    b2,
    fr1,
    fr2,
    c1,
    c2,
    sr1,
    sr2,
    tr1,
    tr2,
    gbuf,
    psem,
    rsem,
    bsem,
    asem,
    gsem,
    got_ref,
    gotm_ref,
):
    dp = lax.axis_index("dp")
    tb = lax.axis_index("table")
    x = dp // 4
    z = dp % 4
    y = tb // 2
    core = tb % 2
    me = dp * N_TABLE + tb
    partner = (dp, y * 2 + 1 - core)
    coords = {"x": x, "y": y, "z": z}

    def device(i):
        other = lax.rem(me + i, N_DEV)
        return other, (other // N_TABLE, other % N_TABLE)

    def along(axis, d):
        v = lax.rem(coords[axis] + d, 4)
        to = {"x": (v * 4 + z, tb), "z": (x * 4 + v, tb), "y": (dp, v * 2 + core)}[axis]
        return v, to

    def plus(i):
        dx, dz = OFFSETS[i]
        return lax.rem(x + dx, 4) * 4 + lax.rem(z + dz, 4)

    def minus(i):
        dx, dz = OFFSETS[i]
        return lax.rem(x + 4 - dx, 4) * 4 + lax.rem(z + 4 - dz, 4)

    def remote(src, dst, sems, index, to):
        return pltpu.make_async_remote_copy(
            src_ref=src,
            dst_ref=dst,
            send_sem=sems.at[(0,) + index],
            recv_sem=sems.at[(1,) + index],
            device_id=to,
            device_id_type=MESH,
        )

    loads = [
        pltpu.make_async_copy(touched_hbm, touched, load_sem.at[0]),
        pltpu.make_async_copy(w_in_hbm, w_in, load_sem.at[1]),
        pltpu.make_async_copy(grad_hbm, grad_bal, load_sem.at[2]),
        pltpu.make_async_copy(w_out_hbm, w_out, load_sem.at[3]),
    ]
    for load in loads:
        load.start()

    barrier = pltpu.get_barrier_semaphore()

    def column(i):
        return (dp, lax.rem(tb + i, N_TABLE))

    for i in range(OWN):
        pl.semaphore_signal(barrier, inc=1, device_id=(plus(i), tb), device_id_type=MESH)
    for i in range(1, N_TABLE):
        pl.semaphore_signal(barrier, inc=1, device_id=column(i), device_id_type=MESH)

    hits = dest_l[...] == iota((N_DP, N_DP), 0)
    lengths = jnp.sum(
        jnp.where(hits, blocks_l[...].astype(F32), 0.0), axis=1, keepdims=True
    )
    lengths = jnp.broadcast_to(lengths, (N_DP, D)).astype(jnp.int32)
    for p in range(N_DP):
        lens[p] = lengths[p : p + 1, :]

    gain_in = gin_ref[...]
    gain_out = gout_ref[...]
    gains_acc[...] = jnp.zeros_like(gains_acc)
    lane = iota((1, 128), 1)

    def item_pair(i):
        rows = []
        for k in range(2):
            peer = plus(i + k)
            slot = jnp.int32(0)
            for j in range(N_DP):
                slot = jnp.where(dest_s[j] == peer, j, slot)
            row = items_ref[pl.ds(slot // 2, 1), :]
            turned = pltpu.roll(row, 64, 1)
            rows.append(jnp.where(jnp.broadcast_to(slot % 2, (1, 128)) == k, row, turned))
        return jnp.where(lane < 64, rows[0], rows[1])

    def forward(g):
        here = slice(g * GROUP, (g + 1) * GROUP)
        items = jnp.concatenate([item_pair(4 * g), item_pair(4 * g + 2)], axis=1)
        hot = (iota((UNIQ, GROUP), 0) == items).astype(F32).astype(BF)
        hot_all[:, here] = hot
        tok = t_dot(hot, touched[...])
        shifted = tok - row_mean(tok)
        rstd = lax.rsqrt(row_mean(shifted * shifted) + EPSILON)
        rstd_in_all[here, :] = rstd
        hat = shifted * rstd
        hat_in_all[here, :] = hat
        normed = hat * gain_in
        norm_t[:, here] = jnp.transpose(normed).astype(BF)
        normed = normed.astype(BF)
        for k in range(4):
            cols = slice(k * D, (k + 1) * D)
            hid = dot(normed, w_in[:, cols])
            sig = sigmoid(hid)
            act = hid * sig
            slope_all[here, cols] = sig + act * (1.0 - sig)
            if k == 0:
                gate_all[here, :] = act
            else:
                vqk_all[k - 1, here, :] = act.astype(BF)
        ri = iota((PAIR, PAIR), 0)
        ci = iota((PAIR, PAIR), 1)
        allowed = ((ri < SLOT) == (ci < SLOT)) & (ci <= ri)
        scale = HDIM ** (-0.5)
        for s in range(2):
            rows = slice(g * GROUP + s * PAIR, g * GROUP + (s + 1) * PAIR)
            for h in range(HEADS):
                cols = slice(h * HDIM, (h + 1) * HDIM)
                n = (g * 2 + s) * HEADS + h
                score = dot_t(vqk_all[1, rows, cols], vqk_all[2, rows, cols]) * scale
                sig = sigmoid(score)
                act = score * sig
                weight = jnp.where(allowed, act, 0.0).astype(BF)
                wts[n, 0] = weight
                wts[n, 1] = jnp.where(allowed, (sig + act * (1.0 - sig)) * scale, 0.0).astype(BF)
                att[s * PAIR : (s + 1) * PAIR, cols] = dot(weight, vqk_all[0, rows, cols])
        attended = att[...]
        shifted = attended - row_mean(attended)
        rstd = lax.rsqrt(row_mean(shifted * shifted) + EPSILON)
        rstd_out_all[here, :] = rstd
        hat = shifted * rstd
        hat_out_all[here, :] = hat
        mixed_t[:, here] = jnp.transpose(hat * gain_out * gate_all[here, :]).astype(BF)

    pl.semaphore_wait(barrier, OWN + N_TABLE - 1)

    def len_copy(i):
        return remote(lens.at[minus(i)], got_len.at[dp], lsem, (i,), (minus(i), tb))

    for i in range(OWN):
        len_copy(i).start()
    got_len[dp] = lens[dp]
    for i in range(1, N_TABLE):
        pl.semaphore_signal(ready, inc=1, device_id=column(i), device_id_type=MESH)
    loads[0].wait()
    loads[1].wait()
    forward(0)
    for i in range(OWN):
        len_copy(i).wait()
    loads[2].wait()
    loads[3].wait()

    start = jnp.zeros((1, D), jnp.int32)
    for p in range(N_DP):
        wide[p] = start
        start = start + got_len[p]
    row_id = iota((SLOT, D), 0)
    col_id = iota((SLOT, D), 1)

    def pick(p):
        hit = (col_id == wide[p] * BLK + row_id) & (row_id < got_len[p] * BLK)
        return hit.astype(F32).astype(BF)

    def data_copy(i):
        return remote(stage.at[i], ret.at[i], dsem, (i,), (minus(i), tb))

    for g in range(N_GROUP):
        hot = jnp.concatenate([pick(minus(4 * g + k)) for k in range(4)], axis=0)
        slabs = dot(hot, grad_bal[...]).astype(BF)
        for k in range(4):
            i = 4 * g + k
            slab = slabs[k * SLOT : (k + 1) * SLOT, :]
            if i == OWN:
                ret[OWN] = slab
            else:
                stage[i] = slab
                data_copy(i).start()

    forward(1)

    owner = jnp.broadcast_to(owner_ref[...].astype(F32), (UNIQ, UNIQ))
    owner_col = jnp.transpose(owner)
    before = iota((UNIQ, UNIQ), 0) < iota((UNIQ, UNIQ), 1)
    rank = jnp.sum(jnp.where((owner == owner_col) & before, 1.0, 0.0), axis=0, keepdims=True)
    mine = iota((N_DEV, UNIQ), 0) == owner_ref[...]
    lanes = iota((N_DEV, 128), 1)
    ids_all = jnp.zeros((N_DEV, 128), F32)
    order_f = orow_ref[...].astype(F32)
    for c in range(CAP):
        sel = jnp.where(mine & (rank == float(c)), 1.0, 0.0)
        sel_all[c] = sel.astype(BF)
        ids_all = jnp.where(lanes == c, jnp.sum(sel * order_f, axis=1, keepdims=True), ids_all)
    meta[...] = ids_all.reshape(N_DEV, 1, 128)

    def meta_out(i, carry):
        other, to = device(i)
        remote(meta.at[other], gotm_ref.at[i], asem, (1,), to).start()
        return carry

    pl.semaphore_wait(ready, N_TABLE - 1)
    lax.fori_loop(1, N_DEV, meta_out, 0)
    gotm_ref[0] = meta[me]

    forward(2)
    forward(3)

    def back_a(g):
        here = slice(g * GROUP, (g + 1) * GROUP)
        gy = ret[4 * g : 4 * g + 4].reshape(GROUP, D)
        hat = hat_out_all[here, :]
        grad_mixed = dot_t(gy, w_out[...])
        gh_all[here, 0:D] = (grad_mixed * (hat * gain_out) * slope_all[here, 0:D]).astype(BF)
        cot = grad_mixed * gate_all[here, :]
        gains_acc[1:2, :] += jnp.sum(cot * hat, axis=0, keepdims=True)
        dhat = cot * gain_out
        half_all[here, :] = (
            rstd_out_all[here, :] * (dhat - row_mean(dhat) - hat * row_mean(dhat * hat))
        ).astype(BF)

    def back_b(g):
        for s in range(2):
            rows = slice(g * GROUP + s * PAIR, g * GROUP + (s + 1) * PAIR)
            for h in range(HEADS):
                cols = slice(h * HDIM, (h + 1) * HDIM)
                n = (g * 2 + s) * HEADS + h
                half = half_all[rows, cols]
                grad_weight = dot_t(half, vqk_all[0, rows, cols])
                gs = (grad_weight * wts[n, 1].astype(F32)).astype(BF)
                parts = (
                    t_dot(wts[n, 0], half),
                    dot(gs, vqk_all[2, rows, cols]),
                    t_dot(gs, vqk_all[1, rows, cols]),
                )
                for k in range(3):
                    at = slice((k + 1) * D + h * HDIM, (k + 1) * D + (h + 1) * HDIM)
                    gh_all[rows, at] = (parts[k] * slope_all[rows, at]).astype(BF)

    def back_c(g):
        here = slice(g * GROUP, (g + 1) * GROUP)
        gy = ret[4 * g : 4 * g + 4].reshape(GROUP, D).astype(F32)
        hat = hat_in_all[here, :]
        grad_normed = dot_t(gh_all[here, :], w_in[...])
        gains_acc[0:1, :] += jnp.sum(grad_normed * hat, axis=0, keepdims=True)
        dhat = grad_normed * gain_in
        inner = rstd_in_all[here, :] * (dhat - row_mean(dhat) - hat * row_mean(dhat * hat))
        grad_tok = (inner + gy).astype(BF)
        part = dot(hot_all[:, here], grad_tok)
        if g == 0:
            rows_acc[...] = part
        else:
            rows_acc[...] += part

    def put(dst, first, block):
        for j in range(4):
            dst[first + j * D : first + (j + 1) * D, :] = block[:, j * 128 : (j + 1) * 128].astype(BF)

    def all_reduce(s, ch, a, pr, b, fr, c, sr, tr, out):
        third = 16 * ch
        quarter = 4 * ch

        def at(row, size):
            return pl.ds(pl.multiple_of(row, 16), size)

        def pair(q, d):
            v = along(ORDERS[q][0], d)[0]
            src = a.at[at(((1 - core) * 3 + q) * third + v * quarter, quarter)]
            return remote(src, pr.at[q, at(v * quarter, quarter)], psem, (s, 0, q, d), partner)

        def add_pair(q, d):
            v = along(ORDERS[q][0], d)[0]
            own = a[at((core * 3 + q) * third + v * quarter, quarter), :].astype(F32)
            rows = at(v * quarter, quarter)
            b[q, rows, :] = (own + pr[q, rows, :].astype(F32)).astype(BF)

        def first(q, d):
            v, to = along(ORDERS[q][0], d)
            return remote(b.at[q, at(v * quarter, quarter)], fr.at[q, d - 1], rsem, (s, 0, q, d - 1), to)

        def second(q, d):
            v, to = along(ORDERS[q][1], d)
            return remote(c.at[q, at(v * ch, ch)], sr.at[q, d - 1], rsem, (s, 1, q, d - 1), to)

        def third_copy(q, d):
            mine = coords[ORDERS[q][2]]
            to = along(ORDERS[q][2], d)[1]
            return remote(tr.at[q, mine], tr.at[q, mine], rsem, (s, 2, q, d - 1), to)

        def piece(q, da, db):
            va = along(ORDERS[q][0], 4 - da)[0]
            vb = along(ORDERS[q][1], 4 - db)[0]
            return at((core * 3 + q) * third + va * quarter + vb * ch, ch)

        def back_two(q, d):
            ref = out.at[piece(q, 0, 0)]
            return remote(ref, ref, rsem, (s, 3, q, d - 1), along(ORDERS[q][1], d)[1])

        def back_one(q, d, k):
            ref = out.at[piece(q, 0, k)]
            return remote(ref, ref, bsem, (s, q, d - 1, k), along(ORDERS[q][0], d)[1])

        def back_pair(q, d):
            va = along(ORDERS[q][0], 4 - d)[0]
            ref = out.at[at((core * 3 + q) * third + va * quarter, quarter)]
            return remote(ref, ref, psem, (s, 1, q, d), partner)

        for d in (2, 1, 3, 0):
            for q in range(3):
                pair(q, d).start()
        yield
        for d in (2, 1, 3, 0):
            for q in range(3):
                pair(q, d).wait()
                add_pair(q, d)
                if d:
                    first(q, d).start()
        yield
        for q in range(3):
            for d in range(1, 4):
                first(q, d).wait()
            total = b[q, at(coords[ORDERS[q][0]] * quarter, quarter), :].astype(F32)
            for d in range(3):
                total = total + fr[q, d].astype(F32)
            c[q] = total.astype(BF)
            for d in range(1, 4):
                second(q, d).start()
        yield
        for q in range(3):
            for d in range(1, 4):
                second(q, d).wait()
            total = c[q, at(coords[ORDERS[q][1]] * ch, ch), :].astype(F32)
            for d in range(3):
                total = total + sr[q, d].astype(F32)
            tr[q, coords[ORDERS[q][2]]] = total.astype(BF)
            for d in range(1, 4):
                third_copy(q, d).start()
        yield
        for q in range(3):
            for d in range(1, 4):
                third_copy(q, d).wait()
            total = tr[q, 0].astype(F32)
            for d in range(1, 4):
                total = total + tr[q, d].astype(F32)
            out[piece(q, 0, 0), :] = total.astype(BF)
            for d in (2, 1, 3):
                back_two(q, d).start()
            for d in (2, 1, 3):
                back_one(q, d, 0).start()
        yield
        for k in (1, 3, 2):
            for q in range(3):
                back_two(q, k).wait()
                for d in (2, 1, 3):
                    back_one(q, d, k).start()
        for q in range(3):
            back_pair(q, 0).start()
        yield
        for d in (1, 3, 2):
            for q in range(3):
                for k in range(4):
                    back_one(q, d, k).wait()
                back_pair(q, d).start()
        yield
        for d in (0, 1, 3, 2):
            for q in range(3):
                back_pair(q, d).wait()
        yield

    def gain_reduce():
        def pair():
            ref = gbuf.at[0, core]
            return remote(ref, ref, gsem, (0, 0), partner)

        def copy(k, d):
            axis = "xyz"[k - 1]
            ref = gbuf.at[k, coords[axis]]
            return remote(ref, ref, gsem, (k, d - 1), along(axis, d)[1])

        gbuf[0, core] = jnp.concatenate(
            [gains_acc[r : r + 1, j * 128 : (j + 1) * 128] for r in range(2) for j in range(4)],
            axis=0,
        )
        pair().start()
        yield
        pair().wait()
        total = gbuf[0, 0] + gbuf[0, 1]
        for k in range(1, 4):
            gbuf[k, coords["xyz"[k - 1]]] = total
            for d in range(1, 4):
                copy(k, d).start()
            yield
            for d in range(1, 4):
                copy(k, d).wait()
            total = (gbuf[k, 0] + gbuf[k, 1]) + (gbuf[k, 2] + gbuf[k, 3])
        gains_ref[...] = total
        yield

    red1 = all_reduce(0, CH1, a1, pr1, b1, fr1, c1, sr1, tr1, g1_ref)
    red2 = all_reduce(1, CH2, a2, pr2, b2, fr2, c2, sr2, tr2, g2_ref)
    red_g = gain_reduce()

    for g in range(N_GROUP):
        for i in range(4 * g, min(4 * g + 4, OWN)):
            data_copy(i).wait_recv()
        back_a(g)
        if g < N_GROUP - 2:
            back_b(g)
    put(a1, 0, dot(mixed_t[...], ret[...].reshape(TOK, D)))
    put(a1, 4 * D, dot(norm_t[...], gh_all[:, 0:D]))
    a1[8 * D : ROWS1, :] = jnp.zeros((ROWS1 - 8 * D, 128), BF)
    next(red1)
    back_b(2)
    next(red1)
    back_b(3)
    for k in range(3):
        put(a2, k * 4 * D, dot(norm_t[...], gh_all[:, (k + 1) * D : (k + 2) * D]))
    next(red2)
    next(red1)
    back_c(0)
    next(red2)
    back_c(1)
    next(red1)
    back_c(2)
    back_c(3)
    next(red_g)

    row_half = rows_acc[...].astype(BF)
    for c in range(CAP):
        picked = dot(sel_all[c], row_half)
        for k in range(4):
            spread[pl.ds(k * CAP + c, N_DEV, stride=16), :] = picked[:, k * 128 : (k + 1) * 128]
    send[...] = spread[...].astype(BF).reshape(N_DEV, 16, 128)
    got_ref[0] = send[me]

    def scatter_out(i, carry):
        other, to = device(i)
        remote(send.at[other], got_ref.at[i], asem, (0,), to).start()
        return carry

    next(red2)
    lax.fori_loop(1, 49, scatter_out, 0)
    next(red1)
    next(red_g)
    lax.fori_loop(49, 81, scatter_out, 0)
    next(red2)
    next(red1)
    next(red_g)
    lax.fori_loop(81, N_DEV, scatter_out, 0)
    next(red2)
    next(red1)
    next(red_g)
    next(red2)
    next(red_g)
    next(red2)
    next(red1)

    others = pl.ds(1, N_DEV - 1)
    remote(send.at[others], got_ref.at[others], asem, (0,), partner).wait()
    remote(meta.at[others], gotm_ref.at[others], asem, (1,), partner).wait()
    spread[...] = got_ref[...].reshape(N_DEV * 16, 128).astype(F32)
    for c in range(CAP):
        for k in range(4):
            picked_ref[c * N_DEV : (c + 1) * N_DEV, k * 128 : (k + 1) * 128] = spread[
                pl.ds(k * CAP + c, N_DEV, stride=16), :
            ].astype(BF)
    ids_ref[...] = jnp.transpose(gotm_ref[...].reshape(N_DEV, 128))
    for i in range(OWN):
        data_copy(i).wait_send()
    next(red2)


def run_step(seq_dest, seq_blocks, items, owner, orow, gain_in, gain_out, touched, grad_out, w_in, w_out):
    smem = pl.BlockSpec(memory_space=pltpu.SMEM)
    vmem = pl.BlockSpec(memory_space=pltpu.VMEM)
    far = pl.BlockSpec(memory_space=pl.ANY)
    v = pltpu.VMEM
    dma = pltpu.SemaphoreType.DMA
    scratch = [
        v((UNIQ, D), BF),
        v((D, D), BF),
        v((D, 4 * D), BF),
        v((D, D), BF),
        dma((4,)),
        v((N_DP, 1, D), jnp.int32),
        v((N_DP, 1, D), jnp.int32),
        v((N_DP, 1, D), jnp.int32),
        v((N_DP, SLOT, D), BF),
        v((N_DP, SLOT, D), BF),
        dma((2, N_DP)),
        dma((2, N_DP)),
        pltpu.SemaphoreType.REGULAR,
        v((UNIQ, TOK), BF),
        v((D, TOK), BF),
        v((D, TOK), BF),
        v((TOK, D), F32),
        v((TOK, 1), F32),
        v((TOK, D), F32),
        v((TOK, 1), F32),
        v((TOK, 4 * D), F32),
        v((TOK, D), F32),
        v((3, TOK, D), BF),
        v((GROUP, D), F32),
        v((N_GROUP * 2 * HEADS, 2, PAIR, PAIR), BF),
        v((TOK, D), BF),
        v((TOK, 4 * D), BF),
        v((UNIQ, D), F32),
        v((8, D), F32),
        v((N_DEV * 16, 128), F32),
        v((N_DEV, 16, 128), BF),
        v((N_DEV, 1, 128), F32),
        v((CAP, N_DEV, UNIQ), BF),
        v((ROWS1, 128), BF),
        v((ROWS2, 128), BF),
    ]
    for shape in ((3, 16), (3, 16), (3, 3, 4), (3, 4), (3, 3, 1), (3, 4, 1)):
        for ch in (CH1, CH2):
            scratch.append(v(shape[:-1] + (shape[-1] * ch, 128), BF))
    scratch += [
        v((4, 4, 8, 128), F32),
        dma((2, 2, 2, 3, 4)),
        dma((2, 2, 4, 3, 3)),
        dma((2, 2, 3, 3, 4)),
        dma((2, 2)),
        dma((2, 4, 3)),
        v((N_DEV, 16, 128), BF),
        v((N_DEV, 1, 128), F32),
    ]
    return pl.pallas_call(
        step_kernel,
        out_shape=(
            pltpu.VMEM((ROWS1, 128), BF),
            pltpu.VMEM((ROWS2, 128), BF),
            pltpu.VMEM((CAP * N_DEV, D), BF),
            pltpu.VMEM((128, N_DEV), F32),
            pltpu.VMEM((8, 128), F32),
        ),
        in_specs=[smem] + [vmem] * 7 + [far] * 4,
        out_specs=(vmem,) * 5,
        scratch_shapes=scratch,
        compiler_params=pltpu.CompilerParams(
            collective_id=0, has_side_effects=True, vmem_limit_bytes=60_000_000
        ),
        name="step",
    )(
        seq_dest,
        seq_dest.reshape(1, -1),
        seq_blocks.reshape(1, -1),
        items.reshape(8, 128),
        owner.reshape(1, -1),
        orow.reshape(1, -1),
        gain_in.reshape(1, -1),
        gain_out.reshape(1, -1),
        touched,
        grad_out,
        w_in,
        w_out,
    )


def finish_kernel(
    g1,
    g2,
    picked,
    ids_ref,
    gains_in,
    table_out,
    win_out,
    wout_out,
    gin_ref,
    gout_ref,
    table,
    win,
    wout,
    out_sem,
    *,
    factor
):
    part = 4 * D

    def give(n):
        if n < 4:
            rows = pl.ds(n * 256, 256)
            return pltpu.make_async_copy(table.at[rows], table_out.at[rows], out_sem.at[n])
        if n == 4:
            return pltpu.make_async_copy(wout, wout_out, out_sem.at[n])
        cols = pl.ds((n - 5) * D, D)
        return pltpu.make_async_copy(win.at[n - 5], win_out.at[:, cols], out_sem.at[n])

    for j in range(4):
        gin_ref[:, j * 128 : (j + 1) * 128] = gains_in[j : j + 1, :] * factor
        gout_ref[:, j * 128 : (j + 1) * 128] = gains_in[4 + j : 5 + j, :] * factor
    for n in range(4):
        rows = (iota((256, N_DEV), 0) + n * 256).astype(F32)
        hot = jnp.concatenate(
            [jnp.where(rows == ids_ref[c : c + 1, :], 1.0, 0.0).astype(BF) for c in range(CAP)],
            axis=1,
        )
        table[n * 256 : (n + 1) * 256, :] = dot(hot, picked[...])
        give(n).start()
    for n in range(5):
        src, first = (g1, n * part) if n < 2 else (g2, (n - 2) * part)
        for j in range(4):
            block = src[first + j * D : first + (j + 1) * D, :].astype(F32) * factor
            cols = slice(j * 128, (j + 1) * 128)
            if n == 0:
                wout[:, cols] = block
            else:
                win[n - 1, :, cols] = block
        give(4 + n).start()
    for n in range(9):
        give(n).wait()


def finish(g1, g2, picked, ids, gains, factor):
    far = pl.BlockSpec(memory_space=pl.ANY)
    vmem = pl.BlockSpec(memory_space=pltpu.VMEM)

    def body(*refs):
        finish_kernel(*refs, factor=factor)

    return pl.pallas_call(
        body,
        out_shape=(
            jax.ShapeDtypeStruct((ROWS_DEV, D), F32),
            jax.ShapeDtypeStruct((D, 4 * D), F32),
            jax.ShapeDtypeStruct((D, D), F32),
            jax.ShapeDtypeStruct((1, D), F32),
            jax.ShapeDtypeStruct((1, D), F32),
        ),
        in_specs=[vmem] * 5,
        out_specs=(far, far, far, vmem, vmem),
        scratch_shapes=[
            pltpu.VMEM((ROWS_DEV, D), F32),
            pltpu.VMEM((4, D, D), F32),
            pltpu.VMEM((D, D), F32),
            pltpu.SemaphoreType.DMA((9,)),
        ],
        compiler_params=pltpu.CompilerParams(vmem_limit_bytes=24_000_000),
        name="finish",
    )(g1, g2, picked, ids, gains)


def on_device(
    touched_rows,
    row_of_token,
    row_owner,
    owner_row,
    seq_blocks,
    seq_dest,
    grad_out,
    w_in,
    w_out,
    gain_in,
    gain_out,
):
    g1, g2, picked, ids, gains = run_step(
        seq_dest,
        seq_blocks,
        row_of_token,
        row_owner,
        owner_row,
        gain_in,
        gain_out,
        touched_rows,
        grad_out,
        w_in,
        w_out,
    )
    factor = 1.0 / math.sqrt(grad_out.shape[0] * N_DEV)
    table, grad_in, grad_w_out, gin, gout = finish(g1, g2, picked, ids, gains, factor)
    return (table, grad_in, grad_w_out, gin.reshape(-1), gout.reshape(-1))


def solution(mesh):
    in_specs = (
        P(("dp", "table"), None),
        P(("dp", "table")),
        P(("dp", "table"), None),
        P(("dp", "table")),
        P(("dp", "table")),
        P(("dp", "table")),
        P(("dp", "table"), None),
        P(),
        P(),
        P(),
        P(),
    )
    out_specs = (P(("dp", "table"), None), P(), P(), P(), P())
    return jax.shard_map(
        on_device, mesh=mesh, in_specs=in_specs, out_specs=out_specs, check_vma=False
    )
```
